256 devices in a mesh: slab: 8 (over y, core), tile: 32 (over z, x).
Axes of the slice: x: 4, y: 4, z: 8, core: 2. Of those that a mesh axis runs over, the one named last changes fastest.
Arguments:
- volume: float32 [3072, 512, 128], P('tile', 'slab'), may hold values from 0 to 2
- footprints: bfloat16 [32, 128, 128], replicated, may hold values from -0.02734375 to 0.02734375
- foot_index: int32 [3072, 8], P('tile'), may hold values from 0 to 31
- ray_block: int32 [3072, 8], replicated, may hold values from 0 to 63, as said below
- ray_slot: int32 [64], replicated, may hold values from 0 to 63, as said below
- measured: float32 [64, 512, 128], P('tile', 'slab'), may hold values from -6 to 6
- weights: float32 [64, 512, 128], P('tile', 'slab'), may hold values from 0.25 to 4
Outputs:
- updated_volume: float32 [3072, 512, 128], P('tile', 'slab')
The draws below stay inside these ranges and needn't reach their ends.
Inputs may be any that keep to these rules, and one draw needn't show every extreme that they name: A permutation of the 64 ray blocks; ray block b is held by index ray_slot[b] // 2 of tile, and its rows of measured and weights are row ray_slot[b]. `ray_block`: the crossings of the rows held by one index of tile name at most 16 distinct ray blocks, no two of them held by the same owner.
All inputs are finite; a program needn't handle non-finite values.
Results may differ from the reference program's by a relative error of at most 0.002.
Values may be sent and summed in bfloat16 or wider, within the bound.
No kernel may reach another device: no remote copies, remote signals or barrier semaphores. Data moves between devices by JAX's collectives and lax.ppermute only.
A program may use at most 128 MiB of HBM per device.

```python
import math
import jax
import jax.numpy as jnp
from jax import lax

PX = 128
RAYS = 128
ROWS_DEV = 96
K = 8
NFOOT = 32
RB_DEV = 2
OWNERS = 32
RB = 64
TOUCH = 16
NROWS = 3072
NZ = 512
N_TILE = 32


def crossing_tables(key):
    folded = jax.random.fold_in(key, 11)
    key_slot, key_owner, key_local, key_pick = jax.random.split(folded, 4)
    slot_table = jax.random.permutation(key_slot, RB).astype(jnp.int32)
    block_of_slot = jnp.argsort(slot_table).astype(jnp.int32)
    owner_keys = jax.random.split(key_owner, OWNERS)
    chosen = jax.vmap(lambda single: jax.random.permutation(single, OWNERS)[:TOUCH])(owner_keys)
    local_index = jax.random.randint(key_local, (OWNERS, TOUCH), 0, RB_DEV)
    touched = block_of_slot[chosen * RB_DEV + local_index]
    pick_keys = jax.random.split(key_pick, OWNERS)
    picks = jax.vmap(lambda single: jax.random.permutation(single, ROWS_DEV * K) % TOUCH)(pick_keys)
    blocks = jnp.take_along_axis(touched, picks, axis=1)
    return (slot_table, blocks.reshape(NROWS, K).astype(jnp.int32))


def draw_ray_slot(key, part):
    return crossing_tables(key)[0]


def draw_ray_block(key, part):
    return crossing_tables(key)[1]


def plant(array, rng, smallest, high):
    spot = [jax.random.randint(jax.random.fold_in(rng, axis), (), 0, length) for axis, length in enumerate(array.shape)]
    widest = array.shape.index(max(array.shape))
    beside = spot[:widest] + [(spot[widest] + 1) % array.shape[widest]] + spot[widest + 1:]
    return array.at[tuple(spot)].set(smallest).at[tuple(beside)].set(high)


def level_of(own_key, dims, cuts, smallest, high):
    def one(axis_at, parts):
        draws = jax.random.uniform(jax.random.fold_in(jax.random.fold_in(own_key, 6), axis_at), (parts,), jnp.float32, smallest / len(cuts), high / len(cuts))
        return jnp.repeat(jnp.exp(draws), dims[axis_at] // parts).reshape((-1,) + (1,) * (len(dims) - axis_at - 1))

    level = one(*cuts[0])
    for cut in cuts[1:]:
        level = level * one(*cut)
    return level


def scatter_about(stream_key, dims, scale, limit, cuts=(), dtype=jnp.bfloat16):
    array = scale * jax.random.normal(stream_key, dims, jnp.float32)
    if cuts:
        array = array * level_of(stream_key, dims, cuts, -0.22, 0.18)
    return jnp.clip(array, -limit, limit).astype(dtype)


def setup_inputs(seed: int = 0) -> dict:
    key_list = jax.random.split(jax.random.key(seed), 8)
    volume = jnp.clip(2.0 * jax.random.uniform(key_list[0], (NROWS, NZ, PX), jnp.float32) ** level_of(key_list[0], (NROWS, NZ, PX), ((0, 32), (1, 8)), -0.2, 0.2), 0.0, 2.0)
    footprints = scatter_about(key_list[1], (NFOOT, PX, RAYS), (PX * ROWS_DEV * K // RB_DEV) ** -0.5, 0.02734375)
    foot_index = plant(jax.random.randint(key_list[2], (NROWS, K), 0, NFOOT), jax.random.fold_in(key_list[2], 1), 0, NFOOT - 1).astype(jnp.int32)
    ray_block = draw_ray_block(jax.random.fold_in(key_list[7], 71), 0)
    ray_slot = draw_ray_slot(jax.random.fold_in(key_list[7], 71), 0)
    measured = scatter_about(key_list[5], (RB, NZ, RAYS), 1.0, 6.0, ((0, 32), (1, 8)), jnp.float32)
    weights = jnp.clip(jnp.exp(math.log(4.0) - 2.7725887 * jax.random.uniform(key_list[6], (RB, NZ, RAYS), jnp.float32) ** level_of(key_list[6], (RB, NZ, RAYS), ((0, 32), (1, 8)), -0.2, 0.2)), 0.25, 4.0)
    return dict(volume=volume, footprints=footprints, foot_index=foot_index, ray_block=ray_block, ray_slot=ray_slot, measured=measured, weights=weights)


smoothing = 0.04
step_length = 2.0
variation_weight = 1.0

def variation_gradient(density):
    grad_rows = jnp.concatenate([density[1:] - density[:-1], jnp.zeros_like(density[:1])], axis=0)
    grad_slices = jnp.concatenate([density[:, 1:] - density[:, :-1], jnp.zeros_like(density[:, :1])], axis=1)
    grad_cols = jnp.concatenate([density[:, :, 1:] - density[:, :, :-1], jnp.zeros_like(density[:, :, :1])], axis=2)
    magnitude = jnp.sqrt(grad_rows * grad_rows + grad_slices * grad_slices + grad_cols * grad_cols + smoothing)
    flux_rows = grad_rows / magnitude
    flux_slices = grad_slices / magnitude
    flux_cols = grad_cols / magnitude
    part_rows = jnp.concatenate([jnp.zeros_like(flux_rows[:1]), flux_rows[:-1]], axis=0) - flux_rows
    part_slices = jnp.concatenate([jnp.zeros_like(flux_slices[:, :1]), flux_slices[:, :-1]], axis=1) - flux_slices
    part_cols = jnp.concatenate([jnp.zeros_like(flux_cols[:, :, :1]), flux_cols[:, :, :-1]], axis=2) - flux_cols
    return part_rows + part_slices + part_cols

def reference(volume, footprints, foot_index, ray_block, ray_slot, measured, weights):
    row_total, slice_total, column_count = volume.shape
    ray_width = footprints.shape[2]
    crossings = ray_block.shape[1]
    slots = jnp.take(ray_slot, ray_block, axis=0).astype(jnp.int32)
    rounded = volume.astype(jnp.bfloat16)
    pixel_groups = rounded.reshape(N_TILE, ROWS_DEV, slice_total, column_count)
    offset_groups = foot_index.reshape(N_TILE, ROWS_DEV, crossings)
    slot_groups = slots.reshape(N_TILE, ROWS_DEV, crossings)

    def project(running_sum, inputs):
        pixels, offsets, targets = inputs
        stencil = jnp.take(footprints, offsets, axis=0).astype(jnp.float32)
        partial_value = jnp.einsum('rzp,rkpq->rkzq', pixels.astype(jnp.float32), stencil)
        running_sum = running_sum.at[targets.reshape(-1)].add(partial_value.reshape(-1, slice_total, ray_width))
        return (running_sum, None)
    start = jnp.zeros((ray_slot.shape[0], slice_total, ray_width), jnp.float32)
    projection, _ = lax.scan(project, start, (pixel_groups, offset_groups, slot_groups))
    residual = (weights * (projection - measured)).astype(jnp.bfloat16)

    def backproject(running, inputs):
        offsets, targets = inputs
        stencil = jnp.take(footprints, offsets, axis=0).astype(jnp.float32)
        values = jnp.take(residual, targets, axis=0).astype(jnp.float32)
        return (running, jnp.einsum('rkzq,rkpq->rzp', values, stencil))
    _, pieces = lax.scan(backproject, jnp.zeros((), jnp.float32), (offset_groups, slot_groups))
    data_grad = pieces.reshape(row_total, slice_total, column_count)
    updated = volume - step_length * (data_grad + variation_weight * variation_gradient(volume))
    return jnp.maximum(updated, 0.0)
```

```python
import functools

import jax
import jax.numpy as jnp
from jax import lax
from jax.experimental import pallas as pl
from jax.experimental.pallas import tpu as pltpu
from jax.sharding import PartitionSpec as P

smoothing = 0.04
step_length = 2.0
variation_weight = 1.0
lanes = 128

F32 = jnp.float32
BF16 = jnp.bfloat16
VMEM = pl.BlockSpec(memory_space=pltpu.VMEM)
SMEM = pl.BlockSpec(memory_space=pltpu.SMEM)
ANY = pl.BlockSpec(memory_space=pl.ANY)


def iota(shape, dim):
    return lax.broadcasted_iota(jnp.int32, shape, dim)


def forward_kernel(
    touch, owned, ray_slot, blocks, foots, volume, prints,
    sent, table, counts, head, tail,
    rows_buf, prints_buf, grouped, sums, table_buf, sems, table_sem, prints_sem,
):
    row_count, slice_count, pixels = volume.shape
    foot_count = prints.shape[0]
    owners = sent.shape[0]
    crossings = blocks.shape[0]
    chunk_count = sems.shape[0]
    depth = slice_count // chunk_count
    copies = []
    for c in range(chunk_count):
        span = pl.ds(c * depth, depth)
        copies.append(
            pltpu.make_async_copy(
                volume.at[:, span, :],
                rows_buf.reshape(row_count, slice_count, pixels).at[:, span, :],
                sems.at[c],
            )
        )
        copies[c].start()
    prints_copy = pltpu.make_async_copy(prints, prints_buf, prints_sem)
    prints_copy.start()

    position = lax.axis_index("tile")
    offset = position * row_count
    limit = blocks.shape[1] - 2 * lanes
    base = jnp.minimum((offset // lanes) * lanes, limit)
    window = blocks[:, pl.ds(pl.multiple_of(base, lanes), 2 * lanes)]
    mine = pltpu.roll(window, 2 * lanes - (offset - base), 1)[:, :lanes]
    slot = jnp.zeros_like(mine)
    for b in range(ray_slot.shape[0]):
        slot = jnp.where(mine == b, ray_slot[b], slot)
    valid = iota((crossings, lanes), 1) < row_count
    owner = jnp.where(valid, slot // owned, -1)
    label = iota((owners, lanes), 0)
    present = jnp.zeros((owners, lanes), F32)
    for k in range(crossings):
        present = jnp.where(owner[k : k + 1] == label, 1.0, present)
    present = jnp.broadcast_to(jnp.max(present, axis=1, keepdims=True), (owners, lanes))
    lower = (iota((owners, owners), 1) < iota((owners, owners), 0)).astype(BF16)
    rank = jnp.dot(lower, present.astype(BF16), preferred_element_type=F32)
    column = iota((owners, lanes), 1)
    rank_row = jnp.sum(jnp.where(label < column, present, 0.0), axis=0, keepdims=True)
    present_row = jnp.sum(jnp.where(label == column, present, 0.0), axis=0, keepdims=True)
    row = jnp.where(present_row > 0.5, rank_row, -1.0).astype(jnp.int32)
    table_buf[...] = jnp.broadcast_to(row, table_buf.shape)
    table_copy = pltpu.make_async_copy(table_buf, table, table_sem)
    table_copy.start()

    code_row = iota((foot_count * touch, lanes), 0)
    total = jnp.zeros((foot_count * touch, lanes), F32)
    foots_here = jnp.concatenate(
        [foots[...], jnp.zeros((crossings, lanes - row_count), jnp.int32)], axis=1
    )
    for k in range(crossings):
        place = jnp.sum(
            jnp.where(owner[k : k + 1] == label, rank, 0.0), axis=0, keepdims=True
        ).astype(jnp.int32)
        code = jnp.where(valid[k : k + 1], foots_here[k : k + 1] * touch + place, -1)
        total = total + jnp.where(code_row == code, 1.0, 0.0)
    counts[...] = total.astype(BF16)

    for c in range(chunk_count):
        copies[c].wait()

        @pl.loop(0, depth // 2)
        def _(i, c=c):
            z = c * depth + 2 * i
            pair = jnp.concatenate(
                [
                    rows_buf[pl.ds(z, row_count, stride=slice_count), :],
                    rows_buf[pl.ds(z + 1, row_count, stride=slice_count), :],
                ],
                axis=1,
            ).astype(BF16)
            group = jnp.dot(counts[:, :row_count], pair, preferred_element_type=F32).astype(BF16)
            for half in range(2):
                for f in range(foot_count):
                    grouped[
                        pl.ds(pl.multiple_of((z + half) * touch, touch), touch),
                        f * pixels : (f + 1) * pixels,
                    ] = group[f * touch : (f + 1) * touch, half * pixels : (half + 1) * pixels]

    head[...] = rows_buf[pl.ds(0, row_count, stride=slice_count), :]
    tail[...] = rows_buf[pl.ds(slice_count - 1, row_count, stride=slice_count), :]
    prints_copy.wait()
    step = 256

    @pl.loop(0, slice_count * touch // step)
    def _(m):
        span = pl.ds(pl.multiple_of(m * step, step), step)
        sums[span, :] = jnp.dot(
            grouped[span, :],
            prints_buf[...].reshape(foot_count * pixels, -1),
            preferred_element_type=F32,
        )

    table_copy.wait()
    for t in range(owners):
        place = table[0, t]
        block = sums[pl.ds(jnp.maximum(place, 0), slice_count, stride=touch), :]
        sent[t] = jnp.where(place >= 0, block, 0.0).astype(BF16)


def forward(touch, owned, owners, ray_slot, blocks, foots, volume, prints):
    rows, slices, pixels = volume.shape
    foot_count, _, rays = prints.shape
    chunks = 4
    return pl.pallas_call(
        functools.partial(forward_kernel, touch, owned),
        out_shape=(
            jax.ShapeDtypeStruct((owners, slices, rays), BF16),
            jax.ShapeDtypeStruct((8, lanes), jnp.int32),
            jax.ShapeDtypeStruct((foot_count * touch, lanes), BF16),
            jax.ShapeDtypeStruct((rows, pixels), F32),
            jax.ShapeDtypeStruct((rows, pixels), F32),
        ),
        in_specs=[SMEM, VMEM, VMEM, ANY, ANY],
        out_specs=(VMEM, SMEM, VMEM, VMEM, VMEM),
        scratch_shapes=[
            pltpu.VMEM((rows * slices, pixels), F32),
            pltpu.VMEM(prints.shape, BF16),
            pltpu.VMEM((slices * touch, foot_count * pixels), BF16),
            pltpu.VMEM((slices * touch, rays), F32),
            pltpu.VMEM((8, lanes), jnp.int32),
            pltpu.SemaphoreType.DMA((chunks,)),
            pltpu.SemaphoreType.DMA,
            pltpu.SemaphoreType.DMA,
        ],
        name="forward",
    )(ray_slot, blocks, foots, volume, prints)


def middle_kernel(
    owned, ray_slot, blocks, volume, before_slice, after_slice, before_row, after_row, counts,
    prints,
    base, turned, counts_turned, picks,
    slice_flux,
):
    rows, slices, pixels = volume.shape
    position = lax.axis_index("tile")
    layer = lax.axis_index("slab")
    last_position = lax.axis_size("tile") - 1
    last_layer = lax.axis_size("slab") - 1
    lane = iota((1, pixels), 1)
    inner = lane < pixels - 1
    first = lane == 0

    def col_grad(x):
        return jnp.where(inner, pltpu.roll(x, pixels - 1, 1) - x, 0.0)

    def scale(a, b, c):
        return lax.rsqrt(a * a + b * b + c * c + smoothing)

    low = before_slice[...]
    low_next = jnp.concatenate([low[1:], after_row[0:1]], axis=0)
    grad_rows = low_next - low
    row_id = iota((rows, 1), 0)
    grad_rows = jnp.where((row_id == rows - 1) & (position == last_position), 0.0, grad_rows)
    grad_slices = volume.reshape(rows * slices, pixels)[pl.ds(0, rows, stride=slices), :] - low
    flux = grad_slices * scale(grad_rows, grad_slices, col_grad(low))
    slice_flux[...] = jnp.where(layer == 0, 0.0, flux)

    z_id = iota((slices, 1), 0)
    top = z_id == slices - 1
    bottom = z_id == 0
    top_edge = top & (layer == last_layer)

    def fluxes(here, next_row, beyond, last):
        up = pltpu.roll(here, slices - 1, 0)
        up = jnp.where(top, beyond, up)
        grad_slices = jnp.where(top_edge, 0.0, up - here)
        grad_rows = jnp.where(last, 0.0, next_row - here)
        grad_cols = col_grad(here)
        inverse = scale(grad_rows, grad_slices, grad_cols)
        return grad_rows * inverse, grad_slices * inverse, grad_cols * inverse

    start, _, _ = fluxes(
        before_row[1 : slices + 1], volume[0], before_row[slices + 1 : slices + 2], False
    )
    start = jnp.where(position == 0, 0.0, start)

    def one(r, here, next_row, previous, last):
        flux_rows, flux_slices, flux_cols = fluxes(
            here, next_row, after_slice[pl.ds(r, 1), :], last
        )
        below = pltpu.roll(flux_slices, 1, 0)
        below = jnp.where(bottom, slice_flux[pl.ds(r, 1), :], below)
        left = jnp.where(first, 0.0, pltpu.roll(flux_cols, 1, 1))
        variation = (previous - flux_rows) + (below - flux_slices) + (left - flux_cols)
        base[r] = here - (step_length * variation_weight) * variation
        return flux_rows

    final = lax.fori_loop(
        0, rows - 1, lambda r, previous: one(r, volume[r], volume[r + 1], previous, False), start
    )
    one(rows - 1, volume[rows - 1], after_row[1 : slices + 1], final, position == last_position)

    @pl.loop(0, prints.shape[0])
    def _(f):
        turned[f] = prints[f].astype(F32).T.astype(BF16)

    counts_turned[...] = counts[...].astype(F32).T[:rows].astype(BF16)

    owners = picks.shape[0]
    width = blocks.shape[1]
    second = jnp.int32(0)
    for b in range(ray_slot.shape[0]):
        second = jnp.where(ray_slot[b] == position * owned + 1, b, second)
    hit = jnp.max(jnp.where(blocks[...] == second, 1.0, 0.0), axis=0, keepdims=True)
    member = (iota((owners, width), 1) // rows == iota((owners, width), 0)).astype(BF16)
    count = lax.dot_general(
        member,
        jnp.broadcast_to(hit, (lanes, width)).astype(BF16),
        (((1,), (1,)), ((), ())),
        preferred_element_type=F32,
    )
    picks[...] = jnp.where(count > 0.5, 1.0, 0.0)


def middle(owned, owners, ray_slot, blocks, volume, halos, counts, prints):
    rows, slices, pixels = volume.shape
    return pl.pallas_call(
        functools.partial(middle_kernel, owned),
        out_shape=(
            jax.ShapeDtypeStruct(volume.shape, F32),
            jax.ShapeDtypeStruct((prints.shape[0], prints.shape[2], prints.shape[1]), BF16),
            jax.ShapeDtypeStruct((rows, counts.shape[0]), BF16),
            jax.ShapeDtypeStruct((owners, lanes), F32),
        ),
        in_specs=[SMEM] + [VMEM] * 8,
        out_specs=(VMEM,) * 4,
        scratch_shapes=[pltpu.VMEM((rows, pixels), F32)],
        name="middle",
    )(ray_slot, blocks, volume, *halos, counts, prints)


def residual_kernel(arrived, picks, measured, weights, returned, second):
    owners = arrived.shape[0]
    sums = [jnp.zeros(measured.shape[1:], F32) for _ in range(2)]
    for j in range(owners):
        part = arrived[j].astype(F32)
        chosen = picks[j : j + 1, :] > 0.5
        sums[0] = sums[0] + jnp.where(chosen, 0.0, part)
        sums[1] = sums[1] + jnp.where(chosen, part, 0.0)
    out = [(weights[i] * (sums[i] - measured[i])).astype(BF16).astype(F32) for i in range(2)]
    for j in range(owners):
        returned[j] = jnp.where(picks[j : j + 1, :] > 0.5, out[1], out[0]).astype(BF16)


def residual(arrived, picks, measured, weights):
    return pl.pallas_call(
        residual_kernel,
        out_shape=jax.ShapeDtypeStruct(arrived.shape, BF16),
        in_specs=[VMEM] * 4,
        out_specs=VMEM,
        scratch_shapes=[pltpu.VMEM((8, lanes), F32)],
        name="residual",
    )(arrived, picks, measured, weights)


def backward_kernel(
    touch, table, returned, turned, counts_turned, base, out, gathered, spread, out_buf, sems
):
    rows, slices, pixels = base.shape
    owners = returned.shape[0]
    foot_count = turned.shape[0]
    codes = foot_count * touch
    gathered[...] = jnp.zeros_like(gathered)
    for t in range(owners):
        place = table[0, t]

        @pl.when(place >= 0)
        def _(t=t, place=place):
            gathered[pl.ds(place, slices, stride=touch), :] = returned[t].astype(F32)

    step = 256
    deep = step // touch

    @pl.loop(0, slices * touch // step)
    def _(m):
        part = gathered[pl.ds(pl.multiple_of(m * step, step), step), :].astype(BF16)
        for f in range(0, foot_count, 2):
            wide = jnp.concatenate([turned[f], turned[f + 1]], axis=1)
            value = jnp.dot(part, wide, preferred_element_type=F32).astype(BF16)
            for i in range(deep):
                for g in range(2):
                    row = (m * (deep // 2) + i // 2) * codes + (f + g) * touch
                    spread[
                        pl.ds(pl.multiple_of(row, touch), touch),
                        (i % 2) * pixels : (i % 2 + 1) * pixels,
                    ] = value[i * touch : (i + 1) * touch, g * pixels : (g + 1) * pixels]

    base_flat = base.reshape(rows * slices, pixels)
    chunk_count = sems.shape[0]
    depth = slices // chunk_count
    copies = []
    for c in range(chunk_count):

        @pl.loop(0, depth // 2)
        def _(i, c=c):
            z = c * depth + 2 * i
            row = (c * (depth // 2) + i) * codes
            grad = jnp.dot(
                counts_turned[...],
                spread[pl.ds(pl.multiple_of(row, codes), codes), :],
                preferred_element_type=F32,
            )
            for g in range(2):
                span = pl.ds(z + g, rows, stride=slices)
                out_buf[span, :] = jnp.maximum(
                    base_flat[span, :] - step_length * grad[:, g * pixels : (g + 1) * pixels], 0.0
                )

        span = pl.ds(c * depth, depth)
        copies.append(
            pltpu.make_async_copy(
                out_buf.reshape(rows, slices, pixels).at[:, span, :],
                out.at[:, span, :],
                sems.at[c],
            )
        )
        copies[c].start()
    for copy in copies:
        copy.wait()


def backward(touch, table, returned, turned, counts_turned, base):
    rows, slices, pixels = base.shape
    codes = turned.shape[0] * touch
    chunks = 4
    return pl.pallas_call(
        functools.partial(backward_kernel, touch),
        out_shape=jax.ShapeDtypeStruct(base.shape, F32),
        in_specs=[SMEM] + [VMEM] * 4,
        out_specs=ANY,
        scratch_shapes=[
            pltpu.VMEM((slices * touch, pixels), F32),
            pltpu.VMEM((slices // 2 * codes, 2 * pixels), BF16),
            pltpu.VMEM((rows * slices, pixels), F32),
            pltpu.SemaphoreType.DMA((chunks,)),
        ],
        name="backward",
    )(table, returned, turned, counts_turned, base)


def shifted(x, axis, forward_way):
    count = lax.axis_size(axis)
    if forward_way:
        pairs = [(i, i + 1) for i in range(count - 1)]
    else:
        pairs = [(i + 1, i) for i in range(count - 1)]
    return lax.ppermute(x, axis, pairs)


def per_device(volume, footprints, foot_index, ray_block, ray_slot, measured, weights):
    row_count, slice_count, pixels = volume.shape
    owners = lax.axis_size("tile")
    owned = measured.shape[0]
    touch = owners // 2
    blocks = ray_block.T
    sent, table, counts, head, tail = forward(
        touch, owned, owners, ray_slot, blocks, foot_index.T, volume, footprints
    )
    before_slice = shifted(tail, "slab", True)
    after_slice = shifted(head, "slab", False)
    arrived = lax.all_to_all(sent, "tile", split_axis=0, concat_axis=0, tiled=True)

    def edge(r):
        return jnp.concatenate(
            [before_slice[r : r + 1], volume[r], after_slice[r : r + 1]], axis=0
        )

    before_row = shifted(edge(row_count - 1), "tile", True)
    after_row = shifted(edge(0), "tile", False)
    base, turned, counts_turned, picks = middle(
        owned, owners, ray_slot, blocks, volume,
        (before_slice, after_slice, before_row, after_row), counts, footprints,
    )
    answer = residual(arrived, picks, measured, weights)
    returned = lax.all_to_all(answer, "tile", split_axis=0, concat_axis=0, tiled=True)
    return backward(touch, table, returned, turned, counts_turned, base)


def solution(mesh):
    in_specs = (
        P("tile", "slab", None),
        P(),
        P("tile", None),
        P(),
        P(),
        P("tile", "slab", None),
        P("tile", "slab", None),
    )
    out_specs = P("tile", "slab", None)
    return jax.shard_map(
        per_device, mesh=mesh, in_specs=in_specs, out_specs=out_specs, check_vma=False
    )
```

```python
import functools

import jax
import jax.numpy as jnp
from jax import lax
from jax.experimental import pallas as pl
from jax.experimental.pallas import tpu as pltpu
from jax.sharding import PartitionSpec as P

smoothing = 0.04
step_length = 2.0
variation_weight = 1.0
lanes = 128

F32 = jnp.float32
BF16 = jnp.bfloat16
VMEM = pl.BlockSpec(memory_space=pltpu.VMEM)
SMEM = pl.BlockSpec(memory_space=pltpu.SMEM)
HBM = pl.BlockSpec(memory_space=pltpu.HBM)


def in_hbm(*arrays):
    return [pltpu.with_memory_space_constraint(x, pltpu.HBM) for x in arrays]


def iota(shape, dim):
    return lax.broadcasted_iota(jnp.int32, shape, dim)


def forward_kernel(
    touch, owned, ray_slot, blocks, foots, volume, prints,
    sent, table, counts, head, tail,
    window, foots_buf, slot_buf, by_slice, prints_buf, grouped, sums, compact, table_buf,
    sems, small_sems, table_sem, prints_sem,
):
    row_count, slice_count, pixels = volume.shape
    foot_count = prints.shape[0]
    owners = sent.shape[0]
    crossings = blocks.shape[0]

    def slice_copy(z):
        return pltpu.make_async_copy(volume.at[:, z, :], by_slice.at[z], sems.at[z])

    position = lax.axis_index("tile")
    offset = position * row_count
    limit = blocks.shape[1] - 2 * lanes
    base = jnp.minimum((offset // lanes) * lanes, limit)
    small = [
        pltpu.make_async_copy(source, target, small_sems.at[i])
        for i, (source, target) in enumerate(
            [
                (blocks.at[:, pl.ds(pl.multiple_of(base, lanes), 2 * lanes)], window),
                (foots, foots_buf),
                (ray_slot, slot_buf),
            ]
        )
    ]
    for copy in small:
        copy.start()
    for z in range(slice_count):
        slice_copy(z).start()
    prints_copy = pltpu.make_async_copy(prints, prints_buf, prints_sem)
    prints_copy.start()

    for copy in small:
        copy.wait()
    mine = pltpu.roll(window[...], 2 * lanes - (offset - base), 1)[:, :lanes]
    slot = jnp.zeros_like(mine)
    for b in range(ray_slot.shape[0]):
        slot = jnp.where(mine == b, slot_buf[b], slot)
    valid = iota((crossings, lanes), 1) < row_count
    owner = jnp.where(valid, slot // owned, -1)
    label = iota((owners, lanes), 0)
    present = jnp.zeros((owners, lanes), F32)
    for k in range(crossings):
        present = jnp.where(owner[k : k + 1] == label, 1.0, present)
    present = jnp.broadcast_to(jnp.max(present, axis=1, keepdims=True), (owners, lanes))
    lower = (iota((owners, owners), 1) < iota((owners, owners), 0)).astype(BF16)
    rank = jnp.dot(lower, present.astype(BF16), preferred_element_type=F32)
    column = iota((owners, lanes), 1)
    rank_row = jnp.sum(jnp.where(label < column, present, 0.0), axis=0, keepdims=True)
    present_row = jnp.sum(jnp.where(label == column, present, 0.0), axis=0, keepdims=True)
    rank_row = jnp.where(present_row > 0.5, rank_row, -1.0).astype(jnp.int32)
    match = jnp.where((rank.astype(jnp.int32) == column) & (present > 0.5), label + 1, 0)
    owner_row = jnp.sum(match, axis=0, keepdims=True) - 1
    table_buf[...] = jnp.where(iota(table_buf.shape, 0) == 0, rank_row, owner_row)
    table_copy = pltpu.make_async_copy(table_buf, table, table_sem)
    table_copy.start()

    foots_here = jnp.concatenate(
        [foots_buf[...], jnp.zeros((crossings, lanes - row_count), jnp.int32)], axis=1
    )
    codes = []
    for k in range(crossings):
        place = jnp.sum(
            jnp.where(owner[k : k + 1] == label, rank, 0.0), axis=0, keepdims=True
        ).astype(jnp.int32)
        codes.append(jnp.where(valid[k : k + 1], foots_here[k : k + 1] * touch + place, -1))
    part = 4 * touch
    for first in range(0, foot_count * touch, part):
        code_row = iota((part, lanes), 0) + first
        total = jnp.zeros((part, lanes), F32)
        for code in codes:
            total = total + jnp.where(code_row == code, 1.0, 0.0)
        counts[first : first + part] = total.astype(BF16)

    group_size = 4

    @pl.loop(0, slice_count // group_size)
    def _(i):
        for j in range(group_size):
            slice_copy(i * group_size + j).wait()
        for j in range(0, group_size, 2):
            z = i * group_size + j
            pair = jnp.concatenate([by_slice[z], by_slice[z + 1]], axis=1).astype(BF16)
            group = jnp.dot(counts[:, :row_count], pair, preferred_element_type=F32).astype(BF16)
            for half in range(2):
                for f in range(foot_count):
                    grouped[
                        f // 2,
                        pl.ds(pl.multiple_of((z + half) * touch, touch), touch),
                        (f % 2) * pixels : (f % 2 + 1) * pixels,
                    ] = group[f * touch : (f + 1) * touch, half * pixels : (half + 1) * pixels]

    head[...] = by_slice[0]
    tail[...] = by_slice[slice_count - 1]
    prints_copy.wait()
    sums[...] = jnp.zeros_like(sums)

    @pl.loop(0, foot_count // 4)
    def _(g):
        block = 256
        for m in range(0, slice_count * touch, block):
            span = slice(m, m + block)
            total = sums[span]
            for h in range(2):
                weight = prints_buf[pl.ds(4 * g + 2 * h, 2)].reshape(2 * pixels, -1)
                total = total + jnp.dot(
                    grouped[2 * g + h, span], weight, preferred_element_type=F32
                )
            sums[span] = total

    compact[...] = jnp.swapaxes(sums[...].reshape(slice_count, touch, -1), 0, 1).astype(BF16)
    table_copy.wait()
    for t in range(owners):
        place = table[0, t]
        block = compact[jnp.maximum(place, 0)]
        sent[t] = jnp.where(place >= 0, block, jnp.zeros_like(block))


def forward(touch, owned, owners, ray_slot, blocks, foots, volume, prints):
    rows, slices, pixels = volume.shape
    foot_count, _, rays = prints.shape
    return pl.pallas_call(
        functools.partial(forward_kernel, touch, owned),
        out_shape=(
            jax.ShapeDtypeStruct((owners, slices, rays), BF16),
            jax.ShapeDtypeStruct((8, lanes), jnp.int32),
            jax.ShapeDtypeStruct((foot_count * touch, lanes), BF16),
            jax.ShapeDtypeStruct((rows, pixels), F32),
            jax.ShapeDtypeStruct((rows, pixels), F32),
        ),
        in_specs=[HBM] * 5,
        out_specs=(VMEM, SMEM, VMEM, VMEM, VMEM),
        scratch_shapes=[
            pltpu.VMEM((blocks.shape[0], 2 * lanes), jnp.int32),
            pltpu.VMEM(foots.shape, jnp.int32),
            pltpu.SMEM(ray_slot.shape, jnp.int32),
            pltpu.VMEM((slices, rows, pixels), F32),
            pltpu.VMEM(prints.shape, BF16),
            pltpu.VMEM((foot_count // 2, slices * touch, 2 * pixels), BF16),
            pltpu.VMEM((slices * touch, rays), F32),
            pltpu.VMEM((touch, slices, rays), BF16),
            pltpu.VMEM((8, lanes), jnp.int32),
            pltpu.SemaphoreType.DMA((slices,)),
            pltpu.SemaphoreType.DMA((3,)),
            pltpu.SemaphoreType.DMA,
            pltpu.SemaphoreType.DMA,
        ],
        compiler_params=pltpu.CompilerParams(vmem_limit_bytes=24 << 20),
        name="forward",
    )(*in_hbm(ray_slot, blocks, foots, volume, prints))


def tables_kernel(owned, ray_slot, blocks, counts, counts_turned, picks):
    position = lax.axis_index("tile")
    rows = counts_turned.shape[0]

    counts_turned[...] = counts[...].astype(F32).T[:rows].astype(BF16)

    owners = picks.shape[0]
    width = blocks.shape[1]
    second = jnp.int32(0)
    for b in range(ray_slot.shape[0]):
        second = jnp.where(ray_slot[b] == position * owned + 1, b, second)
    hit = jnp.max(jnp.where(blocks[...] == second, 1.0, 0.0), axis=0, keepdims=True)
    start = iota((owners, width), 0) * rows
    at = iota((owners, width), 1)
    member = ((at >= start) & (at < start + rows)).astype(BF16)
    count = lax.dot_general(
        member,
        jnp.broadcast_to(hit, (lanes, width)).astype(BF16),
        (((1,), (1,)), ((), ())),
        preferred_element_type=F32,
    )
    picks[...] = jnp.where(count > 0.5, 1.0, 0.0)


def tables(owned, owners, rows, ray_slot, blocks, counts):
    return pl.pallas_call(
        functools.partial(tables_kernel, owned),
        out_shape=(
            jax.ShapeDtypeStruct((rows, counts.shape[0]), BF16),
            jax.ShapeDtypeStruct((owners, lanes), F32),
        ),
        in_specs=[SMEM] + [VMEM] * 2,
        out_specs=(VMEM,) * 2,
        compiler_params=pltpu.CompilerParams(vmem_limit_bytes=8 << 20),
        name="tables",
    )(ray_slot, blocks, counts)


def variation_kernel(
    volume, before_slice, after_slice, before_row, after_row, first_row,
    base, by_slice, row_flux, sems,
):
    slices, rows, pixels = base.shape

    def slice_copy(z):
        return pltpu.make_async_copy(volume.at[:, z, :], by_slice.at[z], sems.at[z])

    for z in range(slices):
        slice_copy(z).start()
    position = lax.axis_index("tile")
    layer = lax.axis_index("slab")
    last_position = lax.axis_size("tile") - 1
    last_layer = lax.axis_size("slab") - 1
    lane = iota((1, pixels), 1)
    inner = lane < pixels - 1
    first = lane == 0

    def col_grad(x):
        return jnp.where(inner, pltpu.roll(x, pixels - 1, 1) - x, 0.0)

    def scale(a, b, c):
        return lax.rsqrt(a * a + b * b + c * c + smoothing)

    low = before_row[1 : slices + 1]
    z_id = iota((slices, 1), 0)
    grad_slices = before_row[2 : slices + 2] - low
    grad_slices = jnp.where((z_id == slices - 1) & (layer == last_layer), 0.0, grad_slices)
    grad_rows = first_row[...] - low
    flux = grad_rows * scale(grad_rows, grad_slices, col_grad(low))
    row_flux[...] = jnp.where(position == 0, 0.0, flux)

    row_id = iota((rows, 1), 0)
    top = row_id == rows - 1
    bottom = row_id == 0
    keep = jnp.where(top & (position == last_position), 0.0, 1.0)

    def fluxes(here, next_slice, beyond, last):
        up = jnp.where(top, beyond, pltpu.roll(here, rows - 1, 0))
        grad_rows = (up - here) * keep
        grad_slices = jnp.where(last, 0.0, next_slice - here)
        grad_cols = col_grad(here)
        inverse = scale(grad_rows, grad_slices, grad_cols)
        return grad_rows * inverse, grad_slices * inverse, grad_cols * inverse

    slice_copy(0).wait()
    _, start, _ = fluxes(before_slice[...], by_slice[0], after_row[0:1], False)
    start = jnp.where(layer == 0, 0.0, start)

    def one(z, here, next_slice, previous, last):
        flux_rows, flux_slices, flux_cols = fluxes(
            here, next_slice, after_row[pl.ds(z + 1, 1), :], last
        )
        below = jnp.where(bottom, row_flux[pl.ds(z, 1), :], pltpu.roll(flux_rows, 1, 0))
        left = jnp.where(first, 0.0, pltpu.roll(flux_cols, 1, 1))
        variation = (previous - flux_slices) + (below - flux_rows) + (left - flux_cols)
        base[z] = here - (step_length * variation_weight) * variation
        return flux_slices

    def step(z, previous):
        slice_copy(z + 1).wait()
        return one(z, by_slice[z], by_slice[z + 1], previous, False)

    final = lax.fori_loop(0, slices - 1, step, start)
    one(slices - 1, by_slice[slices - 1], after_slice[...], final, layer == last_layer)


def variation(volume, *halos):
    rows, slices, pixels = volume.shape
    return pl.pallas_call(
        variation_kernel,
        out_shape=jax.ShapeDtypeStruct((slices, rows, pixels), F32),
        in_specs=[HBM] + [VMEM] * 5,
        out_specs=VMEM,
        scratch_shapes=[
            pltpu.VMEM((slices, rows, pixels), F32),
            pltpu.VMEM((slices, pixels), F32),
            pltpu.SemaphoreType.DMA((slices,)),
        ],
        compiler_params=pltpu.CompilerParams(vmem_limit_bytes=8 << 20),
        name="variation",
    )(*in_hbm(volume), *halos)


def residual_kernel(arrived, picks, measured, weights, returned):
    owners = arrived.shape[0]
    sums = [jnp.zeros(measured.shape[1:], F32) for _ in range(2)]
    for j in range(owners):
        part = arrived[j].astype(F32)
        chosen = picks[j : j + 1, :] > 0.5
        sums[0] = sums[0] + jnp.where(chosen, 0.0, part)
        sums[1] = sums[1] + jnp.where(chosen, part, 0.0)
    out = [(weights[i] * (sums[i] - measured[i])).astype(BF16).astype(F32) for i in range(2)]
    for j in range(owners):
        returned[j] = jnp.where(picks[j : j + 1, :] > 0.5, out[1], out[0]).astype(BF16)


def residual(arrived, picks, measured, weights):
    return pl.pallas_call(
        residual_kernel,
        out_shape=jax.ShapeDtypeStruct(arrived.shape, BF16),
        in_specs=[VMEM] * 4,
        out_specs=VMEM,
        compiler_params=pltpu.CompilerParams(vmem_limit_bytes=4 << 20),
        name="residual",
    )(arrived, picks, measured, weights)


def backward_kernel(
    touch, table, returned, prints, counts_turned, base,
    out, gathered, mixed, spread, out_buf, sems,
):
    slices, rows, pixels = base.shape
    foot_count, _, rays = prints.shape
    codes = foot_count * touch
    for s in range(touch):
        owner = table[1, s]
        block = returned[jnp.maximum(owner, 0)].astype(F32)
        gathered[s] = jnp.where(owner >= 0, block, 0.0)
    mixed[...] = jnp.swapaxes(gathered[...], 0, 1).reshape(slices * touch, rays).astype(BF16)
    deep = 16

    @pl.loop(0, foot_count // 4)
    def _(g):
        for f in range(0, 4, 2):
            wide = prints[pl.ds(4 * g + f, 2)].reshape(2 * pixels, rays)
            for z in range(0, slices, deep):
                value = lax.dot_general(
                    mixed[z * touch : (z + deep) * touch, :],
                    wide,
                    (((1,), (1,)), ((), ())),
                    preferred_element_type=F32,
                ).astype(BF16)
                for i in range(deep):
                    for h in range(2):
                        row = (4 * g + f + h) * touch
                        spread[
                            (z + i) // 2,
                            pl.ds(pl.multiple_of(row, touch), touch),
                            (i % 2) * pixels : (i % 2 + 1) * pixels,
                        ] = value[i * touch : (i + 1) * touch, h * pixels : (h + 1) * pixels]

    def slice_copy(z):
        return pltpu.make_async_copy(out_buf.at[z], out.at[:, z, :], sems.at[z])

    group_size = 4

    @pl.loop(0, slices // group_size)
    def _(i):
        for j in range(0, group_size, 2):
            z = i * group_size + j
            grad = jnp.dot(
                counts_turned[...],
                spread[i * (group_size // 2) + j // 2],
                preferred_element_type=F32,
            )
            for g in range(2):
                out_buf[z + g] = jnp.maximum(
                    base[z + g] - step_length * grad[:, g * pixels : (g + 1) * pixels], 0.0
                )
        for j in range(group_size):
            slice_copy(i * group_size + j).start()

    @pl.loop(0, slices)
    def _(z):
        slice_copy(z).wait()


def backward(touch, table, returned, prints, counts_turned, base):
    slices, rows, pixels = base.shape
    codes = prints.shape[0] * touch
    return pl.pallas_call(
        functools.partial(backward_kernel, touch),
        out_shape=jax.ShapeDtypeStruct((rows, slices, pixels), F32),
        in_specs=[SMEM] + [VMEM] * 4,
        out_specs=HBM,
        scratch_shapes=[
            pltpu.VMEM((touch, slices, prints.shape[2]), F32),
            pltpu.VMEM((slices * touch, prints.shape[2]), BF16),
            pltpu.VMEM((slices // 2, codes, 2 * pixels), BF16),
            pltpu.VMEM((slices, rows, pixels), F32),
            pltpu.SemaphoreType.DMA((slices,)),
        ],
        compiler_params=pltpu.CompilerParams(vmem_limit_bytes=24 << 20),
        name="backward",
    )(table, returned, prints, counts_turned, base)


def shifted(x, axis, forward_way):
    count = lax.axis_size(axis)
    if forward_way:
        pairs = [(i, i + 1) for i in range(count - 1)]
    else:
        pairs = [(i + 1, i) for i in range(count - 1)]
    return lax.ppermute(x, axis, pairs)


def per_device(volume, footprints, foot_index, ray_block, ray_slot, measured, weights):
    row_count, slice_count, pixels = volume.shape
    owners = lax.axis_size("tile")
    owned = measured.shape[0]
    touch = owners // 2
    blocks = ray_block.T
    sent, table, counts, head, tail = forward(
        touch, owned, owners, ray_slot, blocks, foot_index.T, volume, footprints
    )
    before_slice = shifted(tail, "slab", True)
    after_slice = shifted(head, "slab", False)
    arrived = lax.all_to_all(sent, "tile", split_axis=0, concat_axis=0, tiled=True)
    counts_turned, picks = tables(owned, owners, row_count, ray_slot, blocks, counts)

    def edge(r):
        return jnp.concatenate(
            [before_slice[r : r + 1], volume[r], after_slice[r : r + 1]], axis=0
        )

    first_edge, last_edge = edge(0), edge(row_count - 1)
    before_row = shifted(last_edge, "tile", True)
    after_row = shifted(first_edge, "tile", False)
    arrived, before_row, after_row = lax.optimization_barrier((arrived, before_row, after_row))
    answer = residual(arrived, picks, measured, weights)
    returned = lax.all_to_all(answer, "tile", split_axis=0, concat_axis=0, tiled=True)
    halos, _ = lax.optimization_barrier(
        ((before_slice, after_slice, before_row, after_row, volume[0]), answer)
    )
    base = variation(volume, *halos)
    return backward(touch, table, returned, footprints, counts_turned, base)


def solution(mesh):
    in_specs = (
        P("tile", "slab", None),
        P(),
        P("tile", None),
        P(),
        P(),
        P("tile", "slab", None),
        P("tile", "slab", None),
    )
    out_specs = P("tile", "slab", None)
    return jax.shard_map(
        per_device, mesh=mesh, in_specs=in_specs, out_specs=out_specs, check_vma=False
    )
```

```python
import functools

import jax
import jax.numpy as jnp
from jax import lax
from jax.experimental import pallas as pl
from jax.experimental.pallas import tpu as pltpu
from jax.sharding import PartitionSpec as P


smoothing = 0.04
step_length = 2.0
variation_weight = 1.0
lanes = 128

F32 = jnp.float32
BF16 = jnp.bfloat16
VMEM = pl.BlockSpec(memory_space=pltpu.VMEM)
SMEM = pl.BlockSpec(memory_space=pltpu.SMEM)
HBM = pl.BlockSpec(memory_space=pltpu.HBM)


def in_hbm(*arrays):
    return [pltpu.with_memory_space_constraint(x, pltpu.HBM) for x in arrays]


def iota(shape, dim):
    return lax.broadcasted_iota(jnp.int32, shape, dim)


def forward_kernel(
    touch, owned, ray_slot, blocks, foots, volume, prints,
    sent, table, counts, head, tail,
    window, foots_buf, slot_buf, by_slice, prints_buf, grouped, sums, compact, table_buf,
    sems, small_sems, table_sem, prints_sem,
):
    row_count, slice_count, pixels = volume.shape
    foot_count = prints.shape[0]
    owners = sent.shape[0]
    crossings = blocks.shape[0]

    def slice_copy(z):
        return pltpu.make_async_copy(volume.at[:, z, :], by_slice.at[z], sems.at[z])

    position = lax.axis_index("tile")
    offset = position * row_count
    limit = blocks.shape[1] - 2 * lanes
    base = jnp.minimum((offset // lanes) * lanes, limit)
    small = [
        pltpu.make_async_copy(source, target, small_sems.at[i])
        for i, (source, target) in enumerate(
            [
                (blocks.at[:, pl.ds(pl.multiple_of(base, lanes), 2 * lanes)], window),
                (foots, foots_buf),
                (ray_slot, slot_buf),
            ]
        )
    ]
    for copy in small:
        copy.start()
    for z in range(slice_count):
        slice_copy(z).start()
    prints_copy = pltpu.make_async_copy(prints, prints_buf, prints_sem)
    prints_copy.start()

    for copy in small:
        copy.wait()
    mine = pltpu.roll(window[...], 2 * lanes - (offset - base), 1)[:, :lanes]
    slot = jnp.zeros_like(mine)
    for b in range(ray_slot.shape[0]):
        slot = jnp.where(mine == b, slot_buf[b], slot)
    valid = iota((crossings, lanes), 1) < row_count
    owner = jnp.where(valid, slot // owned, -1)
    label = iota((owners, lanes), 0)
    present = jnp.zeros((owners, lanes), F32)
    for k in range(crossings):
        present = jnp.where(owner[k : k + 1] == label, 1.0, present)
    present = jnp.broadcast_to(jnp.max(present, axis=1, keepdims=True), (owners, lanes))
    lower = (iota((owners, owners), 1) < iota((owners, owners), 0)).astype(BF16)
    rank = jnp.dot(lower, present.astype(BF16), preferred_element_type=F32)
    column = iota((owners, lanes), 1)
    rank_row = jnp.sum(jnp.where(label < column, present, 0.0), axis=0, keepdims=True)
    present_row = jnp.sum(jnp.where(label == column, present, 0.0), axis=0, keepdims=True)
    rank_row = jnp.where(present_row > 0.5, rank_row, -1.0).astype(jnp.int32)
    match = jnp.where((rank.astype(jnp.int32) == column) & (present > 0.5), label + 1, 0)
    owner_row = jnp.sum(match, axis=0, keepdims=True) - 1
    table_buf[...] = jnp.where(iota(table_buf.shape, 0) == 0, rank_row, owner_row)
    table_copy = pltpu.make_async_copy(table_buf, table, table_sem)
    table_copy.start()

    foots_here = jnp.concatenate(
        [foots_buf[...], jnp.zeros((crossings, lanes - row_count), jnp.int32)], axis=1
    )
    codes = []
    for k in range(crossings):
        place = jnp.sum(
            jnp.where(owner[k : k + 1] == label, rank, 0.0), axis=0, keepdims=True
        ).astype(jnp.int32)
        codes.append(jnp.where(valid[k : k + 1], foots_here[k : k + 1] * touch + place, -1))
    part = 4 * touch
    for first in range(0, foot_count * touch, part):
        code_row = iota((part, lanes), 0) + first
        total = jnp.zeros((part, lanes), F32)
        for code in codes:
            total = total + jnp.where(code_row == code, 1.0, 0.0)
        counts[first : first + part] = total.astype(BF16)

    group_size = 8

    @pl.loop(0, slice_count // group_size)
    def _(i):
        for j in range(group_size):
            slice_copy(i * group_size + j).wait()
        for j in range(0, group_size, 2):
            z = i * group_size + j
            pair = jnp.concatenate([by_slice[z], by_slice[z + 1]], axis=1).astype(BF16)
            group = jnp.dot(counts[:, :row_count], pair, preferred_element_type=F32).astype(BF16)
            for half in range(2):
                for f in range(foot_count):
                    grouped[
                        f // 2,
                        pl.ds(pl.multiple_of((z + half) * touch, touch), touch),
                        (f % 2) * pixels : (f % 2 + 1) * pixels,
                    ] = group[f * touch : (f + 1) * touch, half * pixels : (half + 1) * pixels]

    head[...] = by_slice[0]
    tail[...] = by_slice[slice_count - 1]
    prints_copy.wait()
    sums[...] = jnp.zeros_like(sums)

    @pl.loop(0, foot_count // 8)
    def _(g):
        block = 256
        for m in range(0, slice_count * touch, block):
            span = slice(m, m + block)
            total = sums[span]
            for h in range(4):
                weight = prints_buf[pl.ds(8 * g + 2 * h, 2)].reshape(2 * pixels, -1)
                total = total + jnp.dot(
                    grouped[4 * g + h, span], weight, preferred_element_type=F32
                )
            sums[span] = total

    compact[...] = jnp.swapaxes(sums[...].reshape(slice_count, touch, -1), 0, 1).astype(BF16)
    table_copy.wait()
    for t in range(owners):
        place = table[0, t]
        block = compact[jnp.maximum(place, 0)]
        sent[t] = jnp.where(place >= 0, block, jnp.zeros_like(block))


def forward(touch, owned, owners, ray_slot, blocks, foots, volume, prints):
    rows, slices, pixels = volume.shape
    foot_count, _, rays = prints.shape
    return pl.pallas_call(
        functools.partial(forward_kernel, touch, owned),
        out_shape=(
            jax.ShapeDtypeStruct((owners, slices, rays), BF16),
            jax.ShapeDtypeStruct((8, lanes), jnp.int32),
            jax.ShapeDtypeStruct((foot_count * touch, lanes), BF16),
            jax.ShapeDtypeStruct((rows, pixels), F32),
            jax.ShapeDtypeStruct((rows, pixels), F32),
        ),
        in_specs=[HBM] * 5,
        out_specs=(VMEM, SMEM, VMEM, VMEM, VMEM),
        scratch_shapes=[
            pltpu.VMEM((blocks.shape[0], 2 * lanes), jnp.int32),
            pltpu.VMEM(foots.shape, jnp.int32),
            pltpu.SMEM(ray_slot.shape, jnp.int32),
            pltpu.VMEM((slices, rows, pixels), F32),
            pltpu.VMEM(prints.shape, BF16),
            pltpu.VMEM((foot_count // 2, slices * touch, 2 * pixels), BF16),
            pltpu.VMEM((slices * touch, rays), F32),
            pltpu.VMEM((touch, slices, rays), BF16),
            pltpu.VMEM((8, lanes), jnp.int32),
            pltpu.SemaphoreType.DMA((slices,)),
            pltpu.SemaphoreType.DMA((3,)),
            pltpu.SemaphoreType.DMA,
            pltpu.SemaphoreType.DMA,
        ],
        compiler_params=pltpu.CompilerParams(vmem_limit_bytes=24 << 20),
        name="forward",
    )(*in_hbm(ray_slot, blocks, foots, volume, prints))


def tables_kernel(owned, ray_slot, blocks, counts, counts_turned, picks):
    position = lax.axis_index("tile")
    rows = counts_turned.shape[0]

    counts_turned[...] = counts[...].astype(F32).T[:rows].astype(BF16)

    owners = picks.shape[0]
    width = blocks.shape[1]
    second = jnp.int32(0)
    for b in range(ray_slot.shape[0]):
        second = jnp.where(ray_slot[b] == position * owned + 1, b, second)
    hit = jnp.max(jnp.where(blocks[...] == second, 1.0, 0.0), axis=0, keepdims=True)
    start = iota((owners, width), 0) * rows
    at = iota((owners, width), 1)
    member = ((at >= start) & (at < start + rows)).astype(BF16)
    count = lax.dot_general(
        member,
        jnp.broadcast_to(hit, (lanes, width)).astype(BF16),
        (((1,), (1,)), ((), ())),
        preferred_element_type=F32,
    )
    picks[...] = jnp.where(count > 0.5, 1.0, 0.0)


def tables(owned, owners, rows, ray_slot, blocks, counts):
    return pl.pallas_call(
        functools.partial(tables_kernel, owned),
        out_shape=(
            jax.ShapeDtypeStruct((rows, counts.shape[0]), BF16),
            jax.ShapeDtypeStruct((owners, lanes), F32),
        ),
        in_specs=[SMEM] + [VMEM] * 2,
        out_specs=(VMEM,) * 2,
        compiler_params=pltpu.CompilerParams(vmem_limit_bytes=8 << 20),
        name="tables",
    )(ray_slot, blocks, counts)


def variation_kernel(
    volume, before_slice, after_slice, before_row, after_row, first_row,
    base, by_slice, row_flux, sems,
):
    slices, rows, pixels = base.shape

    def slice_copy(z):
        return pltpu.make_async_copy(volume.at[:, z, :], by_slice.at[z], sems.at[z])

    for z in range(slices):
        slice_copy(z).start()
    position = lax.axis_index("tile")
    layer = lax.axis_index("slab")
    last_position = lax.axis_size("tile") - 1
    last_layer = lax.axis_size("slab") - 1
    lane = iota((1, pixels), 1)
    inner = lane < pixels - 1
    first = lane == 0

    def col_grad(x):
        return jnp.where(inner, pltpu.roll(x, pixels - 1, 1) - x, 0.0)

    def scale(a, b, c):
        return lax.rsqrt(a * a + b * b + c * c + smoothing)

    low = before_row[...]
    z_id = iota((slices, 1), 0)
    above = jnp.where(z_id == slices - 1, after_slice[0:1], pltpu.roll(low, slices - 1, 0))
    grad_slices = above - low
    grad_slices = jnp.where((z_id == slices - 1) & (layer == last_layer), 0.0, grad_slices)
    grad_rows = first_row[...] - low
    flux = grad_rows * scale(grad_rows, grad_slices, col_grad(low))
    row_flux[...] = jnp.where(position == 0, 0.0, flux)

    row_id = iota((rows, 1), 0)
    top = row_id == rows - 1
    bottom = row_id == 0
    keep = jnp.where(top & (position == last_position), 0.0, 1.0)

    def fluxes(here, next_slice, beyond, last):
        up = jnp.where(top, beyond, pltpu.roll(here, rows - 1, 0))
        grad_rows = (up - here) * keep
        grad_slices = jnp.where(last, 0.0, next_slice - here)
        grad_cols = col_grad(here)
        inverse = scale(grad_rows, grad_slices, grad_cols)
        return grad_rows * inverse, grad_slices * inverse, grad_cols * inverse

    slice_copy(0).wait()
    _, start, _ = fluxes(
        before_slice[1 : rows + 1], by_slice[0], before_slice[rows + 1 : rows + 2], False
    )
    start = jnp.where(layer == 0, 0.0, start)

    def one(z, here, next_slice, previous, last):
        flux_rows, flux_slices, flux_cols = fluxes(
            here, next_slice, after_row[pl.ds(z, 1), :], last
        )
        below = jnp.where(bottom, row_flux[pl.ds(z, 1), :], pltpu.roll(flux_rows, 1, 0))
        left = jnp.where(first, 0.0, pltpu.roll(flux_cols, 1, 1))
        variation = (previous - flux_slices) + (below - flux_rows) + (left - flux_cols)
        base[z] = here - (step_length * variation_weight) * variation
        return flux_slices

    def step(z, previous):
        slice_copy(z + 1).wait()
        return one(z, by_slice[z], by_slice[z + 1], previous, False)

    final = lax.fori_loop(0, slices - 1, step, start)
    one(slices - 1, by_slice[slices - 1], after_slice[1 : rows + 1], final, layer == last_layer)


def variation(volume, *halos):
    rows, slices, pixels = volume.shape
    return pl.pallas_call(
        variation_kernel,
        out_shape=jax.ShapeDtypeStruct((slices, rows, pixels), F32),
        in_specs=[HBM] + [VMEM] * 5,
        out_specs=VMEM,
        scratch_shapes=[
            pltpu.VMEM((slices, rows, pixels), F32),
            pltpu.VMEM((slices, pixels), F32),
            pltpu.SemaphoreType.DMA((slices,)),
        ],
        compiler_params=pltpu.CompilerParams(vmem_limit_bytes=8 << 20),
        name="variation",
    )(*in_hbm(volume), *halos)


def residual_kernel(arrived, picks, measured, weights, returned):
    owners = arrived.shape[0]
    sums = [jnp.zeros(measured.shape[1:], F32) for _ in range(2)]
    for j in range(owners):
        part = arrived[j].astype(F32)
        chosen = picks[j : j + 1, :] > 0.5
        sums[0] = sums[0] + jnp.where(chosen, 0.0, part)
        sums[1] = sums[1] + jnp.where(chosen, part, 0.0)
    out = [(weights[i] * (sums[i] - measured[i])).astype(BF16).astype(F32) for i in range(2)]
    for j in range(owners):
        returned[j] = jnp.where(picks[j : j + 1, :] > 0.5, out[1], out[0]).astype(BF16)


def residual(arrived, picks, measured, weights):
    return pl.pallas_call(
        residual_kernel,
        out_shape=jax.ShapeDtypeStruct(arrived.shape, BF16),
        in_specs=[VMEM] * 4,
        out_specs=VMEM,
        compiler_params=pltpu.CompilerParams(vmem_limit_bytes=4 << 20),
        name="residual",
    )(arrived, picks, measured, weights)


def backward_kernel(
    touch, table, returned, prints, counts_turned, base,
    out, gathered, mixed, spread, out_buf, prints_buf, sems, prints_sems,
):
    slices, _, pixels = base.shape
    foot_count, _, rays = prints.shape
    parts = prints_sems.shape[0]
    per_part = foot_count // parts

    def prints_copy(g):
        span = pl.ds(g * per_part, per_part)
        return pltpu.make_async_copy(prints.at[span], prints_buf.at[span], prints_sems.at[g])

    for g in range(parts):
        prints_copy(g).start()
    for s in range(touch):
        owner = table[1, s]
        block = returned[jnp.maximum(owner, 0)].astype(F32)
        gathered[s] = jnp.where(owner >= 0, block, 0.0)
    mixed[...] = jnp.swapaxes(gathered[...], 0, 1).reshape(slices * touch, rays).astype(BF16)
    deep = 16

    @pl.loop(0, parts)
    def _(g):
        prints_copy(g).wait()
        for f in range(0, per_part, 2):
            wide = prints_buf[pl.ds(per_part * g + f, 2)].reshape(2 * pixels, rays)
            for z in range(0, slices, deep):
                value = lax.dot_general(
                    mixed[z * touch : (z + deep) * touch, :],
                    wide,
                    (((1,), (1,)), ((), ())),
                    preferred_element_type=F32,
                ).astype(BF16)
                for i in range(deep):
                    for h in range(2):
                        row = (per_part * g + f + h) * touch
                        spread[
                            (z + i) // 2,
                            pl.ds(pl.multiple_of(row, touch), touch),
                            (i % 2) * pixels : (i % 2 + 1) * pixels,
                        ] = value[i * touch : (i + 1) * touch, h * pixels : (h + 1) * pixels]

    def slice_copy(z):
        return pltpu.make_async_copy(out_buf.at[z], out.at[:, z, :], sems.at[z])

    group_size = 8

    @pl.loop(0, slices // group_size)
    def _(i):
        for j in range(0, group_size, 2):
            z = i * group_size + j
            grad = jnp.dot(
                counts_turned[...],
                spread[i * (group_size // 2) + j // 2],
                preferred_element_type=F32,
            )
            for g in range(2):
                out_buf[z + g] = jnp.maximum(
                    base[z + g] - step_length * grad[:, g * pixels : (g + 1) * pixels], 0.0
                )
        for j in range(group_size):
            slice_copy(i * group_size + j).start()

    @pl.loop(0, slices)
    def _(z):
        slice_copy(z).wait()


def backward(touch, table, returned, prints, counts_turned, base):
    slices, rows, pixels = base.shape
    codes = prints.shape[0] * touch
    return pl.pallas_call(
        functools.partial(backward_kernel, touch),
        out_shape=jax.ShapeDtypeStruct((rows, slices, pixels), F32),
        in_specs=[SMEM, VMEM, HBM, VMEM, VMEM],
        out_specs=HBM,
        scratch_shapes=[
            pltpu.VMEM((touch, slices, prints.shape[2]), F32),
            pltpu.VMEM((slices * touch, prints.shape[2]), BF16),
            pltpu.VMEM((slices // 2, codes, 2 * pixels), BF16),
            pltpu.VMEM((slices, rows, pixels), F32),
            pltpu.VMEM(prints.shape, BF16),
            pltpu.SemaphoreType.DMA((slices,)),
            pltpu.SemaphoreType.DMA((4,)),
        ],
        compiler_params=pltpu.CompilerParams(vmem_limit_bytes=24 << 20),
        name="backward",
    )(table, returned, *in_hbm(prints), counts_turned, base)


def shifted(x, axis, forward_way):
    count = lax.axis_size(axis)
    if forward_way:
        pairs = [(i, i + 1) for i in range(count - 1)]
    else:
        pairs = [(i + 1, i) for i in range(count - 1)]
    return lax.ppermute(x, axis, pairs)


def per_device(volume, footprints, foot_index, ray_block, ray_slot, measured, weights):
    row_count, slice_count, _ = volume.shape
    owners = lax.axis_size("tile")
    owned = measured.shape[0]
    touch = owners // 2
    blocks = ray_block.T
    sent, table, counts, head, tail = forward(
        touch, owned, owners, ray_slot, blocks, foot_index.T, volume, footprints
    )
    arrived = lax.all_to_all(sent, "tile", split_axis=0, concat_axis=0, tiled=True)
    first_row, last_row, _ = lax.optimization_barrier((volume[0], volume[row_count - 1], head))
    before_row = shifted(last_row, "tile", True)
    after_row = shifted(first_row, "tile", False)
    counts_turned, picks = tables(owned, owners, row_count, ray_slot, blocks, counts)

    def edge(z, x):
        return jnp.concatenate([before_row[z : z + 1], x, after_row[z : z + 1]], axis=0)

    edges = (edge(slice_count - 1, tail), edge(0, head))
    before_slice = shifted(edges[0], "slab", True)
    after_slice = shifted(edges[1], "slab", False)
    arrived, _ = lax.optimization_barrier((arrived, edges))
    answer = residual(arrived, picks, measured, weights)
    returned = lax.all_to_all(answer, "tile", split_axis=0, concat_axis=0, tiled=True)
    halos, _ = lax.optimization_barrier(
        ((before_slice, after_slice, before_row, after_row, first_row), answer)
    )
    base = variation(volume, *halos)
    return backward(touch, table, returned, footprints, counts_turned, base)


def solution(mesh):
    in_specs = (
        P("tile", "slab", None),
        P(),
        P("tile", None),
        P(),
        P(),
        P("tile", "slab", None),
        P("tile", "slab", None),
    )
    out_specs = P("tile", "slab", None)
    return jax.shard_map(
        per_device, mesh=mesh, in_specs=in_specs, out_specs=out_specs, check_vma=False
    )
```

```python
import functools

import jax
import jax.numpy as jnp
from jax import lax
from jax.experimental import pallas as pl
from jax.experimental.pallas import tpu as pltpu
from jax.sharding import PartitionSpec as P


smoothing = 0.04
step_length = 2.0
variation_weight = 1.0
lanes = 128

F32 = jnp.float32
BF16 = jnp.bfloat16
VMEM = pl.BlockSpec(memory_space=pltpu.VMEM)
SMEM = pl.BlockSpec(memory_space=pltpu.SMEM)
HBM = pl.BlockSpec(memory_space=pltpu.HBM)


def in_hbm(*arrays):
    return [pltpu.with_memory_space_constraint(x, pltpu.HBM) for x in arrays]


def iota(shape, dim):
    return lax.broadcasted_iota(jnp.int32, shape, dim)


def forward_kernel(
    touch, owned, ray_slot, blocks, foots, volume, prints,
    sent, table, counts, head, tail, first_row, last_row,
    window, foots_buf, slot_buf, by_slice, prints_buf, grouped, sums, compact, table_buf,
    sems, small_sems, table_sem, prints_sem,
):
    row_count, slice_count, _ = volume.shape
    foot_count = prints.shape[0]
    owners = sent.shape[0]
    crossings = blocks.shape[0]

    half = slice_count // 2
    groups = sems.shape[0]
    group_size = half // groups

    position = lax.axis_index("tile")
    offset = position * row_count
    limit = blocks.shape[1] - 2 * lanes
    base = jnp.minimum((offset // lanes) * lanes, limit)
    small = [
        pltpu.make_async_copy(source, target, small_sems.at[i])
        for i, (source, target) in enumerate(
            [
                (blocks.at[:, pl.ds(pl.multiple_of(base, lanes), 2 * lanes)], window),
                (foots, foots_buf),
                (ray_slot, slot_buf),
                (volume.at[0], first_row),
                (volume.at[row_count - 1], last_row),
            ]
        )
    ]
    for copy in small:
        copy.start()
    for z in range(half):
        for z in (z, z + half):
            pltpu.make_async_copy(
                volume.at[:, z, :], by_slice.at[z], sems.at[z % half // group_size]
            ).start()
    prints_copy = pltpu.make_async_copy(prints, prints_buf, prints_sem)
    prints_copy.start()

    for copy in small[:3]:
        copy.wait()
    mine = pltpu.roll(window[...], 2 * lanes - (offset - base), 1)[:, :lanes]
    slot = jnp.zeros_like(mine)
    for b in range(ray_slot.shape[0]):
        slot = jnp.where(mine == b, slot_buf[b], slot)
    valid = iota((crossings, lanes), 1) < row_count
    owner = jnp.where(valid, slot // owned, -1)
    label = iota((owners, lanes), 0)
    present = jnp.zeros((owners, lanes), F32)
    for k in range(crossings):
        present = jnp.where(owner[k : k + 1] == label, 1.0, present)
    present = jnp.broadcast_to(jnp.max(present, axis=1, keepdims=True), (owners, lanes))
    lower = (iota((owners, owners), 1) < iota((owners, owners), 0)).astype(BF16)
    rank = jnp.dot(lower, present.astype(BF16), preferred_element_type=F32)
    column = iota((owners, lanes), 1)
    rank_row = jnp.sum(jnp.where(label < column, present, 0.0), axis=0, keepdims=True)
    present_row = jnp.sum(jnp.where(label == column, present, 0.0), axis=0, keepdims=True)
    rank_row = jnp.where(present_row > 0.5, rank_row, -1.0).astype(jnp.int32)
    match = jnp.where((rank.astype(jnp.int32) == column) & (present > 0.5), label + 1, 0)
    owner_row = jnp.sum(match, axis=0, keepdims=True) - 1
    table_buf[...] = jnp.where(iota(table_buf.shape, 0) == 0, rank_row, owner_row)
    table_copy = pltpu.make_async_copy(table_buf, table, table_sem)
    table_copy.start()

    foots_here = jnp.concatenate(
        [foots_buf[...], jnp.zeros((crossings, lanes - row_count), jnp.int32)], axis=1
    )
    codes = []
    for k in range(crossings):
        place = jnp.sum(
            jnp.where(owner[k : k + 1] == label, rank, 0.0), axis=0, keepdims=True
        ).astype(jnp.int32)
        codes.append(jnp.where(valid[k : k + 1], foots_here[k : k + 1] * touch + place, -1))
    step = 4
    for f in range(0, foot_count, step):
        code_row = iota((step * touch, lanes), 0) + f * touch
        total = jnp.zeros((step * touch, lanes), F32)
        for code in codes:
            total = total + jnp.where(code_row == code, 1.0, 0.0)
        counts[f * touch : (f + step) * touch] = total.astype(BF16)

    @pl.loop(0, groups)
    def _(i):
        both = by_slice.at[pl.ds(0, 2 * group_size)]
        pltpu.make_async_copy(both, both, sems.at[i]).wait()
        for j in range(group_size):
            z = i * group_size + j
            pair = jnp.concatenate([by_slice[z], by_slice[z + half]], axis=1).astype(BF16)
            for first in range(0, foot_count, step):
                group = jnp.dot(
                    counts[first * touch : (first + step) * touch, :row_count],
                    pair,
                    preferred_element_type=F32,
                ).astype(BF16)
                for f in range(step):
                    grouped[first + f, pl.ds(pl.multiple_of(z * touch, touch), touch), :] = group[
                        f * touch : (f + 1) * touch
                    ]

    head[...] = by_slice[0]
    tail[...] = by_slice[slice_count - 1]
    prints_copy.wait()
    sums[...] = jnp.zeros_like(sums)
    deep = 16
    block = 256
    zero = jnp.zeros(prints.shape[1:], BF16)

    @pl.loop(0, foot_count // deep)
    def _(g):
        weights = []
        for h in range(deep):
            weight = prints_buf[g * deep + h]
            weights.append(jnp.concatenate([weight, zero], axis=1))
            weights.append(jnp.concatenate([zero, weight], axis=1))
        weights = jnp.concatenate(weights, axis=0)
        for m in range(0, half * touch, block):
            left = [grouped[g * deep + h, m : m + block, :] for h in range(deep)]
            both = jnp.dot(
                jnp.concatenate(left, axis=1), weights, preferred_element_type=F32
            )
            rays = both.shape[1] // 2
            sums[m : m + block] += both[:, :rays]
            sums[half * touch + m : half * touch + m + block] += both[:, rays:]

    compact[...] = jnp.swapaxes(sums[...].reshape(slice_count, touch, -1), 0, 1).astype(BF16)
    for copy in small[3:]:
        copy.wait()
    table_copy.wait()
    for t in range(owners):
        place = table[0, t]
        block = compact[jnp.maximum(place, 0)]
        sent[t] = jnp.where(place >= 0, block, jnp.zeros_like(block))


def forward(touch, owned, owners, ray_slot, blocks, foots, volume, prints):
    rows, slices, pixels = volume.shape
    foot_count, _, rays = prints.shape
    return pl.pallas_call(
        functools.partial(forward_kernel, touch, owned),
        out_shape=(
            jax.ShapeDtypeStruct((owners, slices, rays), BF16),
            jax.ShapeDtypeStruct((8, lanes), jnp.int32),
            jax.ShapeDtypeStruct((foot_count * touch, lanes), BF16),
            jax.ShapeDtypeStruct((rows, pixels), F32),
            jax.ShapeDtypeStruct((rows, pixels), F32),
            jax.ShapeDtypeStruct((slices, pixels), F32),
            jax.ShapeDtypeStruct((slices, pixels), F32),
        ),
        in_specs=[HBM] * 5,
        out_specs=(VMEM, SMEM) + (VMEM,) * 5,
        scratch_shapes=[
            pltpu.VMEM((blocks.shape[0], 2 * lanes), jnp.int32),
            pltpu.VMEM(foots.shape, jnp.int32),
            pltpu.SMEM(ray_slot.shape, jnp.int32),
            pltpu.VMEM((slices, rows, pixels), F32),
            pltpu.VMEM(prints.shape, BF16),
            pltpu.VMEM((foot_count, slices // 2 * touch, 2 * pixels), BF16),
            pltpu.VMEM((slices * touch, rays), F32),
            pltpu.VMEM((touch, slices, rays), BF16),
            pltpu.VMEM((8, lanes), jnp.int32),
            pltpu.SemaphoreType.DMA((4,)),
            pltpu.SemaphoreType.DMA((5,)),
            pltpu.SemaphoreType.DMA,
            pltpu.SemaphoreType.DMA,
        ],
        compiler_params=pltpu.CompilerParams(vmem_limit_bytes=24 << 20),
        name="forward",
    )(*in_hbm(ray_slot, blocks, foots, volume, prints))


def tables_kernel(owned, ray_slot, blocks, counts, counts_turned, picks):
    position = lax.axis_index("tile")
    rows = counts_turned.shape[0]

    counts_turned[...] = counts[...].astype(F32).T[:rows].astype(BF16)

    owners = picks.shape[0]
    width = blocks.shape[1]
    second = jnp.int32(0)
    for b in range(ray_slot.shape[0]):
        second = jnp.where(ray_slot[b] == position * owned + 1, b, second)
    hit = jnp.max(jnp.where(blocks[...] == second, 1.0, 0.0), axis=0, keepdims=True)
    start = iota((owners, width), 0) * rows
    at = iota((owners, width), 1)
    member = ((at >= start) & (at < start + rows)).astype(BF16)
    count = lax.dot_general(
        member,
        jnp.broadcast_to(hit, (lanes, width)).astype(BF16),
        (((1,), (1,)), ((), ())),
        preferred_element_type=F32,
    )
    picks[...] = jnp.where(count > 0.5, 1.0, 0.0)


def tables(owned, owners, rows, ray_slot, blocks, counts):
    return pl.pallas_call(
        functools.partial(tables_kernel, owned),
        out_shape=(
            jax.ShapeDtypeStruct((rows, counts.shape[0]), BF16),
            jax.ShapeDtypeStruct((owners, lanes), F32),
        ),
        in_specs=[SMEM] + [VMEM] * 2,
        out_specs=(VMEM,) * 2,
        compiler_params=pltpu.CompilerParams(vmem_limit_bytes=8 << 20),
        name="tables",
    )(ray_slot, blocks, counts)


def variation_kernel(
    volume, before_slice, after_slice, before_row, after_row, first_row,
    base, by_slice, row_flux, sems,
):
    slices, rows, pixels = base.shape

    groups = sems.shape[0]
    size = slices // groups
    for z in range(slices):
        pltpu.make_async_copy(volume.at[:, z, :], by_slice.at[z], sems.at[z // size]).start()

    def wait_group(i):
        span = by_slice.at[pl.ds(i * size, size)]
        pltpu.make_async_copy(span, span, sems.at[i]).wait()

    position = lax.axis_index("tile")
    layer = lax.axis_index("slab")
    last_position = lax.axis_size("tile") - 1
    last_layer = lax.axis_size("slab") - 1
    lane = iota((1, pixels), 1)
    inner = lane < pixels - 1
    first = lane == 0

    def col_grad(x):
        return jnp.where(inner, pltpu.roll(x, pixels - 1, 1) - x, 0.0)

    def scale(a, b, c):
        return lax.rsqrt(a * a + b * b + c * c + smoothing)

    low = before_row[...]
    z_id = iota((slices, 1), 0)
    above = jnp.where(z_id == slices - 1, after_slice[0:1], pltpu.roll(low, slices - 1, 0))
    grad_slices = above - low
    grad_slices = jnp.where((z_id == slices - 1) & (layer == last_layer), 0.0, grad_slices)
    grad_rows = first_row[...] - low
    flux = grad_rows * scale(grad_rows, grad_slices, col_grad(low))
    row_flux[...] = jnp.where(position == 0, 0.0, flux)

    row_id = iota((rows, 1), 0)
    top = row_id == rows - 1
    bottom = row_id == 0
    keep = jnp.where(top & (position == last_position), 0.0, 1.0)

    def fluxes(here, next_slice, beyond, last):
        up = jnp.where(top, beyond, pltpu.roll(here, rows - 1, 0))
        grad_rows = (up - here) * keep
        grad_slices = jnp.where(last, 0.0, next_slice - here)
        grad_cols = col_grad(here)
        inverse = scale(grad_rows, grad_slices, grad_cols)
        return grad_rows * inverse, grad_slices * inverse, grad_cols * inverse

    wait_group(0)
    _, start, _ = fluxes(
        before_slice[1 : rows + 1], by_slice[0], before_slice[rows + 1 : rows + 2], False
    )
    start = jnp.where(layer == 0, 0.0, start)

    def one(z, here, next_slice, previous, last):
        flux_rows, flux_slices, flux_cols = fluxes(
            here, next_slice, after_row[pl.ds(z, 1), :], last
        )
        below = jnp.where(bottom, row_flux[pl.ds(z, 1), :], pltpu.roll(flux_rows, 1, 0))
        left = jnp.where(first, 0.0, pltpu.roll(flux_cols, 1, 1))
        variation = (previous - flux_slices) + (below - flux_rows) + (left - flux_cols)
        base[z] = here - (step_length * variation_weight) * variation
        return flux_slices

    def step(z, previous):
        @pl.when((z + 1) % size == 0)
        def _():
            wait_group((z + 1) // size)

        return one(z, by_slice[z], by_slice[z + 1], previous, False)

    final = lax.fori_loop(0, slices - 1, step, start)
    one(slices - 1, by_slice[slices - 1], after_slice[1 : rows + 1], final, layer == last_layer)


def variation(volume, *halos):
    rows, slices, pixels = volume.shape
    return pl.pallas_call(
        variation_kernel,
        out_shape=jax.ShapeDtypeStruct((slices, rows, pixels), F32),
        in_specs=[HBM] + [VMEM] * 5,
        out_specs=VMEM,
        scratch_shapes=[
            pltpu.VMEM((slices, rows, pixels), F32),
            pltpu.VMEM((slices, pixels), F32),
            pltpu.SemaphoreType.DMA((8,)),
        ],
        compiler_params=pltpu.CompilerParams(vmem_limit_bytes=8 << 20),
        name="variation",
    )(*in_hbm(volume), *halos)


def residual_kernel(arrived, picks, measured, weights, returned):
    owners = arrived.shape[0]
    sums = [jnp.zeros(measured.shape[1:], F32) for _ in range(2)]
    for j in range(owners):
        part = arrived[j].astype(F32)
        chosen = picks[j : j + 1, :] > 0.5
        sums[0] = sums[0] + jnp.where(chosen, 0.0, part)
        sums[1] = sums[1] + jnp.where(chosen, part, 0.0)
    out = [(weights[i] * (sums[i] - measured[i])).astype(BF16).astype(F32) for i in range(2)]
    for j in range(owners):
        returned[j] = jnp.where(picks[j : j + 1, :] > 0.5, out[1], out[0]).astype(BF16)


def residual(arrived, picks, measured, weights):
    return pl.pallas_call(
        residual_kernel,
        out_shape=jax.ShapeDtypeStruct(arrived.shape, BF16),
        in_specs=[VMEM] * 4,
        out_specs=VMEM,
        compiler_params=pltpu.CompilerParams(vmem_limit_bytes=4 << 20),
        name="residual",
    )(arrived, picks, measured, weights)


def backward_kernel(
    touch, table, returned, prints, counts_turned, base,
    out, gathered, mixed, spread, out_buf, prints_buf, sems, prints_sems,
):
    slices, _, pixels = base.shape
    foot_count, _, rays = prints.shape
    parts = prints_sems.shape[0]
    per_part = foot_count // parts

    def prints_copy(g):
        span = pl.ds(g * per_part, per_part)
        return pltpu.make_async_copy(prints.at[span], prints_buf.at[span], prints_sems.at[g])

    for g in range(parts):
        prints_copy(g).start()
    for s in range(touch):
        owner = table[1, s]
        block = returned[jnp.maximum(owner, 0)].astype(F32)
        gathered[s] = jnp.where(owner >= 0, block, 0.0)
    mixed[...] = jnp.swapaxes(gathered[...], 0, 1).reshape(slices * touch, rays).astype(BF16)
    half = slices // 2
    block = 256
    zero = jnp.zeros(prints.shape[1:], BF16)

    @pl.loop(0, parts)
    def _(g):
        prints_copy(g).wait()
        for f in range(per_part):
            weight = prints_buf[per_part * g + f]
            weights = jnp.concatenate(
                [
                    jnp.concatenate([weight, zero], axis=1),
                    jnp.concatenate([zero, weight], axis=1),
                ],
                axis=0,
            )
            for m in range(0, half * touch, block):
                left = jnp.concatenate(
                    [mixed[m : m + block], mixed[half * touch + m : half * touch + m + block]], axis=1
                )
                value = lax.dot_general(
                    left, weights, (((1,), (1,)), ((), ())), preferred_element_type=F32
                ).astype(BF16)
                for i in range(block // touch):
                    row = pl.multiple_of((per_part * g + f) * touch, touch)
                    spread[m // touch + i, pl.ds(row, touch), :] = value[
                        i * touch : (i + 1) * touch
                    ]

    groups = sems.shape[0]
    group_size = half // groups

    @pl.loop(0, groups)
    def _(i):
        for j in range(group_size):
            z = i * group_size + j
            grad = jnp.dot(counts_turned[...], spread[z], preferred_element_type=F32)
            for g in range(2):
                at = z + g * half
                out_buf[at] = jnp.maximum(
                    base[at] - step_length * grad[:, g * pixels : (g + 1) * pixels], 0.0
                )
        for j in range(group_size):
            for g in range(2):
                at = i * group_size + j + g * half
                pltpu.make_async_copy(out_buf.at[at], out.at[:, at, :], sems.at[i]).start()

    for i in range(groups):
        both = out_buf.at[pl.ds(0, 2 * group_size)]
        pltpu.make_async_copy(both, both, sems.at[i]).wait()


def backward(touch, table, returned, prints, counts_turned, base):
    slices, rows, pixels = base.shape
    codes = prints.shape[0] * touch
    return pl.pallas_call(
        functools.partial(backward_kernel, touch),
        out_shape=jax.ShapeDtypeStruct((rows, slices, pixels), F32),
        in_specs=[SMEM, VMEM, HBM, VMEM, VMEM],
        out_specs=HBM,
        scratch_shapes=[
            pltpu.VMEM((touch, slices, prints.shape[2]), F32),
            pltpu.VMEM((slices * touch, prints.shape[2]), BF16),
            pltpu.VMEM((slices // 2, codes, 2 * pixels), BF16),
            pltpu.VMEM((slices, rows, pixels), F32),
            pltpu.VMEM(prints.shape, BF16),
            pltpu.SemaphoreType.DMA((4,)),
            pltpu.SemaphoreType.DMA((4,)),
        ],
        compiler_params=pltpu.CompilerParams(vmem_limit_bytes=24 << 20),
        name="backward",
    )(table, returned, *in_hbm(prints), counts_turned, base)


def shifted(x, axis, forward_way):
    count = lax.axis_size(axis)
    if forward_way:
        pairs = [(i, i + 1) for i in range(count - 1)]
    else:
        pairs = [(i + 1, i) for i in range(count - 1)]
    return lax.ppermute(x, axis, pairs)


def per_device(volume, footprints, foot_index, ray_block, ray_slot, measured, weights):
    row_count, slice_count, _ = volume.shape
    owners = lax.axis_size("tile")
    owned = measured.shape[0]
    touch = owners // 2
    blocks = ray_block.T
    sent, table, counts, head, tail, first_row, last_row = forward(
        touch, owned, owners, ray_slot, blocks, foot_index.T, volume, footprints
    )
    arrived = lax.all_to_all(sent, "tile", split_axis=0, concat_axis=0, tiled=True)
    before_row = shifted(last_row, "tile", True)
    after_row = shifted(first_row, "tile", False)
    counts_turned, picks = tables(owned, owners, row_count, ray_slot, blocks, counts)

    def edge(z, x):
        return jnp.concatenate([before_row[z : z + 1], x, after_row[z : z + 1]], axis=0)

    edges = (edge(slice_count - 1, tail), edge(0, head))
    before_slice = shifted(edges[0], "slab", True)
    after_slice = shifted(edges[1], "slab", False)
    arrived, _ = lax.optimization_barrier((arrived, edges))
    answer = residual(arrived, picks, measured, weights)
    returned = lax.all_to_all(answer, "tile", split_axis=0, concat_axis=0, tiled=True)
    halos, _ = lax.optimization_barrier(
        ((before_slice, after_slice, before_row, after_row, first_row), answer)
    )
    base = variation(volume, *halos)
    return backward(touch, table, returned, footprints, counts_turned, base)


def solution(mesh):
    in_specs = (
        P("tile", "slab", None),
        P(),
        P("tile", None),
        P(),
        P(),
        P("tile", "slab", None),
        P("tile", "slab", None),
    )
    out_specs = P("tile", "slab", None)
    return jax.shard_map(
        per_device, mesh=mesh, in_specs=in_specs, out_specs=out_specs, check_vma=False
    )
```

```python
import functools

import jax
import jax.numpy as jnp
from jax import lax
from jax.experimental import pallas as pl
from jax.experimental.pallas import tpu as pltpu
from jax.sharding import PartitionSpec as P


smoothing = 0.04
step_length = 2.0
variation_weight = 1.0
lanes = 128

F32 = jnp.float32
BF16 = jnp.bfloat16
VMEM = pl.BlockSpec(memory_space=pltpu.VMEM)
SMEM = pl.BlockSpec(memory_space=pltpu.SMEM)
HBM = pl.BlockSpec(memory_space=pltpu.HBM)


def in_hbm(*arrays):
    return [pltpu.with_memory_space_constraint(x, pltpu.HBM) for x in arrays]


def iota(shape, dim):
    return lax.broadcasted_iota(jnp.int32, shape, dim)


def forward_kernel(
    touch, owned, ray_slot, blocks, foots, volume, prints,
    sent, table, counts, head, tail, first_row, last_row,
    window, foots_buf, slot_buf, by_slice, prints_buf, grouped, sums, compact, table_buf,
    sems, small_sems, table_sem, prints_sem,
):
    row_count, slice_count, _ = volume.shape
    foot_count = prints.shape[0]
    owners = sent.shape[0]
    crossings = blocks.shape[0]

    half = slice_count // 2
    groups = sems.shape[0]
    group_size = half // groups

    position = lax.axis_index("tile")
    offset = position * row_count
    limit = blocks.shape[1] - 2 * lanes
    base = jnp.minimum((offset // lanes) * lanes, limit)
    small = [
        pltpu.make_async_copy(source, target, small_sems.at[i])
        for i, (source, target) in enumerate(
            [
                (blocks.at[:, pl.ds(pl.multiple_of(base, lanes), 2 * lanes)], window),
                (foots, foots_buf),
                (ray_slot, slot_buf),
                (volume.at[0], first_row),
                (volume.at[row_count - 1], last_row),
            ]
        )
    ]
    for copy in small:
        copy.start()
    for z in range(half):
        for z in (z, z + half):
            pltpu.make_async_copy(
                volume.at[:, z, :], by_slice.at[z], sems.at[z % half // group_size]
            ).start()
    prints_copy = pltpu.make_async_copy(prints, prints_buf, prints_sem)
    prints_copy.start()

    for copy in small[:3]:
        copy.wait()
    mine = pltpu.roll(window[...], 2 * lanes - (offset - base), 1)[:, :lanes]
    slot = jnp.zeros_like(mine)
    for b in range(ray_slot.shape[0]):
        slot = jnp.where(mine == b, slot_buf[b], slot)
    valid = iota((crossings, lanes), 1) < row_count
    owner = jnp.where(valid, slot // owned, -1)
    label = iota((owners, lanes), 0)
    present = jnp.zeros((owners, lanes), F32)
    for k in range(crossings):
        present = jnp.where(owner[k : k + 1] == label, 1.0, present)
    present = jnp.broadcast_to(jnp.max(present, axis=1, keepdims=True), (owners, lanes))
    lower = (iota((owners, owners), 1) < iota((owners, owners), 0)).astype(BF16)
    rank = jnp.dot(lower, present.astype(BF16), preferred_element_type=F32)
    column = iota((owners, lanes), 1)
    rank_row = jnp.sum(jnp.where(label < column, present, 0.0), axis=0, keepdims=True)
    present_row = jnp.sum(jnp.where(label == column, present, 0.0), axis=0, keepdims=True)
    rank_row = jnp.where(present_row > 0.5, rank_row, -1.0).astype(jnp.int32)
    match = jnp.where((rank.astype(jnp.int32) == column) & (present > 0.5), label + 1, 0)
    owner_row = jnp.sum(match, axis=0, keepdims=True) - 1
    table_buf[...] = jnp.where(iota(table_buf.shape, 0) == 0, rank_row, owner_row)
    table_copy = pltpu.make_async_copy(table_buf, table, table_sem)
    table_copy.start()

    foots_here = jnp.concatenate(
        [foots_buf[...], jnp.zeros((crossings, lanes - row_count), jnp.int32)], axis=1
    )
    step = 4
    hits, feet = [], []
    rank_id = iota((touch, lanes), 0)
    for k in range(crossings):
        place = jnp.sum(
            jnp.where(owner[k : k + 1] == label, rank, 0.0), axis=0, keepdims=True
        ).astype(jnp.int32)
        hits.append(jnp.where((rank_id == place) & valid[k : k + 1], 1.0, 0.0).astype(BF16))
        feet.append(
            jnp.broadcast_to(foots_here[k : k + 1].astype(F32), (touch, lanes)).astype(BF16)
        )
    none = jnp.zeros((touch, lanes), BF16)
    for f in range(foot_count):
        terms = [jnp.where(foot == f, hit, none) for foot, hit in zip(feet, hits)]
        while len(terms) > 1:
            terms = [x + y for x, y in zip(terms[::2], terms[1::2])]
        counts[f * touch : (f + 1) * touch] = terms[0]

    @pl.loop(0, groups)
    def _(i):
        both = by_slice.at[pl.ds(0, 2 * group_size)]
        pltpu.make_async_copy(both, both, sems.at[i]).wait()
        for j in range(group_size):
            z = i * group_size + j
            pair = jnp.concatenate([by_slice[z], by_slice[z + half]], axis=1).astype(BF16)
            for first in range(0, foot_count, step):
                group = jnp.dot(
                    counts[first * touch : (first + step) * touch, :row_count],
                    pair,
                    preferred_element_type=F32,
                ).astype(BF16)
                for f in range(step):
                    grouped[first + f, pl.ds(pl.multiple_of(z * touch, touch), touch), :] = group[
                        f * touch : (f + 1) * touch
                    ]

    head[...] = by_slice[0]
    tail[...] = by_slice[slice_count - 1]
    prints_copy.wait()
    sums[...] = jnp.zeros_like(sums)
    deep = 16
    block = 256
    zero = jnp.zeros(prints.shape[1:], BF16)

    @pl.loop(0, foot_count // deep)
    def _(g):
        weights = []
        for h in range(deep):
            weight = prints_buf[g * deep + h]
            weights.append(jnp.concatenate([weight, zero], axis=1))
            weights.append(jnp.concatenate([zero, weight], axis=1))
        weights = jnp.concatenate(weights, axis=0)
        for m in range(0, half * touch, block):
            left = [grouped[g * deep + h, m : m + block, :] for h in range(deep)]
            both = jnp.dot(
                jnp.concatenate(left, axis=1), weights, preferred_element_type=F32
            )
            rays = both.shape[1] // 2
            sums[m : m + block] += both[:, :rays]
            sums[half * touch + m : half * touch + m + block] += both[:, rays:]

    compact[...] = jnp.swapaxes(sums[...].reshape(slice_count, touch, -1), 0, 1).astype(BF16)
    for copy in small[3:]:
        copy.wait()
    table_copy.wait()
    for t in range(owners):
        place = table[0, t]
        block = compact[jnp.maximum(place, 0)]
        sent[t] = jnp.where(place >= 0, block, jnp.zeros_like(block))


def forward(touch, owned, owners, ray_slot, blocks, foots, volume, prints):
    rows, slices, pixels = volume.shape
    foot_count, _, rays = prints.shape
    return pl.pallas_call(
        functools.partial(forward_kernel, touch, owned),
        out_shape=(
            jax.ShapeDtypeStruct((owners, slices, rays), BF16),
            jax.ShapeDtypeStruct((8, lanes), jnp.int32),
            jax.ShapeDtypeStruct((foot_count * touch, lanes), BF16),
            jax.ShapeDtypeStruct((rows, pixels), F32),
            jax.ShapeDtypeStruct((rows, pixels), F32),
            jax.ShapeDtypeStruct((slices, pixels), F32),
            jax.ShapeDtypeStruct((slices, pixels), F32),
        ),
        in_specs=[HBM] * 5,
        out_specs=(VMEM, SMEM) + (VMEM,) * 5,
        scratch_shapes=[
            pltpu.VMEM((blocks.shape[0], 2 * lanes), jnp.int32),
            pltpu.VMEM(foots.shape, jnp.int32),
            pltpu.SMEM(ray_slot.shape, jnp.int32),
            pltpu.VMEM((slices, rows, pixels), F32),
            pltpu.VMEM(prints.shape, BF16),
            pltpu.VMEM((foot_count, slices // 2 * touch, 2 * pixels), BF16),
            pltpu.VMEM((slices * touch, rays), F32),
            pltpu.VMEM((touch, slices, rays), BF16),
            pltpu.VMEM((8, lanes), jnp.int32),
            pltpu.SemaphoreType.DMA((4,)),
            pltpu.SemaphoreType.DMA((5,)),
            pltpu.SemaphoreType.DMA,
            pltpu.SemaphoreType.DMA,
        ],
        compiler_params=pltpu.CompilerParams(vmem_limit_bytes=24 << 20),
        name="forward",
    )(*in_hbm(ray_slot, blocks, foots, volume, prints))


def tables_kernel(owned, ray_slot, blocks, counts, counts_turned, picks):
    position = lax.axis_index("tile")
    rows = counts_turned.shape[0]

    counts_turned[...] = counts[...].astype(F32).T[:rows].astype(BF16)

    owners = picks.shape[0]
    width = blocks.shape[1]
    second = jnp.int32(0)
    for b in range(ray_slot.shape[0]):
        second = jnp.where(ray_slot[b] == position * owned + 1, b, second)
    hit = jnp.max(jnp.where(blocks[...] == second, 1.0, 0.0), axis=0, keepdims=True)
    start = iota((owners, width), 0) * rows
    at = iota((owners, width), 1)
    member = ((at >= start) & (at < start + rows)).astype(BF16)
    count = lax.dot_general(
        member,
        jnp.broadcast_to(hit, (lanes, width)).astype(BF16),
        (((1,), (1,)), ((), ())),
        preferred_element_type=F32,
    )
    picks[...] = jnp.where(count > 0.5, 1.0, 0.0)


def tables(owned, owners, rows, ray_slot, blocks, counts):
    return pl.pallas_call(
        functools.partial(tables_kernel, owned),
        out_shape=(
            jax.ShapeDtypeStruct((rows, counts.shape[0]), BF16),
            jax.ShapeDtypeStruct((owners, lanes), F32),
        ),
        in_specs=[SMEM] + [VMEM] * 2,
        out_specs=(VMEM,) * 2,
        compiler_params=pltpu.CompilerParams(vmem_limit_bytes=8 << 20),
        name="tables",
    )(ray_slot, blocks, counts)


def variation_kernel(
    volume, before_slice, after_slice, before_row, after_row, first_row,
    base, by_slice, row_flux, sems,
):
    slices, rows, pixels = base.shape

    groups = sems.shape[0]
    size = slices // groups
    for z in range(slices):
        pltpu.make_async_copy(volume.at[:, z, :], by_slice.at[z], sems.at[z // size]).start()

    def wait_group(i):
        span = by_slice.at[pl.ds(i * size, size)]
        pltpu.make_async_copy(span, span, sems.at[i]).wait()

    position = lax.axis_index("tile")
    layer = lax.axis_index("slab")
    last_position = lax.axis_size("tile") - 1
    last_layer = lax.axis_size("slab") - 1
    lane = iota((1, pixels), 1)
    inner = lane < pixels - 1
    first = lane == 0

    def col_grad(x):
        return jnp.where(inner, pltpu.roll(x, pixels - 1, 1) - x, 0.0)

    def scale(a, b, c):
        return lax.rsqrt(a * a + b * b + c * c + smoothing)

    low = before_row[...]
    z_id = iota((slices, 1), 0)
    above = jnp.where(z_id == slices - 1, after_slice[0:1], pltpu.roll(low, slices - 1, 0))
    grad_slices = above - low
    grad_slices = jnp.where((z_id == slices - 1) & (layer == last_layer), 0.0, grad_slices)
    grad_rows = first_row[...] - low
    flux = grad_rows * scale(grad_rows, grad_slices, col_grad(low))
    row_flux[...] = jnp.where(position == 0, 0.0, flux)

    row_id = iota((rows, 1), 0)
    top = row_id == rows - 1
    bottom = row_id == 0
    keep = jnp.where(top & (position == last_position), 0.0, 1.0)

    def fluxes(here, next_slice, beyond, last):
        up = jnp.where(top, beyond, pltpu.roll(here, rows - 1, 0))
        grad_rows = (up - here) * keep
        grad_slices = jnp.where(last, 0.0, next_slice - here)
        grad_cols = col_grad(here)
        inverse = scale(grad_rows, grad_slices, grad_cols)
        return grad_rows * inverse, grad_slices * inverse, grad_cols * inverse

    wait_group(0)
    _, start, _ = fluxes(
        before_slice[1 : rows + 1], by_slice[0], before_slice[rows + 1 : rows + 2], False
    )
    start = jnp.where(layer == 0, 0.0, start)

    def one(z, here, next_slice, previous, last):
        flux_rows, flux_slices, flux_cols = fluxes(
            here, next_slice, after_row[pl.ds(z, 1), :], last
        )
        below = jnp.where(bottom, row_flux[pl.ds(z, 1), :], pltpu.roll(flux_rows, 1, 0))
        left = jnp.where(first, 0.0, pltpu.roll(flux_cols, 1, 1))
        variation = (previous - flux_slices) + (below - flux_rows) + (left - flux_cols)
        base[z] = here - (step_length * variation_weight) * variation
        return flux_slices

    def step(z, previous):
        @pl.when((z + 1) % size == 0)
        def _():
            wait_group((z + 1) // size)

        return one(z, by_slice[z], by_slice[z + 1], previous, False)

    final = lax.fori_loop(0, slices - 1, step, start)
    one(slices - 1, by_slice[slices - 1], after_slice[1 : rows + 1], final, layer == last_layer)


def variation(volume, *halos):
    rows, slices, pixels = volume.shape
    return pl.pallas_call(
        variation_kernel,
        out_shape=jax.ShapeDtypeStruct((slices, rows, pixels), F32),
        in_specs=[HBM] + [VMEM] * 5,
        out_specs=VMEM,
        scratch_shapes=[
            pltpu.VMEM((slices, rows, pixels), F32),
            pltpu.VMEM((slices, pixels), F32),
            pltpu.SemaphoreType.DMA((8,)),
        ],
        compiler_params=pltpu.CompilerParams(vmem_limit_bytes=8 << 20),
        name="variation",
    )(*in_hbm(volume), *halos)


def residual_kernel(arrived, picks, measured, weights, returned):
    owners = arrived.shape[0]
    sums = [jnp.zeros(measured.shape[1:], F32) for _ in range(2)]
    for j in range(owners):
        part = arrived[j].astype(F32)
        chosen = picks[j : j + 1, :] > 0.5
        sums[0] = sums[0] + jnp.where(chosen, 0.0, part)
        sums[1] = sums[1] + jnp.where(chosen, part, 0.0)
    out = [(weights[i] * (sums[i] - measured[i])).astype(BF16).astype(F32) for i in range(2)]
    for j in range(owners):
        returned[j] = jnp.where(picks[j : j + 1, :] > 0.5, out[1], out[0]).astype(BF16)


def residual(arrived, picks, measured, weights):
    return pl.pallas_call(
        residual_kernel,
        out_shape=jax.ShapeDtypeStruct(arrived.shape, BF16),
        in_specs=[VMEM] * 4,
        out_specs=VMEM,
        compiler_params=pltpu.CompilerParams(vmem_limit_bytes=4 << 20),
        name="residual",
    )(arrived, picks, measured, weights)


def backward_kernel(
    touch, table, returned, prints, counts_turned, base,
    out, gathered, mixed, spread, out_buf, prints_buf, sems, prints_sems,
):
    slices, _, pixels = base.shape
    foot_count, _, rays = prints.shape
    parts = prints_sems.shape[0]
    per_part = foot_count // parts

    def prints_copy(g):
        span = pl.ds(g * per_part, per_part)
        return pltpu.make_async_copy(prints.at[span], prints_buf.at[span], prints_sems.at[g])

    for g in range(parts):
        prints_copy(g).start()
    for s in range(touch):
        owner = table[1, s]
        block = returned[jnp.maximum(owner, 0)].astype(F32)
        gathered[s] = jnp.where(owner >= 0, block, 0.0)
    mixed[...] = jnp.swapaxes(gathered[...], 0, 1).reshape(slices * touch, rays).astype(BF16)
    half = slices // 2
    block = 256
    zero = jnp.zeros(prints.shape[1:], BF16)

    @pl.loop(0, parts)
    def _(g):
        prints_copy(g).wait()
        for f in range(per_part):
            weight = prints_buf[per_part * g + f]
            weights = jnp.concatenate(
                [
                    jnp.concatenate([weight, zero], axis=1),
                    jnp.concatenate([zero, weight], axis=1),
                ],
                axis=0,
            )
            for m in range(0, half * touch, block):
                left = jnp.concatenate(
                    [mixed[m : m + block], mixed[half * touch + m : half * touch + m + block]], axis=1
                )
                value = lax.dot_general(
                    left, weights, (((1,), (1,)), ((), ())), preferred_element_type=F32
                ).astype(BF16)
                for i in range(block // touch):
                    row = pl.multiple_of((per_part * g + f) * touch, touch)
                    spread[m // touch + i, pl.ds(row, touch), :] = value[
                        i * touch : (i + 1) * touch
                    ]

    groups = sems.shape[0]
    group_size = half // groups

    @pl.loop(0, groups)
    def _(i):
        for j in range(group_size):
            z = i * group_size + j
            grad = jnp.dot(counts_turned[...], spread[z], preferred_element_type=F32)
            for g in range(2):
                at = z + g * half
                out_buf[at] = jnp.maximum(
                    base[at] - step_length * grad[:, g * pixels : (g + 1) * pixels], 0.0
                )
        for j in range(group_size):
            for g in range(2):
                at = i * group_size + j + g * half
                pltpu.make_async_copy(out_buf.at[at], out.at[:, at, :], sems.at[i]).start()

    for i in range(groups):
        both = out_buf.at[pl.ds(0, 2 * group_size)]
        pltpu.make_async_copy(both, both, sems.at[i]).wait()


def backward(touch, table, returned, prints, counts_turned, base):
    slices, rows, pixels = base.shape
    codes = prints.shape[0] * touch
    return pl.pallas_call(
        functools.partial(backward_kernel, touch),
        out_shape=jax.ShapeDtypeStruct((rows, slices, pixels), F32),
        in_specs=[SMEM, VMEM, HBM, VMEM, VMEM],
        out_specs=HBM,
        scratch_shapes=[
            pltpu.VMEM((touch, slices, prints.shape[2]), F32),
            pltpu.VMEM((slices * touch, prints.shape[2]), BF16),
            pltpu.VMEM((slices // 2, codes, 2 * pixels), BF16),
            pltpu.VMEM((slices, rows, pixels), F32),
            pltpu.VMEM(prints.shape, BF16),
            pltpu.SemaphoreType.DMA((4,)),
            pltpu.SemaphoreType.DMA((4,)),
        ],
        compiler_params=pltpu.CompilerParams(vmem_limit_bytes=24 << 20),
        name="backward",
    )(table, returned, *in_hbm(prints), counts_turned, base)


def shifted(x, axis, forward_way):
    count = lax.axis_size(axis)
    if forward_way:
        pairs = [(i, i + 1) for i in range(count - 1)]
    else:
        pairs = [(i + 1, i) for i in range(count - 1)]
    return lax.ppermute(x, axis, pairs)


def per_device(volume, footprints, foot_index, ray_block, ray_slot, measured, weights):
    row_count, slice_count, _ = volume.shape
    owners = lax.axis_size("tile")
    owned = measured.shape[0]
    touch = owners // 2
    blocks = ray_block.T
    sent, table, counts, head, tail, first_row, last_row = forward(
        touch, owned, owners, ray_slot, blocks, foot_index.T, volume, footprints
    )
    arrived = lax.all_to_all(sent, "tile", split_axis=0, concat_axis=0, tiled=True)
    before_row = shifted(last_row, "tile", True)
    after_row = shifted(first_row, "tile", False)
    counts_turned, picks = tables(owned, owners, row_count, ray_slot, blocks, counts)

    def edge(z, x):
        return jnp.concatenate([before_row[z : z + 1], x, after_row[z : z + 1]], axis=0)

    edges = (edge(slice_count - 1, tail), edge(0, head))
    before_slice = shifted(edges[0], "slab", True)
    after_slice = shifted(edges[1], "slab", False)
    arrived, _ = lax.optimization_barrier((arrived, edges))
    answer = residual(arrived, picks, measured, weights)
    returned = lax.all_to_all(answer, "tile", split_axis=0, concat_axis=0, tiled=True)
    halos, _ = lax.optimization_barrier(
        ((before_slice, after_slice, before_row, after_row, first_row), answer)
    )
    base = variation(volume, *halos)
    return backward(touch, table, returned, footprints, counts_turned, base)


def solution(mesh):
    in_specs = (
        P("tile", "slab", None),
        P(),
        P("tile", None),
        P(),
        P(),
        P("tile", "slab", None),
        P("tile", "slab", None),
    )
    out_specs = P("tile", "slab", None)
    return jax.shard_map(
        per_device, mesh=mesh, in_specs=in_specs, out_specs=out_specs, check_vma=False
    )
```

```python
import functools

import jax
import jax.numpy as jnp
from jax import lax
from jax.experimental import pallas as pl
from jax.experimental.pallas import tpu as pltpu
from jax.sharding import PartitionSpec as P


smoothing = 0.04
step_length = 2.0
variation_weight = 1.0
lanes = 128

F32 = jnp.float32
BF16 = jnp.bfloat16
VMEM = pl.BlockSpec(memory_space=pltpu.VMEM)
SMEM = pl.BlockSpec(memory_space=pltpu.SMEM)
HBM = pl.BlockSpec(memory_space=pltpu.HBM)


def in_hbm(*arrays):
    return [pltpu.with_memory_space_constraint(x, pltpu.HBM) for x in arrays]


def iota(shape, dim):
    return lax.broadcasted_iota(jnp.int32, shape, dim)


def forward_kernel(
    touch, owned, ray_slot, blocks, foots, volume, prints,
    sent, table, counts, head, tail, first_row, last_row,
    window, foots_buf, slot_buf, by_slice, prints_buf, grouped, sums, compact, table_buf,
    sems, small_sems, table_sem, prints_sem,
):
    row_count, slice_count, _ = volume.shape
    foot_count = prints.shape[0]
    owners = sent.shape[0]
    crossings = blocks.shape[0]

    half = slice_count // 2
    groups = sems.shape[0]
    group_size = half // groups

    position = lax.axis_index("tile")
    offset = position * row_count
    limit = blocks.shape[1] - 2 * lanes
    base = jnp.minimum((offset // lanes) * lanes, limit)
    small = [
        pltpu.make_async_copy(source, target, small_sems.at[i])
        for i, (source, target) in enumerate(
            [
                (blocks.at[:, pl.ds(pl.multiple_of(base, lanes), 2 * lanes)], window),
                (foots, foots_buf),
                (ray_slot, slot_buf),
                (volume.at[0], first_row),
                (volume.at[row_count - 1], last_row),
            ]
        )
    ]
    for copy in small:
        copy.start()
    for z in range(half):
        for z in (z, z + half):
            pltpu.make_async_copy(
                volume.at[:, z, :], by_slice.at[z], sems.at[z % half // group_size]
            ).start()
    prints_copy = pltpu.make_async_copy(prints, prints_buf, prints_sem)
    prints_copy.start()

    for copy in small[:3]:
        copy.wait()
    mine = pltpu.roll(window[...], 2 * lanes - (offset - base), 1)[:, :lanes]
    slot = jnp.zeros_like(mine)
    for b in range(ray_slot.shape[0]):
        slot = jnp.where(mine == b, slot_buf[b], slot)
    valid = iota((crossings, lanes), 1) < row_count
    owner = jnp.where(valid, slot // owned, -1)
    label = iota((owners, lanes), 0)
    present = jnp.zeros((owners, lanes), F32)
    for k in range(crossings):
        present = jnp.where(owner[k : k + 1] == label, 1.0, present)
    present = jnp.broadcast_to(jnp.max(present, axis=1, keepdims=True), (owners, lanes))
    lower = (iota((owners, owners), 1) < iota((owners, owners), 0)).astype(BF16)
    rank = jnp.dot(lower, present.astype(BF16), preferred_element_type=F32)
    column = iota((owners, lanes), 1)
    rank_row = jnp.sum(jnp.where(label < column, present, 0.0), axis=0, keepdims=True)
    present_row = jnp.sum(jnp.where(label == column, present, 0.0), axis=0, keepdims=True)
    rank_row = jnp.where(present_row > 0.5, rank_row, -1.0).astype(jnp.int32)
    match = jnp.where((rank.astype(jnp.int32) == column) & (present > 0.5), label + 1, 0)
    owner_row = jnp.sum(match, axis=0, keepdims=True) - 1
    table_buf[...] = jnp.where(iota(table_buf.shape, 0) == 0, rank_row, owner_row)
    table_copy = pltpu.make_async_copy(table_buf, table, table_sem)
    table_copy.start()

    foots_here = jnp.concatenate(
        [foots_buf[...], jnp.zeros((crossings, lanes - row_count), jnp.int32)], axis=1
    )
    step = 4
    hits, feet = [], []
    rank_id = iota((touch, lanes), 0)
    for k in range(crossings):
        place = jnp.sum(
            jnp.where(owner[k : k + 1] == label, rank, 0.0), axis=0, keepdims=True
        ).astype(jnp.int32)
        hits.append(jnp.where((rank_id == place) & valid[k : k + 1], 1.0, 0.0).astype(BF16))
        feet.append(
            jnp.broadcast_to(foots_here[k : k + 1].astype(F32), (touch, lanes)).astype(BF16)
        )
    none = jnp.zeros((touch, lanes), BF16)
    for f in range(foot_count):
        terms = [jnp.where(foot == f, hit, none) for foot, hit in zip(feet, hits)]
        while len(terms) > 1:
            terms = [x + y for x, y in zip(terms[::2], terms[1::2])]
        counts[f * touch : (f + 1) * touch] = terms[0]

    @pl.loop(0, groups)
    def _(i):
        both = by_slice.at[pl.ds(0, 2 * group_size)]
        pltpu.make_async_copy(both, both, sems.at[i]).wait()
        for j in range(group_size):
            z = i * group_size + j
            pair = jnp.concatenate([by_slice[z], by_slice[z + half]], axis=1).astype(BF16)
            for first in range(0, foot_count, step):
                group = jnp.dot(
                    counts[first * touch : (first + step) * touch, :row_count],
                    pair,
                    preferred_element_type=F32,
                ).astype(BF16)
                for f in range(step):
                    grouped[first + f, pl.ds(pl.multiple_of(z * touch, touch), touch), :] = group[
                        f * touch : (f + 1) * touch
                    ]

    head[...] = by_slice[0]
    tail[...] = by_slice[slice_count - 1]
    prints_copy.wait()
    sums[...] = jnp.zeros_like(sums)
    deep = 16
    block = 256
    zero = jnp.zeros(prints.shape[1:], BF16)

    @pl.loop(0, foot_count // deep)
    def _(g):
        weights = []
        for h in range(deep):
            weight = prints_buf[g * deep + h]
            weights.append(jnp.concatenate([weight, zero], axis=1))
            weights.append(jnp.concatenate([zero, weight], axis=1))
        weights = jnp.concatenate(weights, axis=0)
        for m in range(0, half * touch, block):
            left = [grouped[g * deep + h, m : m + block, :] for h in range(deep)]
            both = jnp.dot(
                jnp.concatenate(left, axis=1), weights, preferred_element_type=F32
            )
            rays = both.shape[1] // 2
            sums[m : m + block] += both[:, :rays]
            sums[half * touch + m : half * touch + m + block] += both[:, rays:]

    compact[...] = jnp.swapaxes(sums[...].reshape(slice_count, touch, -1), 0, 1).astype(BF16)
    for copy in small[3:]:
        copy.wait()
    table_copy.wait()
    for t in range(owners):
        place = table[0, t]
        block = compact[jnp.maximum(place, 0)]
        sent[t] = jnp.where(place >= 0, block, jnp.zeros_like(block))


def forward(touch, owned, owners, ray_slot, blocks, foots, volume, prints):
    rows, slices, pixels = volume.shape
    foot_count, _, rays = prints.shape
    return pl.pallas_call(
        functools.partial(forward_kernel, touch, owned),
        out_shape=(
            jax.ShapeDtypeStruct((owners, slices, rays), BF16),
            jax.ShapeDtypeStruct((8, lanes), jnp.int32),
            jax.ShapeDtypeStruct((foot_count * touch, lanes), BF16),
            jax.ShapeDtypeStruct((rows, pixels), F32),
            jax.ShapeDtypeStruct((rows, pixels), F32),
            jax.ShapeDtypeStruct((slices, pixels), F32),
            jax.ShapeDtypeStruct((slices, pixels), F32),
        ),
        in_specs=[HBM] * 5,
        out_specs=(VMEM, SMEM) + (VMEM,) * 5,
        scratch_shapes=[
            pltpu.VMEM((blocks.shape[0], 2 * lanes), jnp.int32),
            pltpu.VMEM(foots.shape, jnp.int32),
            pltpu.SMEM(ray_slot.shape, jnp.int32),
            pltpu.VMEM((slices, rows, pixels), F32),
            pltpu.VMEM(prints.shape, BF16),
            pltpu.VMEM((foot_count, slices // 2 * touch, 2 * pixels), BF16),
            pltpu.VMEM((slices * touch, rays), F32),
            pltpu.VMEM((touch, slices, rays), BF16),
            pltpu.VMEM((8, lanes), jnp.int32),
            pltpu.SemaphoreType.DMA((4,)),
            pltpu.SemaphoreType.DMA((5,)),
            pltpu.SemaphoreType.DMA,
            pltpu.SemaphoreType.DMA,
        ],
        compiler_params=pltpu.CompilerParams(vmem_limit_bytes=24 << 20),
        name="forward",
    )(*in_hbm(ray_slot, blocks, foots, volume, prints))


def tables_kernel(owned, ray_slot, blocks, counts, counts_turned, picks):
    position = lax.axis_index("tile")
    rows = counts_turned.shape[0]

    counts_turned[...] = counts[...].astype(F32).T[:rows].astype(BF16)

    owners = picks.shape[0]
    width = blocks.shape[1]
    second = jnp.int32(0)
    for b in range(ray_slot.shape[0]):
        second = jnp.where(ray_slot[b] == position * owned + 1, b, second)
    hit = jnp.max(jnp.where(blocks[...] == second, 1.0, 0.0), axis=0, keepdims=True)
    start = iota((owners, width), 0) * rows
    at = iota((owners, width), 1)
    member = ((at >= start) & (at < start + rows)).astype(BF16)
    count = lax.dot_general(
        member,
        jnp.broadcast_to(hit, (lanes, width)).astype(BF16),
        (((1,), (1,)), ((), ())),
        preferred_element_type=F32,
    )
    picks[...] = jnp.where(count > 0.5, 1.0, 0.0)


def tables(owned, owners, rows, ray_slot, blocks, counts):
    return pl.pallas_call(
        functools.partial(tables_kernel, owned),
        out_shape=(
            jax.ShapeDtypeStruct((rows, counts.shape[0]), BF16),
            jax.ShapeDtypeStruct((owners, lanes), F32),
        ),
        in_specs=[SMEM] + [VMEM] * 2,
        out_specs=(VMEM,) * 2,
        compiler_params=pltpu.CompilerParams(vmem_limit_bytes=8 << 20),
        name="tables",
    )(ray_slot, blocks, counts)


def variation_kernel(spans, refs, base, rows_buf, out_buf, slice_flux, in_sems, out_sems):
    volume, before_slice, after_slice = refs[:3]
    before_row, after_row = refs[3:5] if len(refs) > 3 else (None, None)
    rows, slices, pixels = volume.shape
    position = lax.axis_index("tile")
    layer = lax.axis_index("slab")
    last_position = lax.axis_size("tile") - 1
    last_layer = lax.axis_size("slab") - 1

    pieces = []
    for first, end in spans:
        pieces += [(r, min(r + 16, end)) for r in range(first, end, 16)]
    seen = set()
    loads = []
    for first, end in pieces:
        need = [r for r in range(max(first - 1, 0), min(end + 1, rows)) if r not in seen]
        seen |= set(need)
        span = pl.ds(need[0], len(need))
        copy = pltpu.make_async_copy(
            volume.at[span], rows_buf.at[span], in_sems.at[len(loads)]
        )
        copy.start()
        loads.append(copy)

    lane = iota((1, pixels), 1)
    inner = lane < pixels - 1
    left_edge = lane == 0

    def col_grad(x):
        return jnp.where(inner, pltpu.roll(x, pixels - 1, 1) - x, 0.0)

    def scale(a, b, c):
        return lax.rsqrt(a * a + b * b + c * c + smoothing)

    z_id = iota((slices, 1), 0)
    top = z_id == slices - 1
    bottom = z_id == 0
    keep = jnp.where(top & (layer == last_layer), 0.0, 1.0)

    def fluxes(here, next_row, beyond, last=False):
        up = jnp.where(top, beyond, pltpu.roll(here, slices - 1, 0))
        grad_slices = (up - here) * keep
        grad_rows = jnp.where(last, 0.0, next_row - here)
        grad_cols = col_grad(here)
        inverse = scale(grad_rows, grad_slices, grad_cols)
        return grad_rows * inverse, grad_slices * inverse, grad_cols * inverse

    stores = []
    held = None
    for i, (first, end) in enumerate(pieces):
        loads[i].wait()
        count = end - first
        low = before_slice[first:end]
        if end < rows:
            low_next = jnp.concatenate([low[1:], before_slice[end : end + 1]], axis=0)
        else:
            low_next = jnp.concatenate([low[1:], after_row[0:1]], axis=0)
        grad_rows = low_next - low
        if end == rows:
            final = (iota((count, 1), 0) == count - 1) & (position == last_position)
            grad_rows = jnp.where(final, 0.0, grad_rows)
        bottoms = jnp.concatenate([rows_buf[r, 0:1] for r in range(first, end)], axis=0)
        grad_slices = bottoms - low
        flux = grad_slices * scale(grad_rows, grad_slices, col_grad(low))
        slice_flux[first:end] = jnp.where(layer == 0, 0.0, flux)

        if held is None or pieces[i - 1][1] != first:
            if first == 0:
                held, _, _ = fluxes(
                    before_row[1 : slices + 1], rows_buf[0], before_row[slices + 1 : slices + 2]
                )
                held = jnp.where(position == 0, 0.0, held)
            else:
                held, _, _ = fluxes(
                    rows_buf[first - 1], rows_buf[first], after_slice[first - 1 : first]
                )

        def one(r, here, next_row, previous, last=False):
            flux_rows, flux_slices, flux_cols = fluxes(
                here, next_row, after_slice[pl.ds(r, 1), :], last
            )
            below = jnp.where(
                bottom, slice_flux[pl.ds(r, 1), :], pltpu.roll(flux_slices, 1, 0)
            )
            left = jnp.where(left_edge, 0.0, pltpu.roll(flux_cols, 1, 1))
            variation = (previous - flux_rows) + (below - flux_slices) + (left - flux_cols)
            out_buf[r] = here - (step_length * variation_weight) * variation
            return flux_rows

        held = lax.fori_loop(
            first,
            min(end, rows - 1),
            lambda r, previous: one(r, rows_buf[r], rows_buf[r + 1], previous),
            held,
        )
        if end == rows:
            one(
                rows - 1, rows_buf[rows - 1], after_row[1 : slices + 1], held,
                position == last_position,
            )
        span = pl.ds(first, count)
        copy = pltpu.make_async_copy(out_buf.at[span], base.at[span], out_sems.at[i])
        copy.start()
        stores.append(copy)
    for copy in stores:
        copy.wait()


def variation_first_kernel(volume, before_slice, after_slice, base, *scratch):
    spans = [(8, volume.shape[0] // 2 + 8)]
    variation_kernel(spans, (volume, before_slice, after_slice), base, *scratch)


def variation_rest_kernel(part, *refs):
    rows = refs[0].shape[0]
    spans = [(rows // 2 + 8, rows), (0, 8)]
    variation_kernel(spans, refs[:5], *refs[5:])


def variation_call(kernel, aliases, volume, begin, halos):
    rows, _, pixels = volume.shape
    return pl.pallas_call(
        kernel,
        out_shape=pltpu.HBM(volume.shape, F32),
        in_specs=[HBM] * (len(begin) + 1) + [VMEM] * len(halos),
        out_specs=HBM,
        scratch_shapes=[
            pltpu.VMEM(volume.shape, F32),
            pltpu.VMEM(volume.shape, F32),
            pltpu.VMEM((rows, pixels), F32),
            pltpu.SemaphoreType.DMA((8,)),
            pltpu.SemaphoreType.DMA((8,)),
        ],
        input_output_aliases=aliases,
        compiler_params=pltpu.CompilerParams(vmem_limit_bytes=16 << 20),
    )(*in_hbm(*begin, volume), *halos)


def variation_first(volume, *halos):
    return variation_call(variation_first_kernel, {}, volume, (), halos)


def variation_rest(part, volume, *halos):
    return variation_call(variation_rest_kernel, {0: 0}, volume, (part,), halos)


def residual_kernel(arrived, picks, measured, weights, returned):
    owners = arrived.shape[0]
    sums = [jnp.zeros(measured.shape[1:], F32) for _ in range(2)]
    for j in range(owners):
        part = arrived[j].astype(F32)
        chosen = picks[j : j + 1, :] > 0.5
        sums[0] = sums[0] + jnp.where(chosen, 0.0, part)
        sums[1] = sums[1] + jnp.where(chosen, part, 0.0)
    out = [(weights[i] * (sums[i] - measured[i])).astype(BF16).astype(F32) for i in range(2)]
    for j in range(owners):
        returned[j] = jnp.where(picks[j : j + 1, :] > 0.5, out[1], out[0]).astype(BF16)


def residual(arrived, picks, measured, weights):
    return pl.pallas_call(
        residual_kernel,
        out_shape=jax.ShapeDtypeStruct(arrived.shape, BF16),
        in_specs=[VMEM] * 4,
        out_specs=VMEM,
        compiler_params=pltpu.CompilerParams(vmem_limit_bytes=4 << 20),
        name="residual",
    )(arrived, picks, measured, weights)


def backward_kernel(
    touch, table, returned, prints, counts_turned, base,
    out, gathered, mixed, spread, base_buf, out_buf, prints_buf, sems, prints_sems, base_sems,
):
    _, slices, pixels = base.shape
    foot_count, _, rays = prints.shape
    parts = prints_sems.shape[0]
    per_part = foot_count // parts

    def prints_copy(g):
        span = pl.ds(g * per_part, per_part)
        return pltpu.make_async_copy(prints.at[span], prints_buf.at[span], prints_sems.at[g])

    for g in range(parts):
        prints_copy(g).start()
    half = slices // 2
    groups = sems.shape[0]
    group_size = half // groups
    for z in range(half):
        for z in (z, z + half):
            pltpu.make_async_copy(
                base.at[:, z, :], base_buf.at[z], base_sems.at[z % half // group_size]
            ).start()
    for s in range(touch):
        owner = table[1, s]
        block = returned[jnp.maximum(owner, 0)].astype(F32)
        gathered[s] = jnp.where(owner >= 0, block, 0.0)
    mixed[...] = jnp.swapaxes(gathered[...], 0, 1).reshape(slices * touch, rays).astype(BF16)
    block = 256
    zero = jnp.zeros(prints.shape[1:], BF16)

    @pl.loop(0, parts)
    def _(g):
        prints_copy(g).wait()
        for f in range(per_part):
            weight = prints_buf[per_part * g + f]
            weights = jnp.concatenate(
                [
                    jnp.concatenate([weight, zero], axis=1),
                    jnp.concatenate([zero, weight], axis=1),
                ],
                axis=0,
            )
            for m in range(0, half * touch, block):
                left = jnp.concatenate(
                    [mixed[m : m + block], mixed[half * touch + m : half * touch + m + block]], axis=1
                )
                value = lax.dot_general(
                    left, weights, (((1,), (1,)), ((), ())), preferred_element_type=F32
                ).astype(BF16)
                for i in range(block // touch):
                    row = pl.multiple_of((per_part * g + f) * touch, touch)
                    spread[m // touch + i, pl.ds(row, touch), :] = value[
                        i * touch : (i + 1) * touch
                    ]

    @pl.loop(0, groups)
    def _(i):
        arrived = base_buf.at[pl.ds(0, 2 * group_size)]
        pltpu.make_async_copy(arrived, arrived, base_sems.at[i]).wait()
        for j in range(group_size):
            z = i * group_size + j
            grad = jnp.dot(counts_turned[...], spread[z], preferred_element_type=F32)
            for g in range(2):
                at = z + g * half
                out_buf[at] = jnp.maximum(
                    base_buf[at] - step_length * grad[:, g * pixels : (g + 1) * pixels], 0.0
                )
        for j in range(group_size):
            for g in range(2):
                at = i * group_size + j + g * half
                pltpu.make_async_copy(out_buf.at[at], out.at[:, at, :], sems.at[i]).start()

    for i in range(groups):
        both = out_buf.at[pl.ds(0, 2 * group_size)]
        pltpu.make_async_copy(both, both, sems.at[i]).wait()


def backward(touch, table, returned, prints, counts_turned, base):
    rows, slices, pixels = base.shape
    codes = prints.shape[0] * touch
    return pl.pallas_call(
        functools.partial(backward_kernel, touch),
        out_shape=jax.ShapeDtypeStruct((rows, slices, pixels), F32),
        in_specs=[SMEM, VMEM, HBM, VMEM, HBM],
        out_specs=HBM,
        scratch_shapes=[
            pltpu.VMEM((touch, slices, prints.shape[2]), F32),
            pltpu.VMEM((slices * touch, prints.shape[2]), BF16),
            pltpu.VMEM((slices // 2, codes, 2 * pixels), BF16),
            pltpu.VMEM((slices, rows, pixels), F32),
            pltpu.VMEM((slices, rows, pixels), F32),
            pltpu.VMEM(prints.shape, BF16),
            pltpu.SemaphoreType.DMA((4,)),
            pltpu.SemaphoreType.DMA((4,)),
            pltpu.SemaphoreType.DMA((4,)),
        ],
        compiler_params=pltpu.CompilerParams(vmem_limit_bytes=24 << 20),
        name="backward",
    )(table, returned, *in_hbm(prints), counts_turned, *in_hbm(base))


def shifted(x, axis, forward_way):
    count = lax.axis_size(axis)
    if forward_way:
        pairs = [(i, i + 1) for i in range(count - 1)]
    else:
        pairs = [(i + 1, i) for i in range(count - 1)]
    return lax.ppermute(x, axis, pairs)


def per_device(volume, footprints, foot_index, ray_block, ray_slot, measured, weights):
    row_count, _, _ = volume.shape
    owners = lax.axis_size("tile")
    owned = measured.shape[0]
    touch = owners // 2
    blocks = ray_block.T
    sent, table, counts, head, tail, first_row, last_row = forward(
        touch, owned, owners, ray_slot, blocks, foot_index.T, volume, footprints
    )
    arrived = lax.all_to_all(sent, "tile", split_axis=0, concat_axis=0, tiled=True)
    before_slice = shifted(tail, "slab", True)
    after_slice = shifted(head, "slab", False)
    counts_turned, picks = tables(owned, owners, row_count, ray_slot, blocks, counts)
    part = variation_first(volume, before_slice, after_slice)

    def edge(r, x):
        return jnp.concatenate(
            [before_slice[r : r + 1], x, after_slice[r : r + 1]], axis=0
        )

    edges = (edge(row_count - 1, last_row), edge(0, first_row))
    edges, part = lax.optimization_barrier((edges, part))
    before_row = shifted(edges[0], "tile", True)
    after_row = shifted(edges[1], "tile", False)
    arrived, _ = lax.optimization_barrier((arrived, edges))
    answer = residual(arrived, picks, measured, weights)
    returned = lax.all_to_all(answer, "tile", split_axis=0, concat_axis=0, tiled=True)
    halos, part, _ = lax.optimization_barrier(
        ((before_slice, after_slice, before_row, after_row), part, answer)
    )
    base = variation_rest(part, volume, *halos)
    return backward(touch, table, returned, footprints, counts_turned, base)


def solution(mesh):
    in_specs = (
        P("tile", "slab", None),
        P(),
        P("tile", None),
        P(),
        P(),
        P("tile", "slab", None),
        P("tile", "slab", None),
    )
    out_specs = P("tile", "slab", None)
    return jax.shard_map(
        per_device, mesh=mesh, in_specs=in_specs, out_specs=out_specs, check_vma=False
    )
```

```python
import functools

import jax
import jax.numpy as jnp
from jax import lax
from jax.experimental import pallas as pl
from jax.experimental.pallas import tpu as pltpu
from jax.sharding import PartitionSpec as P


smoothing = 0.04
step_length = 2.0
variation_weight = 1.0
lanes = 128

F32 = jnp.float32
BF16 = jnp.bfloat16
VMEM = pl.BlockSpec(memory_space=pltpu.VMEM)
SMEM = pl.BlockSpec(memory_space=pltpu.SMEM)
HBM = pl.BlockSpec(memory_space=pltpu.HBM)


def in_hbm(*arrays):
    return [pltpu.with_memory_space_constraint(x, pltpu.HBM) for x in arrays]


def iota(shape, dim):
    return lax.broadcasted_iota(jnp.int32, shape, dim)


def forward_kernel(
    touch, owned, ray_slot, blocks, foots, volume, prints,
    sent, table, counts, head, tail, first_row, last_row,
    window, foots_buf, slot_buf, by_slice, prints_buf, grouped, sums, compact, table_buf,
    sems, small_sems, table_sem, prints_sem,
):
    row_count, slice_count, _ = volume.shape
    foot_count = prints.shape[0]
    owners = sent.shape[0]
    crossings = blocks.shape[0]

    half = slice_count // 2
    groups = sems.shape[0]
    group_size = half // groups

    position = lax.axis_index("tile")
    offset = position * row_count
    limit = blocks.shape[1] - 2 * lanes
    base = jnp.minimum((offset // lanes) * lanes, limit)
    small = [
        pltpu.make_async_copy(source, target, small_sems.at[i])
        for i, (source, target) in enumerate(
            [
                (blocks.at[:, pl.ds(pl.multiple_of(base, lanes), 2 * lanes)], window),
                (foots, foots_buf),
                (ray_slot, slot_buf),
                (volume.at[0], first_row),
                (volume.at[row_count - 1], last_row),
            ]
        )
    ]
    for copy in small:
        copy.start()
    for z in range(half):
        for z in (z, z + half):
            pltpu.make_async_copy(
                volume.at[:, z, :], by_slice.at[z], sems.at[z % half // group_size]
            ).start()
    prints_copy = pltpu.make_async_copy(prints, prints_buf, prints_sem)
    prints_copy.start()

    for copy in small[:3]:
        copy.wait()
    mine = pltpu.roll(window[...], 2 * lanes - (offset - base), 1)[:, :lanes]
    slot = jnp.zeros_like(mine)
    for b in range(ray_slot.shape[0]):
        slot = jnp.where(mine == b, slot_buf[b], slot)
    valid = iota((crossings, lanes), 1) < row_count
    owner = jnp.where(valid, slot // owned, -1)
    label = iota((owners, lanes), 0)
    present = jnp.zeros((owners, lanes), F32)
    for k in range(crossings):
        present = jnp.where(owner[k : k + 1] == label, 1.0, present)
    present = jnp.broadcast_to(jnp.max(present, axis=1, keepdims=True), (owners, lanes))
    lower = (iota((owners, owners), 1) < iota((owners, owners), 0)).astype(BF16)
    rank = jnp.dot(lower, present.astype(BF16), preferred_element_type=F32)
    column = iota((owners, lanes), 1)
    rank_row = jnp.sum(jnp.where(label < column, present, 0.0), axis=0, keepdims=True)
    present_row = jnp.sum(jnp.where(label == column, present, 0.0), axis=0, keepdims=True)
    rank_row = jnp.where(present_row > 0.5, rank_row, -1.0).astype(jnp.int32)
    match = jnp.where((rank.astype(jnp.int32) == column) & (present > 0.5), label + 1, 0)
    owner_row = jnp.sum(match, axis=0, keepdims=True) - 1
    table_buf[...] = jnp.where(iota(table_buf.shape, 0) == 0, rank_row, owner_row)
    table_copy = pltpu.make_async_copy(table_buf, table, table_sem)
    table_copy.start()

    foots_here = jnp.concatenate(
        [foots_buf[...], jnp.zeros((crossings, lanes - row_count), jnp.int32)], axis=1
    )
    step = 4
    hits, feet = [], []
    rank_id = iota((touch, lanes), 0)
    for k in range(crossings):
        place = jnp.sum(
            jnp.where(owner[k : k + 1] == label, rank, 0.0), axis=0, keepdims=True
        ).astype(jnp.int32)
        hits.append(jnp.where((rank_id == place) & valid[k : k + 1], 1.0, 0.0).astype(BF16))
        feet.append(
            jnp.broadcast_to(foots_here[k : k + 1].astype(F32), (touch, lanes)).astype(BF16)
        )
    none = jnp.zeros((touch, lanes), BF16)
    for f in range(foot_count):
        terms = [jnp.where(foot == f, hit, none) for foot, hit in zip(feet, hits)]
        while len(terms) > 1:
            terms = [x + y for x, y in zip(terms[::2], terms[1::2])]
        counts[f * touch : (f + 1) * touch] = terms[0]

    @pl.loop(0, groups)
    def _(i):
        both = by_slice.at[pl.ds(0, 2 * group_size)]
        pltpu.make_async_copy(both, both, sems.at[i]).wait()
        for j in range(group_size):
            z = i * group_size + j
            pair = jnp.concatenate([by_slice[z], by_slice[z + half]], axis=1).astype(BF16)
            for first in range(0, foot_count, step):
                group = jnp.dot(
                    counts[first * touch : (first + step) * touch, :row_count],
                    pair,
                    preferred_element_type=F32,
                ).astype(BF16)
                for f in range(step):
                    grouped[first + f, pl.ds(pl.multiple_of(z * touch, touch), touch), :] = group[
                        f * touch : (f + 1) * touch
                    ]

    head[...] = by_slice[0]
    tail[...] = by_slice[slice_count - 1]
    prints_copy.wait()
    sums[...] = jnp.zeros_like(sums)
    deep = 16
    block = 256
    zero = jnp.zeros(prints.shape[1:], BF16)

    @pl.loop(0, foot_count // deep)
    def _(g):
        weights = []
        for h in range(deep):
            weight = prints_buf[g * deep + h]
            weights.append(jnp.concatenate([weight, zero], axis=1))
            weights.append(jnp.concatenate([zero, weight], axis=1))
        weights = jnp.concatenate(weights, axis=0)
        for m in range(0, half * touch, block):
            left = [grouped[g * deep + h, m : m + block, :] for h in range(deep)]
            both = jnp.dot(
                jnp.concatenate(left, axis=1), weights, preferred_element_type=F32
            )
            rays = both.shape[1] // 2
            sums[m : m + block] += both[:, :rays]
            sums[half * touch + m : half * touch + m + block] += both[:, rays:]

    compact[...] = jnp.swapaxes(sums[...].reshape(slice_count, touch, -1), 0, 1).astype(BF16)
    for copy in small[3:]:
        copy.wait()
    table_copy.wait()
    for t in range(owners):
        place = table[0, t]
        block = compact[jnp.maximum(place, 0)]
        sent[t] = jnp.where(place >= 0, block, jnp.zeros_like(block))


def forward(touch, owned, owners, ray_slot, blocks, foots, volume, prints):
    rows, slices, pixels = volume.shape
    foot_count, _, rays = prints.shape
    return pl.pallas_call(
        functools.partial(forward_kernel, touch, owned),
        out_shape=(
            jax.ShapeDtypeStruct((owners, slices, rays), BF16),
            jax.ShapeDtypeStruct((8, lanes), jnp.int32),
            jax.ShapeDtypeStruct((foot_count * touch, lanes), BF16),
            jax.ShapeDtypeStruct((rows, pixels), F32),
            jax.ShapeDtypeStruct((rows, pixels), F32),
            jax.ShapeDtypeStruct((slices, pixels), F32),
            jax.ShapeDtypeStruct((slices, pixels), F32),
        ),
        in_specs=[HBM] * 5,
        out_specs=(VMEM, SMEM) + (VMEM,) * 5,
        scratch_shapes=[
            pltpu.VMEM((blocks.shape[0], 2 * lanes), jnp.int32),
            pltpu.VMEM(foots.shape, jnp.int32),
            pltpu.SMEM(ray_slot.shape, jnp.int32),
            pltpu.VMEM((slices, rows, pixels), F32),
            pltpu.VMEM(prints.shape, BF16),
            pltpu.VMEM((foot_count, slices // 2 * touch, 2 * pixels), BF16),
            pltpu.VMEM((slices * touch, rays), F32),
            pltpu.VMEM((touch, slices, rays), BF16),
            pltpu.VMEM((8, lanes), jnp.int32),
            pltpu.SemaphoreType.DMA((4,)),
            pltpu.SemaphoreType.DMA((5,)),
            pltpu.SemaphoreType.DMA,
            pltpu.SemaphoreType.DMA,
        ],
        compiler_params=pltpu.CompilerParams(vmem_limit_bytes=24 << 20),
        name="forward",
    )(*in_hbm(ray_slot, blocks, foots, volume, prints))


def tables_kernel(owned, ray_slot, blocks, counts, counts_turned, picks):
    position = lax.axis_index("tile")
    rows = counts_turned.shape[0]

    counts_turned[...] = counts[...].astype(F32).T[:rows].astype(BF16)

    owners = picks.shape[0]
    width = blocks.shape[1]
    second = jnp.int32(0)
    for b in range(ray_slot.shape[0]):
        second = jnp.where(ray_slot[b] == position * owned + 1, b, second)
    hit = jnp.max(jnp.where(blocks[...] == second, 1.0, 0.0), axis=0, keepdims=True)
    start = iota((owners, width), 0) * rows
    at = iota((owners, width), 1)
    member = ((at >= start) & (at < start + rows)).astype(BF16)
    count = lax.dot_general(
        member,
        jnp.broadcast_to(hit, (lanes, width)).astype(BF16),
        (((1,), (1,)), ((), ())),
        preferred_element_type=F32,
    )
    picks[...] = jnp.where(count > 0.5, 1.0, 0.0)


def tables(owned, owners, rows, ray_slot, blocks, counts):
    return pl.pallas_call(
        functools.partial(tables_kernel, owned),
        out_shape=(
            jax.ShapeDtypeStruct((rows, counts.shape[0]), BF16),
            jax.ShapeDtypeStruct((owners, lanes), F32),
        ),
        in_specs=[SMEM] + [VMEM] * 2,
        out_specs=(VMEM,) * 2,
        compiler_params=pltpu.CompilerParams(vmem_limit_bytes=8 << 20),
        name="tables",
    )(ray_slot, blocks, counts)


def variation_kernel(
    volume, before_slice, after_slice, before_row, after_row, first_row,
    base, by_slice, row_flux, sems,
):
    slices, rows, pixels = base.shape

    groups = sems.shape[0]
    size = slices // groups
    for z in range(slices):
        pltpu.make_async_copy(volume.at[:, z, :], by_slice.at[z], sems.at[z // size]).start()

    def wait_group(i):
        span = by_slice.at[pl.ds(i * size, size)]
        pltpu.make_async_copy(span, span, sems.at[i]).wait()

    position = lax.axis_index("tile")
    layer = lax.axis_index("slab")
    last_position = lax.axis_size("tile") - 1
    last_layer = lax.axis_size("slab") - 1
    lane = iota((1, pixels), 1)
    inner = lane < pixels - 1
    first = lane == 0

    def col_grad(x):
        return jnp.where(inner, pltpu.roll(x, pixels - 1, 1) - x, 0.0)

    def scale(a, b, c):
        return lax.rsqrt(a * a + b * b + c * c + smoothing)

    low = before_row[1 : slices + 1]
    z_id = iota((slices, 1), 0)
    grad_slices = before_row[2 : slices + 2] - low
    grad_slices = jnp.where((z_id == slices - 1) & (layer == last_layer), 0.0, grad_slices)
    grad_rows = first_row[...] - low
    flux = grad_rows * scale(grad_rows, grad_slices, col_grad(low))
    row_flux[...] = jnp.where(position == 0, 0.0, flux)

    row_id = iota((rows, 1), 0)
    top = row_id == rows - 1
    bottom = row_id == 0
    keep = jnp.where(top & (position == last_position), 0.0, 1.0)

    def fluxes(here, next_slice, beyond, last):
        up = jnp.where(top, beyond, pltpu.roll(here, rows - 1, 0))
        grad_rows = (up - here) * keep
        grad_slices = jnp.where(last, 0.0, next_slice - here)
        grad_cols = col_grad(here)
        inverse = scale(grad_rows, grad_slices, grad_cols)
        return grad_rows * inverse, grad_slices * inverse, grad_cols * inverse

    wait_group(0)
    _, start, _ = fluxes(before_slice[...], by_slice[0], after_row[0:1], False)
    start = jnp.where(layer == 0, 0.0, start)

    def one(z, here, next_slice, previous, last):
        flux_rows, flux_slices, flux_cols = fluxes(
            here, next_slice, after_row[pl.ds(z + 1, 1), :], last
        )
        below = jnp.where(bottom, row_flux[pl.ds(z, 1), :], pltpu.roll(flux_rows, 1, 0))
        left = jnp.where(first, 0.0, pltpu.roll(flux_cols, 1, 1))
        variation = (previous - flux_slices) + (below - flux_rows) + (left - flux_cols)
        base[z] = here - (step_length * variation_weight) * variation
        return flux_slices

    def step(z, previous):
        @pl.when((z + 1) % size == 0)
        def _():
            wait_group((z + 1) // size)

        return one(z, by_slice[z], by_slice[z + 1], previous, False)

    final = lax.fori_loop(0, slices - 1, step, start)
    one(slices - 1, by_slice[slices - 1], after_slice[...], final, layer == last_layer)


def variation(volume, *halos):
    rows, slices, pixels = volume.shape
    return pl.pallas_call(
        variation_kernel,
        out_shape=jax.ShapeDtypeStruct((slices, rows, pixels), F32),
        in_specs=[HBM] + [VMEM] * 5,
        out_specs=VMEM,
        scratch_shapes=[
            pltpu.VMEM((slices, rows, pixels), F32),
            pltpu.VMEM((slices, pixels), F32),
            pltpu.SemaphoreType.DMA((8,)),
        ],
        compiler_params=pltpu.CompilerParams(vmem_limit_bytes=8 << 20),
        name="variation",
    )(*in_hbm(volume), *halos)


def residual_kernel(arrived, picks, measured, weights, returned):
    owners = arrived.shape[0]
    sums = [jnp.zeros(measured.shape[1:], F32) for _ in range(2)]
    for j in range(owners):
        part = arrived[j].astype(F32)
        chosen = picks[j : j + 1, :] > 0.5
        sums[0] = sums[0] + jnp.where(chosen, 0.0, part)
        sums[1] = sums[1] + jnp.where(chosen, part, 0.0)
    out = [(weights[i] * (sums[i] - measured[i])).astype(BF16).astype(F32) for i in range(2)]
    for j in range(owners):
        returned[j] = jnp.where(picks[j : j + 1, :] > 0.5, out[1], out[0]).astype(BF16)


def residual(arrived, picks, measured, weights):
    return pl.pallas_call(
        residual_kernel,
        out_shape=jax.ShapeDtypeStruct(arrived.shape, BF16),
        in_specs=[VMEM] * 4,
        out_specs=VMEM,
        compiler_params=pltpu.CompilerParams(vmem_limit_bytes=4 << 20),
        name="residual",
    )(arrived, picks, measured, weights)


def backward_kernel(
    touch, table, returned, prints, counts_turned, base,
    out, gathered, mixed, spread, out_buf, prints_buf, sems, prints_sems,
):
    slices, _, pixels = base.shape
    foot_count, _, rays = prints.shape
    parts = prints_sems.shape[0]
    per_part = foot_count // parts

    def prints_copy(g):
        span = pl.ds(g * per_part, per_part)
        return pltpu.make_async_copy(prints.at[span], prints_buf.at[span], prints_sems.at[g])

    for g in range(parts):
        prints_copy(g).start()
    for s in range(touch):
        owner = table[1, s]
        block = returned[jnp.maximum(owner, 0)].astype(F32)
        gathered[s] = jnp.where(owner >= 0, block, 0.0)
    mixed[...] = jnp.swapaxes(gathered[...], 0, 1).reshape(slices * touch, rays).astype(BF16)
    half = slices // 2
    block = 256
    zero = jnp.zeros(prints.shape[1:], BF16)

    @pl.loop(0, parts)
    def _(g):
        prints_copy(g).wait()
        for f in range(per_part):
            weight = prints_buf[per_part * g + f]
            weights = jnp.concatenate(
                [
                    jnp.concatenate([weight, zero], axis=1),
                    jnp.concatenate([zero, weight], axis=1),
                ],
                axis=0,
            )
            for m in range(0, half * touch, block):
                left = jnp.concatenate(
                    [mixed[m : m + block], mixed[half * touch + m : half * touch + m + block]], axis=1
                )
                value = lax.dot_general(
                    left, weights, (((1,), (1,)), ((), ())), preferred_element_type=F32
                ).astype(BF16)
                for i in range(block // touch):
                    row = pl.multiple_of((per_part * g + f) * touch, touch)
                    spread[m // touch + i, pl.ds(row, touch), :] = value[
                        i * touch : (i + 1) * touch
                    ]

    groups = sems.shape[0]
    group_size = half // groups

    @pl.loop(0, groups)
    def _(i):
        for j in range(group_size):
            z = i * group_size + j
            grad = jnp.dot(counts_turned[...], spread[z], preferred_element_type=F32)
            for g in range(2):
                at = z + g * half
                out_buf[at] = jnp.maximum(
                    base[at] - step_length * grad[:, g * pixels : (g + 1) * pixels], 0.0
                )
        for j in range(group_size):
            for g in range(2):
                at = i * group_size + j + g * half
                pltpu.make_async_copy(out_buf.at[at], out.at[:, at, :], sems.at[i]).start()

    for i in range(groups):
        both = out_buf.at[pl.ds(0, 2 * group_size)]
        pltpu.make_async_copy(both, both, sems.at[i]).wait()


def backward(touch, table, returned, prints, counts_turned, base):
    slices, rows, pixels = base.shape
    codes = prints.shape[0] * touch
    return pl.pallas_call(
        functools.partial(backward_kernel, touch),
        out_shape=jax.ShapeDtypeStruct((rows, slices, pixels), F32),
        in_specs=[SMEM, VMEM, HBM, VMEM, VMEM],
        out_specs=HBM,
        scratch_shapes=[
            pltpu.VMEM((touch, slices, prints.shape[2]), F32),
            pltpu.VMEM((slices * touch, prints.shape[2]), BF16),
            pltpu.VMEM((slices // 2, codes, 2 * pixels), BF16),
            pltpu.VMEM((slices, rows, pixels), F32),
            pltpu.VMEM(prints.shape, BF16),
            pltpu.SemaphoreType.DMA((4,)),
            pltpu.SemaphoreType.DMA((4,)),
        ],
        compiler_params=pltpu.CompilerParams(vmem_limit_bytes=24 << 20),
        name="backward",
    )(table, returned, *in_hbm(prints), counts_turned, base)


def shifted(x, axis, forward_way):
    count = lax.axis_size(axis)
    if forward_way:
        pairs = [(i, i + 1) for i in range(count - 1)]
    else:
        pairs = [(i + 1, i) for i in range(count - 1)]
    return lax.ppermute(x, axis, pairs)


def per_device(volume, footprints, foot_index, ray_block, ray_slot, measured, weights):
    row_count, _, _ = volume.shape
    owners = lax.axis_size("tile")
    owned = measured.shape[0]
    touch = owners // 2
    blocks = ray_block.T
    sent, table, counts, head, tail, first_row, last_row = forward(
        touch, owned, owners, ray_slot, blocks, foot_index.T, volume, footprints
    )
    arrived = lax.all_to_all(sent, "tile", split_axis=0, concat_axis=0, tiled=True)
    before_slice = shifted(tail, "slab", True)
    after_slice = shifted(head, "slab", False)
    counts_turned, picks = tables(owned, owners, row_count, ray_slot, blocks, counts)

    def edge(r, x):
        return jnp.concatenate(
            [before_slice[r : r + 1], x, after_slice[r : r + 1]], axis=0
        )

    edges = (edge(row_count - 1, last_row), edge(0, first_row))
    before_row = shifted(edges[0], "tile", True)
    after_row = shifted(edges[1], "tile", False)
    arrived, _ = lax.optimization_barrier((arrived, edges))
    answer = residual(arrived, picks, measured, weights)
    returned = lax.all_to_all(answer, "tile", split_axis=0, concat_axis=0, tiled=True)
    halos, _ = lax.optimization_barrier(
        ((before_slice, after_slice, before_row, after_row, first_row), answer)
    )
    base = variation(volume, *halos)
    return backward(touch, table, returned, footprints, counts_turned, base)


def solution(mesh):
    in_specs = (
        P("tile", "slab", None),
        P(),
        P("tile", None),
        P(),
        P(),
        P("tile", "slab", None),
        P("tile", "slab", None),
    )
    out_specs = P("tile", "slab", None)
    return jax.shard_map(
        per_device, mesh=mesh, in_specs=in_specs, out_specs=out_specs, check_vma=False
    )
```

```python
import functools

import jax
import jax.numpy as jnp
from jax import lax
from jax.experimental import pallas as pl
from jax.experimental.pallas import tpu as pltpu
from jax.sharding import PartitionSpec as P


smoothing = 0.04
step_length = 2.0
variation_weight = 1.0
lanes = 128

F32 = jnp.float32
BF16 = jnp.bfloat16
VMEM = pl.BlockSpec(memory_space=pltpu.VMEM)
SMEM = pl.BlockSpec(memory_space=pltpu.SMEM)
HBM = pl.BlockSpec(memory_space=pltpu.HBM)


def in_hbm(*arrays):
    return [pltpu.with_memory_space_constraint(x, pltpu.HBM) for x in arrays]


def iota(shape, dim):
    return lax.broadcasted_iota(jnp.int32, shape, dim)


def forward_kernel(
    touch, owned, ray_slot, blocks, foots, volume, prints,
    sent, table, counts, head, tail, first_row, last_row,
    window, foots_buf, slot_buf, by_slice, prints_buf, grouped, sums, compact, table_buf,
    sems, small_sems, table_sem, prints_sem,
):
    row_count, slice_count, _ = volume.shape
    foot_count = prints.shape[0]
    owners = sent.shape[0]
    crossings = blocks.shape[0]

    half = slice_count // 2
    groups = sems.shape[0]
    group_size = half // groups

    position = lax.axis_index("tile")
    offset = position * row_count
    limit = blocks.shape[1] - 2 * lanes
    base = jnp.minimum((offset // lanes) * lanes, limit)
    small = [
        pltpu.make_async_copy(source, target, small_sems.at[i])
        for i, (source, target) in enumerate(
            [
                (blocks.at[:, pl.ds(pl.multiple_of(base, lanes), 2 * lanes)], window),
                (foots, foots_buf),
                (ray_slot, slot_buf),
                (volume.at[0], first_row),
                (volume.at[row_count - 1], last_row),
            ]
        )
    ]
    for copy in small:
        copy.start()
    for z in range(half):
        for z in (z, z + half):
            pltpu.make_async_copy(
                volume.at[:, z, :], by_slice.at[z], sems.at[z % half // group_size]
            ).start()
    prints_copy = pltpu.make_async_copy(prints, prints_buf, prints_sem)
    prints_copy.start()

    for copy in small[:3]:
        copy.wait()
    mine = pltpu.roll(window[...], 2 * lanes - (offset - base), 1)[:, :lanes]
    slot = jnp.zeros_like(mine)
    for b in range(ray_slot.shape[0]):
        slot = jnp.where(mine == b, slot_buf[b], slot)
    valid = iota((crossings, lanes), 1) < row_count
    owner = jnp.where(valid, slot // owned, -1)
    label = iota((owners, lanes), 0)
    present = jnp.zeros((owners, lanes), F32)
    for k in range(crossings):
        present = jnp.where(owner[k : k + 1] == label, 1.0, present)
    present = jnp.broadcast_to(jnp.max(present, axis=1, keepdims=True), (owners, lanes))
    lower = (iota((owners, owners), 1) < iota((owners, owners), 0)).astype(BF16)
    rank = jnp.dot(lower, present.astype(BF16), preferred_element_type=F32)
    column = iota((owners, lanes), 1)
    rank_row = jnp.sum(jnp.where(label < column, present, 0.0), axis=0, keepdims=True)
    present_row = jnp.sum(jnp.where(label == column, present, 0.0), axis=0, keepdims=True)
    rank_row = jnp.where(present_row > 0.5, rank_row, -1.0).astype(jnp.int32)
    match = jnp.where((rank.astype(jnp.int32) == column) & (present > 0.5), label + 1, 0)
    owner_row = jnp.sum(match, axis=0, keepdims=True) - 1
    table_buf[...] = jnp.where(iota(table_buf.shape, 0) == 0, rank_row, owner_row)
    table_copy = pltpu.make_async_copy(table_buf, table, table_sem)
    table_copy.start()

    foots_here = jnp.concatenate(
        [foots_buf[...], jnp.zeros((crossings, lanes - row_count), jnp.int32)], axis=1
    )
    hits, feet = [], []
    rank_id = iota((touch, lanes), 0)
    for k in range(crossings):
        place = jnp.sum(
            jnp.where(owner[k : k + 1] == label, rank, 0.0), axis=0, keepdims=True
        ).astype(jnp.int32)
        hits.append(jnp.where((rank_id == place) & valid[k : k + 1], 1.0, 0.0).astype(BF16))
        feet.append(
            jnp.broadcast_to(foots_here[k : k + 1].astype(F32), (touch, lanes)).astype(BF16)
        )
    none = jnp.zeros((touch, lanes), BF16)
    for f in range(foot_count):
        terms = [jnp.where(foot == f, hit, none) for foot, hit in zip(feet, hits)]
        while len(terms) > 1:
            terms = [x + y for x, y in zip(terms[::2], terms[1::2])]
        counts[f * touch : (f + 1) * touch] = terms[0]

    wide = 16

    @pl.loop(0, groups)
    def _(i):
        both = by_slice.at[pl.ds(0, 2 * group_size)]
        pltpu.make_async_copy(both, both, sems.at[i]).wait()
        for j in range(group_size):
            z = i * group_size + j
            pair = jnp.concatenate([by_slice[z], by_slice[z + half]], axis=1).astype(BF16)
            for first in range(0, foot_count, wide):
                group = jnp.dot(
                    counts[first * touch : (first + wide) * touch, :row_count],
                    pair,
                    preferred_element_type=F32,
                ).astype(BF16)
                for f in range(wide):
                    grouped[first + f, pl.ds(pl.multiple_of(z * touch, touch), touch), :] = group[
                        f * touch : (f + 1) * touch
                    ]

    head[...] = by_slice[0]
    tail[...] = by_slice[slice_count - 1]
    prints_copy.wait()
    block = 256
    zero = jnp.zeros(prints.shape[1:], BF16)
    weights = []
    for f in range(foot_count):
        weight = prints_buf[f]
        weights.append(jnp.concatenate([weight, zero], axis=1))
        weights.append(jnp.concatenate([zero, weight], axis=1))
    weights = jnp.concatenate(weights, axis=0)
    for m in range(0, half * touch, block):
        left = [grouped[f, m : m + block, :] for f in range(foot_count)]
        both = jnp.dot(jnp.concatenate(left, axis=1), weights, preferred_element_type=F32)
        rays = both.shape[1] // 2
        sums[m : m + block] = both[:, :rays]
        sums[half * touch + m : half * touch + m + block] = both[:, rays:]

    compact[...] = jnp.swapaxes(sums[...].reshape(slice_count, touch, -1), 0, 1).astype(BF16)
    for copy in small[3:]:
        copy.wait()
    table_copy.wait()
    for t in range(owners):
        place = table[0, t]
        block = compact[jnp.maximum(place, 0)]
        sent[t] = jnp.where(place >= 0, block, jnp.zeros_like(block))


def forward(touch, owned, owners, ray_slot, blocks, foots, volume, prints):
    rows, slices, pixels = volume.shape
    foot_count, _, rays = prints.shape
    return pl.pallas_call(
        functools.partial(forward_kernel, touch, owned),
        out_shape=(
            jax.ShapeDtypeStruct((owners, slices, rays), BF16),
            jax.ShapeDtypeStruct((8, lanes), jnp.int32),
            jax.ShapeDtypeStruct((foot_count * touch, lanes), BF16),
            jax.ShapeDtypeStruct((rows, pixels), F32),
            jax.ShapeDtypeStruct((rows, pixels), F32),
            jax.ShapeDtypeStruct((slices, pixels), F32),
            jax.ShapeDtypeStruct((slices, pixels), F32),
        ),
        in_specs=[HBM] * 5,
        out_specs=(VMEM, SMEM) + (VMEM,) * 5,
        scratch_shapes=[
            pltpu.VMEM((blocks.shape[0], 2 * lanes), jnp.int32),
            pltpu.VMEM(foots.shape, jnp.int32),
            pltpu.SMEM(ray_slot.shape, jnp.int32),
            pltpu.VMEM((slices, rows, pixels), F32),
            pltpu.VMEM(prints.shape, BF16),
            pltpu.VMEM((foot_count, slices // 2 * touch, 2 * pixels), BF16),
            pltpu.VMEM((slices * touch, rays), F32),
            pltpu.VMEM((touch, slices, rays), BF16),
            pltpu.VMEM((8, lanes), jnp.int32),
            pltpu.SemaphoreType.DMA((4,)),
            pltpu.SemaphoreType.DMA((5,)),
            pltpu.SemaphoreType.DMA,
            pltpu.SemaphoreType.DMA,
        ],
        compiler_params=pltpu.CompilerParams(vmem_limit_bytes=24 << 20),
        name="forward",
    )(*in_hbm(ray_slot, blocks, foots, volume, prints))


def tables_kernel(owned, ray_slot, blocks, counts, counts_turned, picks):
    position = lax.axis_index("tile")
    rows = counts_turned.shape[0]

    counts_turned[...] = counts[...].astype(F32).T[:rows].astype(BF16)

    owners = picks.shape[0]
    width = blocks.shape[1]
    second = jnp.int32(0)
    for b in range(ray_slot.shape[0]):
        second = jnp.where(ray_slot[b] == position * owned + 1, b, second)
    hit = jnp.max(jnp.where(blocks[...] == second, 1.0, 0.0), axis=0, keepdims=True)
    start = iota((owners, width), 0) * rows
    at = iota((owners, width), 1)
    member = ((at >= start) & (at < start + rows)).astype(BF16)
    count = lax.dot_general(
        member,
        jnp.broadcast_to(hit, (lanes, width)).astype(BF16),
        (((1,), (1,)), ((), ())),
        preferred_element_type=F32,
    )
    picks[...] = jnp.where(count > 0.5, 1.0, 0.0)


def tables(owned, owners, rows, ray_slot, blocks, counts):
    return pl.pallas_call(
        functools.partial(tables_kernel, owned),
        out_shape=(
            jax.ShapeDtypeStruct((rows, counts.shape[0]), BF16),
            jax.ShapeDtypeStruct((owners, lanes), F32),
        ),
        in_specs=[SMEM] + [VMEM] * 2,
        out_specs=(VMEM,) * 2,
        compiler_params=pltpu.CompilerParams(vmem_limit_bytes=8 << 20),
        name="tables",
    )(ray_slot, blocks, counts)


def variation_kernel(
    volume, before_slice, after_slice, before_row, after_row, first_row,
    base, by_slice, row_flux, sems,
):
    slices, rows, pixels = base.shape

    groups = sems.shape[0]
    size = slices // groups
    for z in range(slices):
        pltpu.make_async_copy(volume.at[:, z, :], by_slice.at[z], sems.at[z // size]).start()

    def wait_group(i):
        span = by_slice.at[pl.ds(i * size, size)]
        pltpu.make_async_copy(span, span, sems.at[i]).wait()

    position = lax.axis_index("tile")
    layer = lax.axis_index("slab")
    last_position = lax.axis_size("tile") - 1
    last_layer = lax.axis_size("slab") - 1
    lane = iota((1, pixels), 1)
    inner = lane < pixels - 1
    first = lane == 0

    def col_grad(x):
        return jnp.where(inner, pltpu.roll(x, pixels - 1, 1) - x, 0.0)

    def scale(a, b, c):
        return lax.rsqrt(a * a + b * b + c * c + smoothing)

    low = before_row[:slices]
    z_id = iota((slices, 1), 0)
    grad_slices = before_row[1 : slices + 1] - low
    grad_slices = jnp.where((z_id == slices - 1) & (layer == last_layer), 0.0, grad_slices)
    grad_rows = first_row[...] - low
    flux = grad_rows * scale(grad_rows, grad_slices, col_grad(low))
    row_flux[...] = jnp.where(position == 0, 0.0, flux)

    row_id = iota((rows, 1), 0)
    top = row_id == rows - 1
    bottom = row_id == 0
    keep = jnp.where(top & (position == last_position), 0.0, 1.0)

    def fluxes(here, next_slice, beyond, last):
        up = jnp.where(top, beyond, pltpu.roll(here, rows - 1, 0))
        grad_rows = (up - here) * keep
        grad_slices = jnp.where(last, 0.0, next_slice - here)
        grad_cols = col_grad(here)
        inverse = scale(grad_rows, grad_slices, grad_cols)
        return grad_rows * inverse, grad_slices * inverse, grad_cols * inverse

    wait_group(0)
    _, start, _ = fluxes(before_slice[...], by_slice[0], after_row[slices : slices + 1], False)
    start = jnp.where(layer == 0, 0.0, start)

    def one(z, here, next_slice, previous, last):
        flux_rows, flux_slices, flux_cols = fluxes(
            here, next_slice, after_row[pl.ds(z, 1), :], last
        )
        below = jnp.where(bottom, row_flux[pl.ds(z, 1), :], pltpu.roll(flux_rows, 1, 0))
        left = jnp.where(first, 0.0, pltpu.roll(flux_cols, 1, 1))
        variation = (previous - flux_slices) + (below - flux_rows) + (left - flux_cols)
        base[z] = here - (step_length * variation_weight) * variation
        return flux_slices

    def step(z, previous):
        @pl.when((z + 1) % size == 0)
        def _():
            wait_group((z + 1) // size)

        return one(z, by_slice[z], by_slice[z + 1], previous, False)

    final = lax.fori_loop(0, slices - 1, step, start)
    one(slices - 1, by_slice[slices - 1], after_slice[...], final, layer == last_layer)


def variation(volume, *halos):
    rows, slices, pixels = volume.shape
    return pl.pallas_call(
        variation_kernel,
        out_shape=jax.ShapeDtypeStruct((slices, rows, pixels), F32),
        in_specs=[HBM] + [VMEM] * 5,
        out_specs=VMEM,
        scratch_shapes=[
            pltpu.VMEM((slices, rows, pixels), F32),
            pltpu.VMEM((slices, pixels), F32),
            pltpu.SemaphoreType.DMA((8,)),
        ],
        compiler_params=pltpu.CompilerParams(vmem_limit_bytes=8 << 20),
        name="variation",
    )(*in_hbm(volume), *halos)


def residual_kernel(arrived, picks, measured, weights, returned):
    owners = arrived.shape[0]
    sums = [jnp.zeros(measured.shape[1:], F32) for _ in range(2)]
    for j in range(owners):
        part = arrived[j].astype(F32)
        chosen = picks[j : j + 1, :] > 0.5
        sums[0] = sums[0] + jnp.where(chosen, 0.0, part)
        sums[1] = sums[1] + jnp.where(chosen, part, 0.0)
    out = [(weights[i] * (sums[i] - measured[i])).astype(BF16).astype(F32) for i in range(2)]
    for j in range(owners):
        returned[j] = jnp.where(picks[j : j + 1, :] > 0.5, out[1], out[0]).astype(BF16)


def residual(arrived, picks, measured, weights):
    return pl.pallas_call(
        residual_kernel,
        out_shape=jax.ShapeDtypeStruct(arrived.shape, BF16),
        in_specs=[VMEM] * 4,
        out_specs=VMEM,
        compiler_params=pltpu.CompilerParams(vmem_limit_bytes=4 << 20),
        name="residual",
    )(arrived, picks, measured, weights)


def backward_kernel(
    touch, table, returned, prints, counts_turned, base,
    out, gathered, mixed, spread, out_buf, prints_buf, sems, prints_sems,
):
    slices, _, pixels = base.shape
    foot_count, _, rays = prints.shape
    parts = prints_sems.shape[0]
    per_part = foot_count // parts

    def prints_copy(g):
        span = pl.ds(g * per_part, per_part)
        return pltpu.make_async_copy(prints.at[span], prints_buf.at[span], prints_sems.at[g])

    for g in range(parts):
        prints_copy(g).start()
    for s in range(touch):
        owner = table[1, s]
        block = returned[jnp.maximum(owner, 0)].astype(F32)
        gathered[s] = jnp.where(owner >= 0, block, 0.0)
    mixed[...] = jnp.swapaxes(gathered[...], 0, 1).reshape(slices * touch, rays).astype(BF16)
    half = slices // 2
    block = 256
    zero = jnp.zeros(prints.shape[1:], BF16)

    @pl.loop(0, parts)
    def _(g):
        prints_copy(g).wait()
        for f in range(per_part):
            weight = prints_buf[per_part * g + f]
            weights = jnp.concatenate(
                [
                    jnp.concatenate([weight, zero], axis=1),
                    jnp.concatenate([zero, weight], axis=1),
                ],
                axis=0,
            )
            for m in range(0, half * touch, block):
                left = jnp.concatenate(
                    [mixed[m : m + block], mixed[half * touch + m : half * touch + m + block]], axis=1
                )
                value = lax.dot_general(
                    left, weights, (((1,), (1,)), ((), ())), preferred_element_type=F32
                ).astype(BF16)
                for i in range(block // touch):
                    row = pl.multiple_of((per_part * g + f) * touch, touch)
                    spread[m // touch + i, pl.ds(row, touch), :] = value[
                        i * touch : (i + 1) * touch
                    ]

    groups = sems.shape[0]
    group_size = half // groups

    @pl.loop(0, groups)
    def _(i):
        for j in range(group_size):
            z = i * group_size + j
            grad = jnp.dot(counts_turned[...], spread[z], preferred_element_type=F32)
            for g in range(2):
                at = z + g * half
                out_buf[at] = jnp.maximum(
                    base[at] - step_length * grad[:, g * pixels : (g + 1) * pixels], 0.0
                )
        for j in range(group_size):
            for g in range(2):
                at = i * group_size + j + g * half
                pltpu.make_async_copy(out_buf.at[at], out.at[:, at, :], sems.at[i]).start()

    for i in range(groups):
        both = out_buf.at[pl.ds(0, 2 * group_size)]
        pltpu.make_async_copy(both, both, sems.at[i]).wait()


def backward(touch, table, returned, prints, counts_turned, base):
    slices, rows, pixels = base.shape
    codes = prints.shape[0] * touch
    return pl.pallas_call(
        functools.partial(backward_kernel, touch),
        out_shape=jax.ShapeDtypeStruct((rows, slices, pixels), F32),
        in_specs=[SMEM, VMEM, HBM, VMEM, VMEM],
        out_specs=HBM,
        scratch_shapes=[
            pltpu.VMEM((touch, slices, prints.shape[2]), F32),
            pltpu.VMEM((slices * touch, prints.shape[2]), BF16),
            pltpu.VMEM((slices // 2, codes, 2 * pixels), BF16),
            pltpu.VMEM((slices, rows, pixels), F32),
            pltpu.VMEM(prints.shape, BF16),
            pltpu.SemaphoreType.DMA((4,)),
            pltpu.SemaphoreType.DMA((2,)),
        ],
        compiler_params=pltpu.CompilerParams(vmem_limit_bytes=24 << 20),
        name="backward",
    )(table, returned, *in_hbm(prints), counts_turned, base)


def shifted(x, axis, forward_way):
    count = lax.axis_size(axis)
    if forward_way:
        pairs = [(i, i + 1) for i in range(count - 1)]
    else:
        pairs = [(i + 1, i) for i in range(count - 1)]
    return lax.ppermute(x, axis, pairs)


def per_device(volume, footprints, foot_index, ray_block, ray_slot, measured, weights):
    row_count, _, _ = volume.shape
    owners = lax.axis_size("tile")
    owned = measured.shape[0]
    touch = owners // 2
    blocks = ray_block.T
    sent, table, counts, head, tail, first_row, last_row = forward(
        touch, owned, owners, ray_slot, blocks, foot_index.T, volume, footprints
    )
    arrived = lax.all_to_all(sent, "tile", split_axis=0, concat_axis=0, tiled=True)
    before_slice = shifted(tail, "slab", True)
    after_slice = shifted(head, "slab", False)
    counts_turned, picks = tables(owned, owners, row_count, ray_slot, blocks, counts)

    last_edge = jnp.concatenate([last_row, after_slice[row_count - 1 :]], axis=0)
    first_edge = jnp.concatenate([first_row, before_slice[:1]], axis=0)
    before_row = shifted(last_edge, "tile", True)
    after_row = shifted(first_edge, "tile", False)
    arrived, _, _ = lax.optimization_barrier((arrived, first_edge, last_edge))
    answer = residual(arrived, picks, measured, weights)
    returned = lax.all_to_all(answer, "tile", split_axis=0, concat_axis=0, tiled=True)
    halos, _ = lax.optimization_barrier(
        ((before_slice, after_slice, before_row, after_row, first_row), answer)
    )
    base = variation(volume, *halos)
    return backward(touch, table, returned, footprints, counts_turned, base)


def solution(mesh):
    in_specs = (
        P("tile", "slab", None),
        P(),
        P("tile", None),
        P(),
        P(),
        P("tile", "slab", None),
        P("tile", "slab", None),
    )
    out_specs = P("tile", "slab", None)
    return jax.shard_map(
        per_device, mesh=mesh, in_specs=in_specs, out_specs=out_specs, check_vma=False
    )
```

```python
import functools

import jax
import jax.numpy as jnp
from jax import lax
from jax.experimental import pallas as pl
from jax.experimental.pallas import tpu as pltpu
from jax.sharding import PartitionSpec as P


smoothing = 0.04
step_length = 2.0
variation_weight = 1.0
lanes = 128

F32 = jnp.float32
BF16 = jnp.bfloat16
VMEM = pl.BlockSpec(memory_space=pltpu.VMEM)
SMEM = pl.BlockSpec(memory_space=pltpu.SMEM)
HBM = pl.BlockSpec(memory_space=pltpu.HBM)


def in_hbm(*arrays):
    return [pltpu.with_memory_space_constraint(x, pltpu.HBM) for x in arrays]


def iota(shape, dim):
    return lax.broadcasted_iota(jnp.int32, shape, dim)


def forward_kernel(
    touch, owned, ray_slot, blocks, foots, volume, prints,
    sent, table, counts, head, tail, first_row, last_row,
    window, foots_buf, slot_buf, by_slice, prints_buf, grouped, sums, compact, table_buf,
    sent_buf, sent_sem,
    sems, small_sems, table_sem, prints_sem,
):
    row_count, slice_count, _ = volume.shape
    foot_count = prints.shape[0]
    owners = sent.shape[0]
    crossings = blocks.shape[0]

    half = slice_count // 2
    groups = sems.shape[0]
    group_size = half // groups

    position = lax.axis_index("tile")
    offset = position * row_count
    limit = blocks.shape[1] - 2 * lanes
    base = jnp.minimum((offset // lanes) * lanes, limit)
    small = [
        pltpu.make_async_copy(source, target, small_sems.at[i])
        for i, (source, target) in enumerate(
            [
                (blocks.at[:, pl.ds(pl.multiple_of(base, lanes), 2 * lanes)], window),
                (foots, foots_buf),
                (ray_slot, slot_buf),
                (volume.at[0], first_row),
                (volume.at[row_count - 1], last_row),
            ]
        )
    ]
    for copy in small:
        copy.start()
    for z in range(half):
        for z in (z, z + half):
            pltpu.make_async_copy(
                volume.at[:, z, :], by_slice.at[z], sems.at[z % half // group_size]
            ).start()
    prints_copy = pltpu.make_async_copy(prints, prints_buf, prints_sem)
    prints_copy.start()

    for copy in small[:3]:
        copy.wait()
    mine = pltpu.roll(window[...], 2 * lanes - (offset - base), 1)[:, :lanes]
    slot = jnp.zeros_like(mine)
    for b in range(ray_slot.shape[0]):
        slot = jnp.where(mine == b, slot_buf[b], slot)
    valid = iota((crossings, lanes), 1) < row_count
    owner = jnp.where(valid, slot // owned, -1)
    label = iota((owners, lanes), 0)
    present = jnp.zeros((owners, lanes), F32)
    for k in range(crossings):
        present = jnp.where(owner[k : k + 1] == label, 1.0, present)
    present = jnp.broadcast_to(jnp.max(present, axis=1, keepdims=True), (owners, lanes))
    lower = (iota((owners, owners), 1) < iota((owners, owners), 0)).astype(BF16)
    rank = jnp.dot(lower, present.astype(BF16), preferred_element_type=F32)
    column = iota((owners, lanes), 1)
    rank_row = jnp.sum(jnp.where(label < column, present, 0.0), axis=0, keepdims=True)
    present_row = jnp.sum(jnp.where(label == column, present, 0.0), axis=0, keepdims=True)
    rank_row = jnp.where(present_row > 0.5, rank_row, -1.0).astype(jnp.int32)
    match = jnp.where((rank.astype(jnp.int32) == column) & (present > 0.5), label + 1, 0)
    owner_row = jnp.sum(match, axis=0, keepdims=True) - 1
    table_buf[...] = jnp.where(iota(table_buf.shape, 0) == 0, rank_row, owner_row)
    table_copy = pltpu.make_async_copy(table_buf, table, table_sem)
    table_copy.start()

    foots_here = jnp.concatenate(
        [foots_buf[...], jnp.zeros((crossings, lanes - row_count), jnp.int32)], axis=1
    )
    hits, feet = [], []
    rank_id = iota((touch, lanes), 0)
    for k in range(crossings):
        place = jnp.sum(
            jnp.where(owner[k : k + 1] == label, rank, 0.0), axis=0, keepdims=True
        ).astype(jnp.int32)
        hits.append(jnp.where((rank_id == place) & valid[k : k + 1], 1.0, 0.0).astype(BF16))
        feet.append(
            jnp.broadcast_to(foots_here[k : k + 1].astype(F32), (touch, lanes)).astype(BF16)
        )
    none = jnp.zeros((touch, lanes), BF16)
    for f in range(foot_count):
        terms = [jnp.where(foot == f, hit, none) for foot, hit in zip(feet, hits)]
        while len(terms) > 1:
            terms = [x + y for x, y in zip(terms[::2], terms[1::2])]
        counts[f * touch : (f + 1) * touch] = terms[0]

    wide = 16

    @pl.loop(0, groups)
    def _(i):
        both = by_slice.at[pl.ds(0, 2 * group_size)]
        pltpu.make_async_copy(both, both, sems.at[i]).wait()
        for j in range(group_size):
            z = i * group_size + j
            pair = jnp.concatenate([by_slice[z], by_slice[z + half]], axis=1).astype(BF16)
            for first in range(0, foot_count, wide):
                group = jnp.dot(
                    counts[first * touch : (first + wide) * touch, :row_count],
                    pair,
                    preferred_element_type=F32,
                ).astype(BF16)
                for f in range(wide):
                    grouped[first + f, pl.ds(pl.multiple_of(z * touch, touch), touch), :] = group[
                        f * touch : (f + 1) * touch
                    ]

    head[...] = by_slice[0]
    tail[...] = by_slice[slice_count - 1]
    prints_copy.wait()
    block = 256
    zero = jnp.zeros(prints.shape[1:], BF16)
    weights = []
    for f in range(foot_count):
        weight = prints_buf[f]
        weights.append(jnp.concatenate([weight, zero], axis=1))
        weights.append(jnp.concatenate([zero, weight], axis=1))
    weights = jnp.concatenate(weights, axis=0)
    for m in range(0, half * touch, block):
        left = [grouped[f, m : m + block, :] for f in range(foot_count)]
        both = jnp.dot(jnp.concatenate(left, axis=1), weights, preferred_element_type=F32)
        rays = both.shape[1] // 2
        sums[m : m + block] = both[:, :rays]
        sums[half * touch + m : half * touch + m + block] = both[:, rays:]

    compact[...] = jnp.swapaxes(sums[...].reshape(slice_count, touch, -1), 0, 1).astype(BF16)
    for copy in small[3:]:
        copy.wait()
    table_copy.wait()
    for t in range(owners):
        place = table[0, t]
        block = compact[jnp.maximum(place, 0)]
        sent_buf[t] = jnp.where(place >= 0, block, jnp.zeros_like(block))
        if t % 4 == 3:
            span = pl.ds(t - 3, 4)
            pltpu.make_async_copy(sent_buf.at[span], sent.at[span], sent_sem).start()
    pltpu.make_async_copy(sent_buf, sent, sent_sem).wait()


def forward(touch, owned, owners, ray_slot, blocks, foots, volume, prints):
    rows, slices, pixels = volume.shape
    foot_count, _, rays = prints.shape
    return pl.pallas_call(
        functools.partial(forward_kernel, touch, owned),
        out_shape=(
            jax.ShapeDtypeStruct((owners, slices, rays), BF16),
            jax.ShapeDtypeStruct((8, lanes), jnp.int32),
            jax.ShapeDtypeStruct((foot_count * touch, lanes), BF16),
            jax.ShapeDtypeStruct((rows, pixels), F32),
            jax.ShapeDtypeStruct((rows, pixels), F32),
            jax.ShapeDtypeStruct((slices, pixels), F32),
            jax.ShapeDtypeStruct((slices, pixels), F32),
        ),
        in_specs=[HBM] * 5,
        out_specs=(HBM, SMEM) + (VMEM,) * 5,
        scratch_shapes=[
            pltpu.VMEM((blocks.shape[0], 2 * lanes), jnp.int32),
            pltpu.VMEM(foots.shape, jnp.int32),
            pltpu.SMEM(ray_slot.shape, jnp.int32),
            pltpu.VMEM((slices, rows, pixels), F32),
            pltpu.VMEM(prints.shape, BF16),
            pltpu.VMEM((foot_count, slices // 2 * touch, 2 * pixels), BF16),
            pltpu.VMEM((slices * touch, rays), F32),
            pltpu.VMEM((touch, slices, rays), BF16),
            pltpu.VMEM((8, lanes), jnp.int32),
            pltpu.VMEM((owners, slices, rays), BF16),
            pltpu.SemaphoreType.DMA,
            pltpu.SemaphoreType.DMA((4,)),
            pltpu.SemaphoreType.DMA((5,)),
            pltpu.SemaphoreType.DMA,
            pltpu.SemaphoreType.DMA,
        ],
        compiler_params=pltpu.CompilerParams(vmem_limit_bytes=24 << 20),
        name="forward",
    )(*in_hbm(ray_slot, blocks, foots, volume, prints))


def tables_kernel(owned, ray_slot, blocks, counts, counts_turned, picks):
    position = lax.axis_index("tile")
    rows = counts_turned.shape[0]

    counts_turned[...] = counts[...].astype(F32).T[:rows].astype(BF16)

    owners = picks.shape[0]
    width = blocks.shape[1]
    second = jnp.int32(0)
    for b in range(ray_slot.shape[0]):
        second = jnp.where(ray_slot[b] == position * owned + 1, b, second)
    hit = jnp.max(jnp.where(blocks[...] == second, 1.0, 0.0), axis=0, keepdims=True)
    start = iota((owners, width), 0) * rows
    at = iota((owners, width), 1)
    member = ((at >= start) & (at < start + rows)).astype(BF16)
    count = lax.dot_general(
        member,
        jnp.broadcast_to(hit, (lanes, width)).astype(BF16),
        (((1,), (1,)), ((), ())),
        preferred_element_type=F32,
    )
    picks[...] = jnp.where(count > 0.5, 1.0, 0.0)


def tables(owned, owners, rows, ray_slot, blocks, counts):
    return pl.pallas_call(
        functools.partial(tables_kernel, owned),
        out_shape=(
            jax.ShapeDtypeStruct((rows, counts.shape[0]), BF16),
            jax.ShapeDtypeStruct((owners, lanes), F32),
        ),
        in_specs=[SMEM] + [VMEM] * 2,
        out_specs=(VMEM,) * 2,
        compiler_params=pltpu.CompilerParams(vmem_limit_bytes=8 << 20),
        name="tables",
    )(ray_slot, blocks, counts)


def variation_kernel(
    volume, before_slice, after_slice, before_row, after_row, first_row,
    base, by_slice, row_flux, sems,
):
    slices, rows, pixels = base.shape

    groups = sems.shape[0]
    size = slices // groups
    for z in range(slices):
        pltpu.make_async_copy(volume.at[:, z, :], by_slice.at[z], sems.at[z // size]).start()

    def wait_group(i):
        span = by_slice.at[pl.ds(i * size, size)]
        pltpu.make_async_copy(span, span, sems.at[i]).wait()

    position = lax.axis_index("tile")
    layer = lax.axis_index("slab")
    last_position = lax.axis_size("tile") - 1
    last_layer = lax.axis_size("slab") - 1
    lane = iota((1, pixels), 1)
    inner = lane < pixels - 1
    first = lane == 0

    def col_grad(x):
        return jnp.where(inner, pltpu.roll(x, pixels - 1, 1) - x, 0.0)

    def scale(a, b, c):
        return lax.rsqrt(a * a + b * b + c * c + smoothing)

    low = before_row[:slices]
    z_id = iota((slices, 1), 0)
    grad_slices = before_row[1 : slices + 1] - low
    grad_slices = jnp.where((z_id == slices - 1) & (layer == last_layer), 0.0, grad_slices)
    grad_rows = first_row[...] - low
    flux = grad_rows * scale(grad_rows, grad_slices, col_grad(low))
    row_flux[...] = jnp.where(position == 0, 0.0, flux)

    row_id = iota((rows, 1), 0)
    top = row_id == rows - 1
    bottom = row_id == 0
    keep = jnp.where(top & (position == last_position), 0.0, 1.0)

    def fluxes(here, next_slice, beyond, last):
        up = jnp.where(top, beyond, pltpu.roll(here, rows - 1, 0))
        grad_rows = (up - here) * keep
        grad_slices = jnp.where(last, 0.0, next_slice - here)
        grad_cols = col_grad(here)
        inverse = scale(grad_rows, grad_slices, grad_cols)
        return grad_rows * inverse, grad_slices * inverse, grad_cols * inverse

    wait_group(0)
    _, start, _ = fluxes(before_slice[...], by_slice[0], after_row[slices : slices + 1], False)
    start = jnp.where(layer == 0, 0.0, start)

    def one(z, here, next_slice, previous, last):
        flux_rows, flux_slices, flux_cols = fluxes(
            here, next_slice, after_row[pl.ds(z, 1), :], last
        )
        below = jnp.where(bottom, row_flux[pl.ds(z, 1), :], pltpu.roll(flux_rows, 1, 0))
        left = jnp.where(first, 0.0, pltpu.roll(flux_cols, 1, 1))
        variation = (previous - flux_slices) + (below - flux_rows) + (left - flux_cols)
        base[z] = here - (step_length * variation_weight) * variation
        return flux_slices

    def step(z, previous):
        @pl.when((z + 1) % size == 0)
        def _():
            wait_group((z + 1) // size)

        return one(z, by_slice[z], by_slice[z + 1], previous, False)

    final = lax.fori_loop(0, slices - 1, step, start)
    one(slices - 1, by_slice[slices - 1], after_slice[...], final, layer == last_layer)


def variation(volume, *halos):
    rows, slices, pixels = volume.shape
    return pl.pallas_call(
        variation_kernel,
        out_shape=jax.ShapeDtypeStruct((slices, rows, pixels), F32),
        in_specs=[HBM] + [VMEM] * 5,
        out_specs=VMEM,
        scratch_shapes=[
            pltpu.VMEM((slices, rows, pixels), F32),
            pltpu.VMEM((slices, pixels), F32),
            pltpu.SemaphoreType.DMA((8,)),
        ],
        compiler_params=pltpu.CompilerParams(vmem_limit_bytes=8 << 20),
        name="variation",
    )(*in_hbm(volume), *halos)


def residual_kernel(arrived, picks, measured, weights, returned, answer, sem):
    owners = arrived.shape[0]
    sums = [jnp.zeros(measured.shape[1:], F32) for _ in range(2)]
    for j in range(owners):
        part = arrived[j].astype(F32)
        chosen = picks[j : j + 1, :] > 0.5
        sums[0] = sums[0] + jnp.where(chosen, 0.0, part)
        sums[1] = sums[1] + jnp.where(chosen, part, 0.0)
    out = [(weights[i] * (sums[i] - measured[i])).astype(BF16).astype(F32) for i in range(2)]
    for j in range(owners):
        answer[j] = jnp.where(picks[j : j + 1, :] > 0.5, out[1], out[0]).astype(BF16)
        if j % 4 == 3:
            span = pl.ds(j - 3, 4)
            pltpu.make_async_copy(answer.at[span], returned.at[span], sem).start()
    pltpu.make_async_copy(answer, returned, sem).wait()


def residual(arrived, picks, measured, weights):
    return pl.pallas_call(
        residual_kernel,
        out_shape=jax.ShapeDtypeStruct(arrived.shape, BF16),
        in_specs=[VMEM] * 4,
        out_specs=HBM,
        scratch_shapes=[pltpu.VMEM(arrived.shape, BF16), pltpu.SemaphoreType.DMA],
        compiler_params=pltpu.CompilerParams(vmem_limit_bytes=4 << 20),
        name="residual",
    )(arrived, picks, measured, weights)


def backward_kernel(
    touch, table, returned, prints, counts_turned, base,
    out, gathered, mixed, spread, out_buf, prints_buf, sems, prints_sems,
):
    slices, _, pixels = base.shape
    foot_count, _, rays = prints.shape
    parts = prints_sems.shape[0]
    per_part = foot_count // parts

    def prints_copy(g):
        span = pl.ds(g * per_part, per_part)
        return pltpu.make_async_copy(prints.at[span], prints_buf.at[span], prints_sems.at[g])

    for g in range(parts):
        prints_copy(g).start()
    for s in range(touch):
        owner = table[1, s]
        block = returned[jnp.maximum(owner, 0)].astype(F32)
        gathered[s] = jnp.where(owner >= 0, block, 0.0)
    mixed[...] = jnp.swapaxes(gathered[...], 0, 1).reshape(slices * touch, rays).astype(BF16)
    half = slices // 2
    block = 256
    zero = jnp.zeros(prints.shape[1:], BF16)

    @pl.loop(0, parts)
    def _(g):
        prints_copy(g).wait()
        for f in range(per_part):
            weight = prints_buf[per_part * g + f]
            weights = jnp.concatenate(
                [
                    jnp.concatenate([weight, zero], axis=1),
                    jnp.concatenate([zero, weight], axis=1),
                ],
                axis=0,
            )
            for m in range(0, half * touch, block):
                left = jnp.concatenate(
                    [mixed[m : m + block], mixed[half * touch + m : half * touch + m + block]], axis=1
                )
                value = lax.dot_general(
                    left, weights, (((1,), (1,)), ((), ())), preferred_element_type=F32
                ).astype(BF16)
                for i in range(block // touch):
                    row = pl.multiple_of((per_part * g + f) * touch, touch)
                    spread[m // touch + i, pl.ds(row, touch), :] = value[
                        i * touch : (i + 1) * touch
                    ]

    groups = sems.shape[0]
    group_size = half // groups

    @pl.loop(0, groups)
    def _(i):
        for j in range(group_size):
            z = i * group_size + j
            grad = jnp.dot(counts_turned[...], spread[z], preferred_element_type=F32)
            for g in range(2):
                at = z + g * half
                out_buf[at] = jnp.maximum(
                    base[at] - step_length * grad[:, g * pixels : (g + 1) * pixels], 0.0
                )
            if j % 4 == 3:
                for at in [z - 3 + k + g * half for k in range(4) for g in range(2)]:
                    pltpu.make_async_copy(out_buf.at[at], out.at[:, at, :], sems.at[i]).start()

    for i in range(groups):
        both = out_buf.at[pl.ds(0, 2 * group_size)]
        pltpu.make_async_copy(both, both, sems.at[i]).wait()


def backward(touch, table, returned, prints, counts_turned, base):
    slices, rows, pixels = base.shape
    codes = prints.shape[0] * touch
    return pl.pallas_call(
        functools.partial(backward_kernel, touch),
        out_shape=jax.ShapeDtypeStruct((rows, slices, pixels), F32),
        in_specs=[SMEM, VMEM, HBM, VMEM, VMEM],
        out_specs=HBM,
        scratch_shapes=[
            pltpu.VMEM((touch, slices, prints.shape[2]), F32),
            pltpu.VMEM((slices * touch, prints.shape[2]), BF16),
            pltpu.VMEM((slices // 2, codes, 2 * pixels), BF16),
            pltpu.VMEM((slices, rows, pixels), F32),
            pltpu.VMEM(prints.shape, BF16),
            pltpu.SemaphoreType.DMA((4,)),
            pltpu.SemaphoreType.DMA((2,)),
        ],
        compiler_params=pltpu.CompilerParams(vmem_limit_bytes=24 << 20),
        name="backward",
    )(table, returned, *in_hbm(prints), counts_turned, base)


def shifted(x, axis, forward_way):
    count = lax.axis_size(axis)
    if forward_way:
        pairs = [(i, i + 1) for i in range(count - 1)]
    else:
        pairs = [(i + 1, i) for i in range(count - 1)]
    return lax.ppermute(x, axis, pairs)


def per_device(volume, footprints, foot_index, ray_block, ray_slot, measured, weights):
    row_count, _, _ = volume.shape
    owners = lax.axis_size("tile")
    owned = measured.shape[0]
    touch = owners // 2
    blocks = ray_block.T
    sent, table, counts, head, tail, first_row, last_row = forward(
        touch, owned, owners, ray_slot, blocks, foot_index.T, volume, footprints
    )
    arrived = lax.all_to_all(sent, "tile", split_axis=0, concat_axis=0, tiled=True)
    before_slice = shifted(tail, "slab", True)
    after_slice = shifted(head, "slab", False)
    counts_turned, picks = tables(owned, owners, row_count, ray_slot, blocks, counts)

    last_edge = jnp.concatenate([last_row, after_slice[row_count - 1 :]], axis=0)
    first_edge = jnp.concatenate([first_row, before_slice[:1]], axis=0)
    before_row = shifted(last_edge, "tile", True)
    after_row = shifted(first_edge, "tile", False)
    arrived, _, _ = lax.optimization_barrier((arrived, first_edge, last_edge))
    answer = residual(arrived, picks, measured, weights)
    returned = lax.all_to_all(answer, "tile", split_axis=0, concat_axis=0, tiled=True)
    halos, _ = lax.optimization_barrier(
        ((before_slice, after_slice, before_row, after_row, first_row), answer)
    )
    base = variation(volume, *halos)
    return backward(touch, table, returned, footprints, counts_turned, base)


def solution(mesh):
    in_specs = (
        P("tile", "slab", None),
        P(),
        P("tile", None),
        P(),
        P(),
        P("tile", "slab", None),
        P("tile", "slab", None),
    )
    out_specs = P("tile", "slab", None)
    return jax.shard_map(
        per_device, mesh=mesh, in_specs=in_specs, out_specs=out_specs, check_vma=False
    )
```

```python
import functools

import jax
import jax.numpy as jnp
from jax import lax
from jax.experimental import pallas as pl
from jax.experimental.pallas import tpu as pltpu
from jax.sharding import PartitionSpec as P


smoothing = 0.04
step_length = 2.0
variation_weight = 1.0
lanes = 128

F32 = jnp.float32
BF16 = jnp.bfloat16
VMEM = pl.BlockSpec(memory_space=pltpu.VMEM)
SMEM = pl.BlockSpec(memory_space=pltpu.SMEM)
HBM = pl.BlockSpec(memory_space=pltpu.HBM)


def in_hbm(*arrays):
    return [pltpu.with_memory_space_constraint(x, pltpu.HBM) for x in arrays]


def iota(shape, dim):
    return lax.broadcasted_iota(jnp.int32, shape, dim)


def forward_kernel(
    touch, owned, ray_slot, blocks, foots, volume, prints,
    sent, table, counts, head, tail, first_row, last_row,
    window, foots_buf, slot_buf, by_slice, prints_buf, grouped, sums, compact, table_buf,
    sems, small_sems, table_sem, prints_sem,
):
    row_count, slice_count, _ = volume.shape
    foot_count = prints.shape[0]
    owners = sent.shape[0]
    crossings = blocks.shape[0]

    half = slice_count // 2
    groups = sems.shape[0]
    group_size = half // groups

    position = lax.axis_index("tile")
    offset = position * row_count
    limit = blocks.shape[1] - 2 * lanes
    base = jnp.minimum((offset // lanes) * lanes, limit)
    small = [
        pltpu.make_async_copy(source, target, small_sems.at[i])
        for i, (source, target) in enumerate(
            [
                (blocks.at[:, pl.ds(pl.multiple_of(base, lanes), 2 * lanes)], window),
                (foots, foots_buf),
                (ray_slot, slot_buf),
                (volume.at[0], first_row),
                (volume.at[row_count - 1], last_row),
            ]
        )
    ]
    for copy in small:
        copy.start()
    for z in range(half):
        for z in (z, z + half):
            pltpu.make_async_copy(
                volume.at[:, z, :], by_slice.at[z], sems.at[z % half // group_size]
            ).start()
    prints_copy = pltpu.make_async_copy(prints, prints_buf, prints_sem)
    prints_copy.start()

    for copy in small[:3]:
        copy.wait()
    mine = pltpu.roll(window[...], 2 * lanes - (offset - base), 1)[:, :lanes]
    slot = jnp.zeros_like(mine)
    for b in range(ray_slot.shape[0]):
        slot = jnp.where(mine == b, slot_buf[b], slot)
    valid = iota((crossings, lanes), 1) < row_count
    owner = jnp.where(valid, slot // owned, -1)
    label = iota((owners, lanes), 0)
    present = jnp.zeros((owners, lanes), F32)
    for k in range(crossings):
        present = jnp.where(owner[k : k + 1] == label, 1.0, present)
    present = jnp.broadcast_to(jnp.max(present, axis=1, keepdims=True), (owners, lanes))
    lower = (iota((owners, owners), 1) < iota((owners, owners), 0)).astype(BF16)
    rank = jnp.dot(lower, present.astype(BF16), preferred_element_type=F32)
    column = iota((owners, lanes), 1)
    rank_row = jnp.sum(jnp.where(label < column, present, 0.0), axis=0, keepdims=True)
    present_row = jnp.sum(jnp.where(label == column, present, 0.0), axis=0, keepdims=True)
    rank_row = jnp.where(present_row > 0.5, rank_row, -1.0).astype(jnp.int32)
    match = jnp.where((rank.astype(jnp.int32) == column) & (present > 0.5), label + 1, 0)
    owner_row = jnp.sum(match, axis=0, keepdims=True) - 1
    table_buf[...] = jnp.where(iota(table_buf.shape, 0) == 0, rank_row, owner_row)
    table_copy = pltpu.make_async_copy(table_buf, table, table_sem)
    table_copy.start()

    foots_here = jnp.concatenate(
        [foots_buf[...], jnp.zeros((crossings, lanes - row_count), jnp.int32)], axis=1
    )
    hits, feet = [], []
    rank_id = iota((touch, lanes), 0)
    for k in range(crossings):
        place = jnp.sum(
            jnp.where(owner[k : k + 1] == label, rank, 0.0), axis=0, keepdims=True
        ).astype(jnp.int32)
        hits.append(jnp.where((rank_id == place) & valid[k : k + 1], 1.0, 0.0).astype(BF16))
        feet.append(
            jnp.broadcast_to(foots_here[k : k + 1].astype(F32), (touch, lanes)).astype(BF16)
        )
    none = jnp.zeros((touch, lanes), BF16)
    for f in range(foot_count):
        terms = [jnp.where(foot == f, hit, none) for foot, hit in zip(feet, hits)]
        while len(terms) > 1:
            terms = [x + y for x, y in zip(terms[::2], terms[1::2])]
        counts[f * touch : (f + 1) * touch] = terms[0]

    wide = 16

    @pl.loop(0, groups)
    def _(i):
        both = by_slice.at[pl.ds(0, 2 * group_size)]
        pltpu.make_async_copy(both, both, sems.at[i]).wait()
        for j in range(group_size):
            z = i * group_size + j
            pair = jnp.concatenate([by_slice[z], by_slice[z + half]], axis=1).astype(BF16)
            for first in range(0, foot_count, wide):
                group = jnp.dot(
                    counts[first * touch : (first + wide) * touch, :row_count],
                    pair,
                    preferred_element_type=F32,
                ).astype(BF16)
                for f in range(wide):
                    grouped[first + f, pl.ds(pl.multiple_of(z * touch, touch), touch), :] = group[
                        f * touch : (f + 1) * touch
                    ]

    head[...] = by_slice[0]
    tail[...] = by_slice[slice_count - 1]
    prints_copy.wait()
    block = 256
    zero = jnp.zeros(prints.shape[1:], BF16)
    weights = []
    for f in range(foot_count):
        weight = prints_buf[f]
        weights.append(jnp.concatenate([weight, zero], axis=1))
        weights.append(jnp.concatenate([zero, weight], axis=1))
    weights = jnp.concatenate(weights, axis=0)
    for m in range(0, half * touch, block):
        left = [grouped[f, m : m + block, :] for f in range(foot_count)]
        both = jnp.dot(jnp.concatenate(left, axis=1), weights, preferred_element_type=F32)
        rays = both.shape[1] // 2
        sums[m : m + block] = both[:, :rays]
        sums[half * touch + m : half * touch + m + block] = both[:, rays:]

    compact[...] = jnp.swapaxes(sums[...].reshape(slice_count, touch, -1), 0, 1).astype(BF16)
    for copy in small[3:]:
        copy.wait()
    table_copy.wait()
    for t in range(owners):
        place = table[0, t]
        block = compact[jnp.maximum(place, 0)]
        sent[t] = jnp.where(place >= 0, block, jnp.zeros_like(block))


def forward(touch, owned, owners, ray_slot, blocks, foots, volume, prints):
    rows, slices, pixels = volume.shape
    foot_count, _, rays = prints.shape
    return pl.pallas_call(
        functools.partial(forward_kernel, touch, owned),
        out_shape=(
            jax.ShapeDtypeStruct((owners, slices, rays), BF16),
            jax.ShapeDtypeStruct((8, lanes), jnp.int32),
            jax.ShapeDtypeStruct((foot_count * touch, lanes), BF16),
            jax.ShapeDtypeStruct((rows, pixels), F32),
            jax.ShapeDtypeStruct((rows, pixels), F32),
            jax.ShapeDtypeStruct((slices, pixels), F32),
            jax.ShapeDtypeStruct((slices, pixels), F32),
        ),
        in_specs=[HBM] * 5,
        out_specs=(VMEM, SMEM) + (VMEM,) * 5,
        scratch_shapes=[
            pltpu.VMEM((blocks.shape[0], 2 * lanes), jnp.int32),
            pltpu.VMEM(foots.shape, jnp.int32),
            pltpu.SMEM(ray_slot.shape, jnp.int32),
            pltpu.VMEM((slices, rows, pixels), F32),
            pltpu.VMEM(prints.shape, BF16),
            pltpu.VMEM((foot_count, slices // 2 * touch, 2 * pixels), BF16),
            pltpu.VMEM((slices * touch, rays), F32),
            pltpu.VMEM((touch, slices, rays), BF16),
            pltpu.VMEM((8, lanes), jnp.int32),
            pltpu.SemaphoreType.DMA((4,)),
            pltpu.SemaphoreType.DMA((5,)),
            pltpu.SemaphoreType.DMA,
            pltpu.SemaphoreType.DMA,
        ],
        compiler_params=pltpu.CompilerParams(vmem_limit_bytes=24 << 20),
        name="forward",
    )(*in_hbm(ray_slot, blocks, foots, volume, prints))


def tables_kernel(owned, ray_slot, blocks, counts, counts_turned, picks):
    position = lax.axis_index("tile")
    rows = counts_turned.shape[0]

    counts_turned[...] = counts[...].astype(F32).T[:rows].astype(BF16)

    owners = picks.shape[0]
    width = blocks.shape[1]
    second = jnp.int32(0)
    for b in range(ray_slot.shape[0]):
        second = jnp.where(ray_slot[b] == position * owned + 1, b, second)
    hit = jnp.max(jnp.where(blocks[...] == second, 1.0, 0.0), axis=0, keepdims=True)
    start = iota((owners, width), 0) * rows
    at = iota((owners, width), 1)
    member = ((at >= start) & (at < start + rows)).astype(BF16)
    count = lax.dot_general(
        member,
        jnp.broadcast_to(hit, (lanes, width)).astype(BF16),
        (((1,), (1,)), ((), ())),
        preferred_element_type=F32,
    )
    picks[...] = jnp.where(count > 0.5, 1.0, 0.0)


def tables(owned, owners, rows, ray_slot, blocks, counts):
    return pl.pallas_call(
        functools.partial(tables_kernel, owned),
        out_shape=(
            jax.ShapeDtypeStruct((rows, counts.shape[0]), BF16),
            jax.ShapeDtypeStruct((owners, lanes), F32),
        ),
        in_specs=[SMEM] + [VMEM] * 2,
        out_specs=(VMEM,) * 2,
        compiler_params=pltpu.CompilerParams(vmem_limit_bytes=8 << 20),
        name="tables",
    )(ray_slot, blocks, counts)


def variation_kernel(
    volume, before_slice, after_slice, before_row, after_row, first_row,
    base, by_slice, row_flux, sems,
):
    slices, rows, pixels = base.shape

    groups = sems.shape[0]
    size = slices // groups
    for z in range(slices):
        pltpu.make_async_copy(volume.at[:, z, :], by_slice.at[z], sems.at[z // size]).start()

    def wait_group(i):
        span = by_slice.at[pl.ds(i * size, size)]
        pltpu.make_async_copy(span, span, sems.at[i]).wait()

    position = lax.axis_index("tile")
    layer = lax.axis_index("slab")
    last_position = lax.axis_size("tile") - 1
    last_layer = lax.axis_size("slab") - 1
    lane = iota((1, pixels), 1)
    inner = lane < pixels - 1
    first = lane == 0

    def col_grad(x):
        return jnp.where(inner, pltpu.roll(x, pixels - 1, 1) - x, 0.0)

    def scale(a, b, c):
        return lax.rsqrt(a * a + b * b + c * c + smoothing)

    low = before_row[:slices]
    z_id = iota((slices, 1), 0)
    grad_slices = before_row[1 : slices + 1] - low
    grad_slices = jnp.where((z_id == slices - 1) & (layer == last_layer), 0.0, grad_slices)
    grad_rows = first_row[...] - low
    flux = grad_rows * scale(grad_rows, grad_slices, col_grad(low))
    row_flux[...] = jnp.where(position == 0, 0.0, flux)

    row_id = iota((rows, 1), 0)
    top = row_id == rows - 1
    bottom = row_id == 0
    keep = jnp.where(top & (position == last_position), 0.0, 1.0)

    def fluxes(here, next_slice, beyond, last):
        up = jnp.where(top, beyond, pltpu.roll(here, rows - 1, 0))
        grad_rows = (up - here) * keep
        grad_slices = jnp.where(last, 0.0, next_slice - here)
        grad_cols = col_grad(here)
        inverse = scale(grad_rows, grad_slices, grad_cols)
        return grad_rows * inverse, grad_slices * inverse, grad_cols * inverse

    wait_group(0)
    _, start, _ = fluxes(before_slice[...], by_slice[0], after_row[slices : slices + 1], False)
    start = jnp.where(layer == 0, 0.0, start)

    def one(z, here, next_slice, previous, last):
        flux_rows, flux_slices, flux_cols = fluxes(
            here, next_slice, after_row[pl.ds(z, 1), :], last
        )
        below = jnp.where(bottom, row_flux[pl.ds(z, 1), :], pltpu.roll(flux_rows, 1, 0))
        left = jnp.where(first, 0.0, pltpu.roll(flux_cols, 1, 1))
        variation = (previous - flux_slices) + (below - flux_rows) + (left - flux_cols)
        base[z] = here - (step_length * variation_weight) * variation
        return flux_slices

    def step(z, previous):
        @pl.when((z + 1) % size == 0)
        def _():
            wait_group((z + 1) // size)

        return one(z, by_slice[z], by_slice[z + 1], previous, False)

    final = lax.fori_loop(0, slices - 1, step, start)
    one(slices - 1, by_slice[slices - 1], after_slice[...], final, layer == last_layer)


def variation(volume, *halos):
    rows, slices, pixels = volume.shape
    return pl.pallas_call(
        variation_kernel,
        out_shape=jax.ShapeDtypeStruct((slices, rows, pixels), F32),
        in_specs=[HBM] + [VMEM] * 5,
        out_specs=VMEM,
        scratch_shapes=[
            pltpu.VMEM((slices, rows, pixels), F32),
            pltpu.VMEM((slices, pixels), F32),
            pltpu.SemaphoreType.DMA((8,)),
        ],
        compiler_params=pltpu.CompilerParams(vmem_limit_bytes=8 << 20),
        name="variation",
    )(*in_hbm(volume), *halos)


def residual_kernel(arrived, picks, measured, weights, returned, answer, sem):
    owners = arrived.shape[0]
    sums = [jnp.zeros(measured.shape[1:], F32) for _ in range(2)]
    for j in range(owners):
        part = arrived[j].astype(F32)
        chosen = picks[j : j + 1, :] > 0.5
        sums[0] = sums[0] + jnp.where(chosen, 0.0, part)
        sums[1] = sums[1] + jnp.where(chosen, part, 0.0)
    out = [(weights[i] * (sums[i] - measured[i])).astype(BF16).astype(F32) for i in range(2)]
    for j in range(owners):
        answer[j] = jnp.where(picks[j : j + 1, :] > 0.5, out[1], out[0]).astype(BF16)
        if j % 4 == 3:
            span = pl.ds(j - 3, 4)
            pltpu.make_async_copy(answer.at[span], returned.at[span], sem).start()
    pltpu.make_async_copy(answer, returned, sem).wait()


def residual(arrived, picks, measured, weights):
    return pl.pallas_call(
        residual_kernel,
        out_shape=jax.ShapeDtypeStruct(arrived.shape, BF16),
        in_specs=[VMEM] * 4,
        out_specs=HBM,
        scratch_shapes=[pltpu.VMEM(arrived.shape, BF16), pltpu.SemaphoreType.DMA],
        compiler_params=pltpu.CompilerParams(vmem_limit_bytes=4 << 20),
        name="residual",
    )(arrived, picks, measured, weights)


def backward_kernel(
    touch, table, returned, prints, counts_turned, base,
    out, returned_buf, gathered, mixed, spread, out_buf, prints_buf, sems, prints_sems, returned_sem,
):
    slices, _, pixels = base.shape
    foot_count, _, rays = prints.shape
    parts = prints_sems.shape[0]
    per_part = foot_count // parts

    def prints_copy(g):
        span = pl.ds(g * per_part, per_part)
        return pltpu.make_async_copy(prints.at[span], prints_buf.at[span], prints_sems.at[g])

    returned_copy = pltpu.make_async_copy(returned, returned_buf, returned_sem)
    returned_copy.start()
    for g in range(parts):
        prints_copy(g).start()
    returned_copy.wait()
    for s in range(touch):
        owner = table[1, s]
        block = returned_buf[jnp.maximum(owner, 0)].astype(F32)
        gathered[s] = jnp.where(owner >= 0, block, 0.0)
    mixed[...] = jnp.swapaxes(gathered[...], 0, 1).reshape(slices * touch, rays).astype(BF16)
    half = slices // 2
    block = 256
    zero = jnp.zeros(prints.shape[1:], BF16)

    @pl.loop(0, parts)
    def _(g):
        prints_copy(g).wait()
        for f in range(per_part):
            weight = prints_buf[per_part * g + f]
            weights = jnp.concatenate(
                [
                    jnp.concatenate([weight, zero], axis=1),
                    jnp.concatenate([zero, weight], axis=1),
                ],
                axis=0,
            )
            for m in range(0, half * touch, block):
                left = jnp.concatenate(
                    [mixed[m : m + block], mixed[half * touch + m : half * touch + m + block]], axis=1
                )
                value = lax.dot_general(
                    left, weights, (((1,), (1,)), ((), ())), preferred_element_type=F32
                ).astype(BF16)
                for i in range(block // touch):
                    row = pl.multiple_of((per_part * g + f) * touch, touch)
                    spread[m // touch + i, pl.ds(row, touch), :] = value[
                        i * touch : (i + 1) * touch
                    ]

    groups = sems.shape[0]
    group_size = half // groups

    @pl.loop(0, groups)
    def _(i):
        for j in range(group_size):
            z = i * group_size + j
            grad = jnp.dot(counts_turned[...], spread[z], preferred_element_type=F32)
            for g in range(2):
                at = z + g * half
                out_buf[at] = jnp.maximum(
                    base[at] - step_length * grad[:, g * pixels : (g + 1) * pixels], 0.0
                )
            if j % 4 == 3:
                for at in [z - 3 + k + g * half for k in range(4) for g in range(2)]:
                    pltpu.make_async_copy(out_buf.at[at], out.at[:, at, :], sems.at[i]).start()

    for i in range(groups):
        both = out_buf.at[pl.ds(0, 2 * group_size)]
        pltpu.make_async_copy(both, both, sems.at[i]).wait()


def backward(touch, table, returned, prints, counts_turned, base):
    slices, rows, pixels = base.shape
    codes = prints.shape[0] * touch
    return pl.pallas_call(
        functools.partial(backward_kernel, touch),
        out_shape=jax.ShapeDtypeStruct((rows, slices, pixels), F32),
        in_specs=[SMEM, HBM, HBM, VMEM, VMEM],
        out_specs=HBM,
        scratch_shapes=[
            pltpu.VMEM(returned.shape, BF16),
            pltpu.VMEM((touch, slices, prints.shape[2]), F32),
            pltpu.VMEM((slices * touch, prints.shape[2]), BF16),
            pltpu.VMEM((slices // 2, codes, 2 * pixels), BF16),
            pltpu.VMEM((slices, rows, pixels), F32),
            pltpu.VMEM(prints.shape, BF16),
            pltpu.SemaphoreType.DMA((4,)),
            pltpu.SemaphoreType.DMA((2,)),
            pltpu.SemaphoreType.DMA,
        ],
        compiler_params=pltpu.CompilerParams(vmem_limit_bytes=24 << 20),
        name="backward",
    )(table, *in_hbm(returned, prints), counts_turned, base)


def shifted(x, axis, forward_way):
    count = lax.axis_size(axis)
    if forward_way:
        pairs = [(i, i + 1) for i in range(count - 1)]
    else:
        pairs = [(i + 1, i) for i in range(count - 1)]
    return lax.ppermute(x, axis, pairs)


def per_device(volume, footprints, foot_index, ray_block, ray_slot, measured, weights):
    row_count, _, _ = volume.shape
    owners = lax.axis_size("tile")
    owned = measured.shape[0]
    touch = owners // 2
    blocks = ray_block.T
    sent, table, counts, head, tail, first_row, last_row = forward(
        touch, owned, owners, ray_slot, blocks, foot_index.T, volume, footprints
    )
    arrived = lax.all_to_all(sent, "tile", split_axis=0, concat_axis=0, tiled=True)
    before_slice = shifted(tail, "slab", True)
    after_slice = shifted(head, "slab", False)
    counts_turned, picks = tables(owned, owners, row_count, ray_slot, blocks, counts)

    last_edge = jnp.concatenate([last_row, after_slice[row_count - 1 :]], axis=0)
    first_edge = jnp.concatenate([first_row, before_slice[:1]], axis=0)
    before_row = shifted(last_edge, "tile", True)
    after_row = shifted(first_edge, "tile", False)
    arrived, _, _ = lax.optimization_barrier((arrived, first_edge, last_edge))
    answer = residual(arrived, picks, measured, weights)
    returned = lax.all_to_all(answer, "tile", split_axis=0, concat_axis=0, tiled=True)
    halos, _ = lax.optimization_barrier(
        ((before_slice, after_slice, before_row, after_row, first_row), answer)
    )
    base = variation(volume, *halos)
    return backward(touch, table, returned, footprints, counts_turned, base)


def solution(mesh):
    in_specs = (
        P("tile", "slab", None),
        P(),
        P("tile", None),
        P(),
        P(),
        P("tile", "slab", None),
        P("tile", "slab", None),
    )
    out_specs = P("tile", "slab", None)
    return jax.shard_map(
        per_device, mesh=mesh, in_specs=in_specs, out_specs=out_specs, check_vma=False
    )
```

```python
import functools

import jax
import jax.numpy as jnp
from jax import lax
from jax.experimental import pallas as pl
from jax.experimental.pallas import tpu as pltpu
from jax.sharding import PartitionSpec as P


smoothing = 0.04
step_length = 2.0
variation_weight = 1.0
lanes = 128

F32 = jnp.float32
BF16 = jnp.bfloat16
VMEM = pl.BlockSpec(memory_space=pltpu.VMEM)
SMEM = pl.BlockSpec(memory_space=pltpu.SMEM)
HBM = pl.BlockSpec(memory_space=pltpu.HBM)


def in_hbm(*arrays):
    return [pltpu.with_memory_space_constraint(x, pltpu.HBM) for x in arrays]


def iota(shape, dim):
    return lax.broadcasted_iota(jnp.int32, shape, dim)


def forward_kernel(
    touch, owned, ray_slot, blocks, foots, volume, prints,
    sent, table, counts, head, tail, first_row, last_row,
    window, foots_buf, slot_buf, by_slice, prints_buf, grouped, sums, compact, table_buf,
    sems, small_sems, table_sem, prints_sem,
):
    row_count, slice_count, _ = volume.shape
    foot_count = prints.shape[0]
    owners = sent.shape[0]
    crossings = blocks.shape[0]

    half = slice_count // 2
    groups = sems.shape[0]
    group_size = half // groups

    position = lax.axis_index("tile")
    offset = position * row_count
    limit = blocks.shape[1] - 2 * lanes
    base = jnp.minimum((offset // lanes) * lanes, limit)
    small = [
        pltpu.make_async_copy(source, target, small_sems.at[i])
        for i, (source, target) in enumerate(
            [
                (blocks.at[:, pl.ds(pl.multiple_of(base, lanes), 2 * lanes)], window),
                (foots, foots_buf),
                (ray_slot, slot_buf),
                (volume.at[0], first_row),
                (volume.at[row_count - 1], last_row),
            ]
        )
    ]
    for copy in small:
        copy.start()
    for z in range(half):
        for z in (z, z + half):
            pltpu.make_async_copy(
                volume.at[:, z, :], by_slice.at[z], sems.at[z % half // group_size]
            ).start()
    prints_copy = pltpu.make_async_copy(prints, prints_buf, prints_sem)
    prints_copy.start()

    for copy in small[:3]:
        copy.wait()
    mine = pltpu.roll(window[...], 2 * lanes - (offset - base), 1)[:, :lanes]
    slot = jnp.zeros_like(mine)
    for b in range(ray_slot.shape[0]):
        slot = jnp.where(mine == b, slot_buf[b], slot)
    valid = iota((crossings, lanes), 1) < row_count
    owner = jnp.where(valid, slot // owned, -1)
    label = iota((owners, lanes), 0)
    present = jnp.zeros((owners, lanes), F32)
    for k in range(crossings):
        present = jnp.where(owner[k : k + 1] == label, 1.0, present)
    present = jnp.broadcast_to(jnp.max(present, axis=1, keepdims=True), (owners, lanes))
    lower = (iota((owners, owners), 1) < iota((owners, owners), 0)).astype(BF16)
    rank = jnp.dot(lower, present.astype(BF16), preferred_element_type=F32)
    column = iota((owners, lanes), 1)
    rank_row = jnp.sum(jnp.where(label < column, present, 0.0), axis=0, keepdims=True)
    present_row = jnp.sum(jnp.where(label == column, present, 0.0), axis=0, keepdims=True)
    rank_row = jnp.where(present_row > 0.5, rank_row, -1.0).astype(jnp.int32)
    match = jnp.where((rank.astype(jnp.int32) == column) & (present > 0.5), label + 1, 0)
    owner_row = jnp.sum(match, axis=0, keepdims=True) - 1
    table_buf[...] = jnp.where(iota(table_buf.shape, 0) == 0, rank_row, owner_row)
    table_copy = pltpu.make_async_copy(table_buf, table, table_sem)
    table_copy.start()

    foots_here = jnp.concatenate(
        [foots_buf[...], jnp.zeros((crossings, lanes - row_count), jnp.int32)], axis=1
    )
    hits, feet = [], []
    rank_id = iota((touch, lanes), 0)
    for k in range(crossings):
        place = jnp.sum(
            jnp.where(owner[k : k + 1] == label, rank, 0.0), axis=0, keepdims=True
        ).astype(jnp.int32)
        hits.append(jnp.where((rank_id == place) & valid[k : k + 1], 1.0, 0.0).astype(BF16))
        feet.append(
            jnp.broadcast_to(foots_here[k : k + 1].astype(F32), (touch, lanes)).astype(BF16)
        )
    none = jnp.zeros((touch, lanes), BF16)
    for f in range(foot_count):
        terms = [jnp.where(foot == f, hit, none) for foot, hit in zip(feet, hits)]
        while len(terms) > 1:
            terms = [x + y for x, y in zip(terms[::2], terms[1::2])]
        counts[f * touch : (f + 1) * touch] = terms[0]

    wide = 32

    @pl.loop(0, groups)
    def _(i):
        both = by_slice.at[pl.ds(0, 2 * group_size)]
        pltpu.make_async_copy(both, both, sems.at[i]).wait()
        for j in range(group_size):
            z = i * group_size + j
            pair = jnp.concatenate([by_slice[z], by_slice[z + half]], axis=1).astype(BF16)
            for first in range(0, foot_count, wide):
                group = jnp.dot(
                    counts[first * touch : (first + wide) * touch, :row_count],
                    pair,
                    preferred_element_type=F32,
                ).astype(BF16)
                for f in range(wide):
                    grouped[first + f, pl.ds(pl.multiple_of(z * touch, touch), touch), :] = group[
                        f * touch : (f + 1) * touch
                    ]

    head[...] = by_slice[0]
    tail[...] = by_slice[slice_count - 1]
    prints_copy.wait()
    block = 256
    zero = jnp.zeros(prints.shape[1:], BF16)
    weights = []
    for f in range(foot_count):
        weight = prints_buf[f]
        weights.append(jnp.concatenate([weight, zero], axis=1))
        weights.append(jnp.concatenate([zero, weight], axis=1))
    weights = jnp.concatenate(weights, axis=0)
    for m in range(0, half * touch, block):
        left = [grouped[f, m : m + block, :] for f in range(foot_count)]
        both = jnp.dot(jnp.concatenate(left, axis=1), weights, preferred_element_type=F32)
        rays = both.shape[1] // 2
        sums[m : m + block] = both[:, :rays]
        sums[half * touch + m : half * touch + m + block] = both[:, rays:]

    compact[touch] = jnp.zeros(compact.shape[1:], BF16)
    compact[:touch] = jnp.swapaxes(sums[...].reshape(slice_count, touch, -1), 0, 1).astype(BF16)
    for copy in small[3:]:
        copy.wait()
    table_copy.wait()
    for t in range(owners):
        place = table[0, t]
        sent[t] = compact[jnp.where(place >= 0, place, touch)]


def forward(touch, owned, owners, ray_slot, blocks, foots, volume, prints):
    rows, slices, pixels = volume.shape
    foot_count, _, rays = prints.shape
    return pl.pallas_call(
        functools.partial(forward_kernel, touch, owned),
        out_shape=(
            jax.ShapeDtypeStruct((owners, slices, rays), BF16),
            jax.ShapeDtypeStruct((8, lanes), jnp.int32),
            jax.ShapeDtypeStruct((foot_count * touch, lanes), BF16),
            jax.ShapeDtypeStruct((rows, pixels), F32),
            jax.ShapeDtypeStruct((rows, pixels), F32),
            jax.ShapeDtypeStruct((slices, pixels), F32),
            jax.ShapeDtypeStruct((slices, pixels), F32),
        ),
        in_specs=[HBM] * 5,
        out_specs=(VMEM, SMEM) + (VMEM,) * 5,
        scratch_shapes=[
            pltpu.VMEM((blocks.shape[0], 2 * lanes), jnp.int32),
            pltpu.VMEM(foots.shape, jnp.int32),
            pltpu.SMEM(ray_slot.shape, jnp.int32),
            pltpu.VMEM((slices, rows, pixels), F32),
            pltpu.VMEM(prints.shape, BF16),
            pltpu.VMEM((foot_count, slices // 2 * touch, 2 * pixels), BF16),
            pltpu.VMEM((slices * touch, rays), F32),
            pltpu.VMEM((touch + 1, slices, rays), BF16),
            pltpu.VMEM((8, lanes), jnp.int32),
            pltpu.SemaphoreType.DMA((4,)),
            pltpu.SemaphoreType.DMA((5,)),
            pltpu.SemaphoreType.DMA,
            pltpu.SemaphoreType.DMA,
        ],
        compiler_params=pltpu.CompilerParams(vmem_limit_bytes=24 << 20),
        name="forward",
    )(*in_hbm(ray_slot, blocks, foots, volume, prints))


def tables_kernel(owned, ray_slot, blocks, counts, counts_turned, picks):
    position = lax.axis_index("tile")
    rows = counts_turned.shape[0]

    counts_turned[...] = counts[...].astype(F32).T[:rows].astype(BF16)

    owners = picks.shape[0]
    width = blocks.shape[1]
    second = jnp.int32(0)
    for b in range(ray_slot.shape[0]):
        second = jnp.where(ray_slot[b] == position * owned + 1, b, second)
    hit = jnp.max(jnp.where(blocks[...] == second, 1.0, 0.0), axis=0, keepdims=True)
    start = iota((owners, width), 0) * rows
    at = iota((owners, width), 1)
    member = ((at >= start) & (at < start + rows)).astype(BF16)
    count = lax.dot_general(
        member,
        jnp.broadcast_to(hit, (lanes, width)).astype(BF16),
        (((1,), (1,)), ((), ())),
        preferred_element_type=F32,
    )
    picks[...] = jnp.where(count > 0.5, 1.0, 0.0)


def tables(owned, owners, rows, ray_slot, blocks, counts):
    return pl.pallas_call(
        functools.partial(tables_kernel, owned),
        out_shape=(
            jax.ShapeDtypeStruct((rows, counts.shape[0]), BF16),
            jax.ShapeDtypeStruct((owners, lanes), F32),
        ),
        in_specs=[SMEM] + [VMEM] * 2,
        out_specs=(VMEM,) * 2,
        compiler_params=pltpu.CompilerParams(vmem_limit_bytes=8 << 20),
        name="tables",
    )(ray_slot, blocks, counts)


def variation_kernel(
    volume, before_slice, after_slice, before_row, after_row, first_row,
    base, by_slice, row_flux, sems,
):
    slices, rows, pixels = base.shape

    groups = sems.shape[0]
    size = slices // groups
    for z in range(slices):
        pltpu.make_async_copy(volume.at[:, z, :], by_slice.at[z], sems.at[z // size]).start()

    def wait_group(i):
        span = by_slice.at[pl.ds(i * size, size)]
        pltpu.make_async_copy(span, span, sems.at[i]).wait()

    position = lax.axis_index("tile")
    layer = lax.axis_index("slab")
    last_position = lax.axis_size("tile") - 1
    last_layer = lax.axis_size("slab") - 1
    lane = iota((1, pixels), 1)
    inner = lane < pixels - 1
    first = lane == 0

    def col_grad(x):
        return jnp.where(inner, pltpu.roll(x, pixels - 1, 1) - x, 0.0)

    def scale(a, b, c):
        return lax.rsqrt(a * a + b * b + c * c + smoothing)

    low = before_row[:slices]
    z_id = iota((slices, 1), 0)
    grad_slices = before_row[1 : slices + 1] - low
    grad_slices = jnp.where((z_id == slices - 1) & (layer == last_layer), 0.0, grad_slices)
    grad_rows = first_row[...] - low
    flux = grad_rows * scale(grad_rows, grad_slices, col_grad(low))
    row_flux[...] = jnp.where(position == 0, 0.0, flux)

    row_id = iota((rows, 1), 0)
    top = row_id == rows - 1
    bottom = row_id == 0
    keep = jnp.where(top & (position == last_position), 0.0, 1.0)

    def fluxes(here, next_slice, beyond, last):
        up = jnp.where(top, beyond, pltpu.roll(here, rows - 1, 0))
        grad_rows = (up - here) * keep
        grad_slices = jnp.where(last, 0.0, next_slice - here)
        grad_cols = col_grad(here)
        inverse = scale(grad_rows, grad_slices, grad_cols)
        return grad_rows * inverse, grad_slices * inverse, grad_cols * inverse

    wait_group(0)
    _, start, _ = fluxes(before_slice[...], by_slice[0], after_row[slices : slices + 1], False)
    start = jnp.where(layer == 0, 0.0, start)

    def one(z, here, next_slice, previous, last):
        flux_rows, flux_slices, flux_cols = fluxes(
            here, next_slice, after_row[pl.ds(z, 1), :], last
        )
        below = jnp.where(bottom, row_flux[pl.ds(z, 1), :], pltpu.roll(flux_rows, 1, 0))
        left = jnp.where(first, 0.0, pltpu.roll(flux_cols, 1, 1))
        variation = (previous - flux_slices) + (below - flux_rows) + (left - flux_cols)
        base[z] = here - (step_length * variation_weight) * variation
        return flux_slices

    def step(z, previous):
        @pl.when((z + 1) % size == 0)
        def _():
            wait_group((z + 1) // size)

        return one(z, by_slice[z], by_slice[z + 1], previous, False)

    final = lax.fori_loop(0, slices - 1, step, start)
    one(slices - 1, by_slice[slices - 1], after_slice[...], final, layer == last_layer)


def variation(volume, *halos):
    rows, slices, pixels = volume.shape
    return pl.pallas_call(
        variation_kernel,
        out_shape=jax.ShapeDtypeStruct((slices, rows, pixels), F32),
        in_specs=[HBM] + [VMEM] * 5,
        out_specs=VMEM,
        scratch_shapes=[
            pltpu.VMEM((slices, rows, pixels), F32),
            pltpu.VMEM((slices, pixels), F32),
            pltpu.SemaphoreType.DMA((8,)),
        ],
        compiler_params=pltpu.CompilerParams(vmem_limit_bytes=8 << 20),
        name="variation",
    )(*in_hbm(volume), *halos)


def residual_kernel(arrived, picks, measured, weights, returned, answer, sem):
    owners = arrived.shape[0]
    sums = [jnp.zeros(measured.shape[1:], F32) for _ in range(2)]
    for j in range(owners):
        part = arrived[j].astype(F32)
        chosen = picks[j : j + 1, :] > 0.5
        sums[0] = sums[0] + jnp.where(chosen, 0.0, part)
        sums[1] = sums[1] + jnp.where(chosen, part, 0.0)
    out = [(weights[i] * (sums[i] - measured[i])).astype(BF16).astype(F32) for i in range(2)]
    for j in range(owners):
        answer[j] = jnp.where(picks[j : j + 1, :] > 0.5, out[1], out[0]).astype(BF16)
        if j % 4 == 3:
            span = pl.ds(j - 3, 4)
            pltpu.make_async_copy(answer.at[span], returned.at[span], sem).start()
    pltpu.make_async_copy(answer, returned, sem).wait()


def residual(arrived, picks, measured, weights):
    return pl.pallas_call(
        residual_kernel,
        out_shape=jax.ShapeDtypeStruct(arrived.shape, BF16),
        in_specs=[VMEM] * 4,
        out_specs=HBM,
        scratch_shapes=[pltpu.VMEM(arrived.shape, BF16), pltpu.SemaphoreType.DMA],
        compiler_params=pltpu.CompilerParams(vmem_limit_bytes=4 << 20),
        name="residual",
    )(arrived, picks, measured, weights)


def backward_kernel(
    touch, table, returned, prints, counts_turned, base,
    out, returned_buf, gathered, mixed, spread, out_buf, prints_buf, sems, prints_sems, returned_sem,
):
    slices, _, pixels = base.shape
    foot_count, _, rays = prints.shape
    parts = prints_sems.shape[0]
    per_part = foot_count // parts

    def prints_copy(g):
        span = pl.ds(g * per_part, per_part)
        return pltpu.make_async_copy(prints.at[span], prints_buf.at[span], prints_sems.at[g])

    returned_copy = pltpu.make_async_copy(returned, returned_buf, returned_sem)
    returned_copy.start()
    for g in range(parts):
        prints_copy(g).start()
    returned_copy.wait()
    for s in range(touch):
        owner = table[1, s]
        block = returned_buf[jnp.maximum(owner, 0)].astype(F32)
        gathered[s] = jnp.where(owner >= 0, block, 0.0)
    mixed[...] = jnp.swapaxes(gathered[...], 0, 1).reshape(slices * touch, rays).astype(BF16)
    half = slices // 2
    block = 256
    zero = jnp.zeros(prints.shape[1:], BF16)

    @pl.loop(0, parts)
    def _(g):
        prints_copy(g).wait()
        for f in range(per_part):
            weight = prints_buf[per_part * g + f]
            weights = jnp.concatenate(
                [
                    jnp.concatenate([weight, zero], axis=1),
                    jnp.concatenate([zero, weight], axis=1),
                ],
                axis=0,
            )
            for m in range(0, half * touch, block):
                left = jnp.concatenate(
                    [mixed[m : m + block], mixed[half * touch + m : half * touch + m + block]], axis=1
                )
                value = lax.dot_general(
                    left, weights, (((1,), (1,)), ((), ())), preferred_element_type=F32
                ).astype(BF16)
                for i in range(block // touch):
                    row = pl.multiple_of((per_part * g + f) * touch, touch)
                    spread[m // touch + i, pl.ds(row, touch), :] = value[
                        i * touch : (i + 1) * touch
                    ]

    groups = sems.shape[0]
    group_size = half // groups

    @pl.loop(0, groups)
    def _(i):
        for j in range(group_size):
            z = i * group_size + j
            grad = jnp.dot(counts_turned[...], spread[z], preferred_element_type=F32)
            for g in range(2):
                at = z + g * half
                out_buf[at] = jnp.maximum(
                    base[at] - step_length * grad[:, g * pixels : (g + 1) * pixels], 0.0
                )
            if j % 4 == 3:
                for at in [z - 3 + k + g * half for k in range(4) for g in range(2)]:
                    pltpu.make_async_copy(out_buf.at[at], out.at[:, at, :], sems.at[i]).start()

    for i in range(groups):
        both = out_buf.at[pl.ds(0, 2 * group_size)]
        pltpu.make_async_copy(both, both, sems.at[i]).wait()


def backward(touch, table, returned, prints, counts_turned, base):
    slices, rows, pixels = base.shape
    codes = prints.shape[0] * touch
    return pl.pallas_call(
        functools.partial(backward_kernel, touch),
        out_shape=jax.ShapeDtypeStruct((rows, slices, pixels), F32),
        in_specs=[SMEM, HBM, HBM, VMEM, VMEM],
        out_specs=HBM,
        scratch_shapes=[
            pltpu.VMEM(returned.shape, BF16),
            pltpu.VMEM((touch, slices, prints.shape[2]), F32),
            pltpu.VMEM((slices * touch, prints.shape[2]), BF16),
            pltpu.VMEM((slices // 2, codes, 2 * pixels), BF16),
            pltpu.VMEM((slices, rows, pixels), F32),
            pltpu.VMEM(prints.shape, BF16),
            pltpu.SemaphoreType.DMA((2,)),
            pltpu.SemaphoreType.DMA((2,)),
            pltpu.SemaphoreType.DMA,
        ],
        compiler_params=pltpu.CompilerParams(vmem_limit_bytes=24 << 20),
        name="backward",
    )(table, *in_hbm(returned, prints), counts_turned, base)


def shifted(x, axis, forward_way):
    count = lax.axis_size(axis)
    if forward_way:
        pairs = [(i, i + 1) for i in range(count - 1)]
    else:
        pairs = [(i + 1, i) for i in range(count - 1)]
    return lax.ppermute(x, axis, pairs)


def per_device(volume, footprints, foot_index, ray_block, ray_slot, measured, weights):
    row_count, _, _ = volume.shape
    owners = lax.axis_size("tile")
    owned = measured.shape[0]
    touch = owners // 2
    blocks = ray_block.T
    sent, table, counts, head, tail, first_row, last_row = forward(
        touch, owned, owners, ray_slot, blocks, foot_index.T, volume, footprints
    )
    arrived = lax.all_to_all(sent, "tile", split_axis=0, concat_axis=0, tiled=True)
    before_slice = shifted(tail, "slab", True)
    after_slice = shifted(head, "slab", False)
    counts_turned, picks = tables(owned, owners, row_count, ray_slot, blocks, counts)

    last_edge = jnp.concatenate([last_row, after_slice[row_count - 1 :]], axis=0)
    first_edge = jnp.concatenate([first_row, before_slice[:1]], axis=0)
    before_row = shifted(last_edge, "tile", True)
    after_row = shifted(first_edge, "tile", False)
    arrived, _, _ = lax.optimization_barrier((arrived, first_edge, last_edge))
    answer = residual(arrived, picks, measured, weights)
    returned = lax.all_to_all(answer, "tile", split_axis=0, concat_axis=0, tiled=True)
    halos, _ = lax.optimization_barrier(
        ((before_slice, after_slice, before_row, after_row, first_row), answer)
    )
    base = variation(volume, *halos)
    return backward(touch, table, returned, footprints, counts_turned, base)


def solution(mesh):
    in_specs = (
        P("tile", "slab", None),
        P(),
        P("tile", None),
        P(),
        P(),
        P("tile", "slab", None),
        P("tile", "slab", None),
    )
    out_specs = P("tile", "slab", None)
    return jax.shard_map(
        per_device, mesh=mesh, in_specs=in_specs, out_specs=out_specs, check_vma=False
    )
```

```python
import functools

import jax
import jax.numpy as jnp
from jax import lax
from jax.experimental import pallas as pl
from jax.experimental.pallas import tpu as pltpu
from jax.sharding import PartitionSpec as P


smoothing = 0.04
step_length = 2.0
variation_weight = 1.0
lanes = 128

F32 = jnp.float32
BF16 = jnp.bfloat16
VMEM = pl.BlockSpec(memory_space=pltpu.VMEM)
SMEM = pl.BlockSpec(memory_space=pltpu.SMEM)
HBM = pl.BlockSpec(memory_space=pltpu.HBM)


def in_hbm(*arrays):
    return [pltpu.with_memory_space_constraint(x, pltpu.HBM) for x in arrays]


def iota(shape, dim):
    return lax.broadcasted_iota(jnp.int32, shape, dim)


def forward_kernel(
    touch, owned, ray_slot, blocks, foots, volume, prints,
    sent, table, counts, head, tail, first_row, last_row,
    window, foots_buf, slot_buf, by_slice, prints_buf, grouped, sums, compact, table_buf,
    sems, small_sems, table_sem, prints_sem,
):
    row_count, slice_count, _ = volume.shape
    foot_count = prints.shape[0]
    owners = sent.shape[0]
    crossings = blocks.shape[0]

    half = slice_count // 2
    groups = sems.shape[0]
    group_size = half // groups

    position = lax.axis_index("tile")
    offset = position * row_count
    limit = blocks.shape[1] - 2 * lanes
    base = jnp.minimum((offset // lanes) * lanes, limit)
    small = [
        pltpu.make_async_copy(source, target, small_sems.at[i])
        for i, (source, target) in enumerate(
            [
                (blocks.at[:, pl.ds(pl.multiple_of(base, lanes), 2 * lanes)], window),
                (foots, foots_buf),
                (ray_slot, slot_buf),
                (volume.at[0], first_row),
                (volume.at[row_count - 1], last_row),
            ]
        )
    ]
    for copy in small:
        copy.start()
    for z in range(half):
        for z in (z, z + half):
            pltpu.make_async_copy(
                volume.at[:, z, :], by_slice.at[z], sems.at[z % half // group_size]
            ).start()
    prints_copy = pltpu.make_async_copy(prints, prints_buf, prints_sem)
    prints_copy.start()

    for copy in small[:3]:
        copy.wait()
    mine = pltpu.roll(window[...], 2 * lanes - (offset - base), 1)[:, :lanes]
    slot = jnp.zeros_like(mine)
    for b in range(ray_slot.shape[0]):
        slot = jnp.where(mine == b, slot_buf[b], slot)
    valid = iota((crossings, lanes), 1) < row_count
    owner = jnp.where(valid, slot // owned, -1)
    label = iota((owners, lanes), 0)
    present = jnp.zeros((owners, lanes), F32)
    for k in range(crossings):
        present = jnp.where(owner[k : k + 1] == label, 1.0, present)
    present = jnp.broadcast_to(jnp.max(present, axis=1, keepdims=True), (owners, lanes))
    lower = (iota((owners, owners), 1) < iota((owners, owners), 0)).astype(BF16)
    rank = jnp.dot(lower, present.astype(BF16), preferred_element_type=F32)
    column = iota((owners, lanes), 1)
    rank_row = jnp.sum(jnp.where(label < column, present, 0.0), axis=0, keepdims=True)
    present_row = jnp.sum(jnp.where(label == column, present, 0.0), axis=0, keepdims=True)
    rank_row = jnp.where(present_row > 0.5, rank_row, -1.0).astype(jnp.int32)
    match = jnp.where((rank.astype(jnp.int32) == column) & (present > 0.5), label + 1, 0)
    owner_row = jnp.sum(match, axis=0, keepdims=True) - 1
    table_buf[...] = jnp.where(iota(table_buf.shape, 0) == 0, rank_row, owner_row)
    table_copy = pltpu.make_async_copy(table_buf, table, table_sem)
    table_copy.start()

    foots_here = jnp.concatenate(
        [foots_buf[...], jnp.zeros((crossings, lanes - row_count), jnp.int32)], axis=1
    )
    hits, feet = [], []
    rank_id = iota((touch, lanes), 0)
    for k in range(crossings):
        place = jnp.sum(
            jnp.where(owner[k : k + 1] == label, rank, 0.0), axis=0, keepdims=True
        ).astype(jnp.int32)
        hits.append(jnp.where((rank_id == place) & valid[k : k + 1], 1.0, 0.0).astype(BF16))
        feet.append(
            jnp.broadcast_to(foots_here[k : k + 1].astype(F32), (touch, lanes)).astype(BF16)
        )
    none = jnp.zeros((touch, lanes), BF16)
    for f in range(foot_count):
        terms = [jnp.where(foot == f, hit, none) for foot, hit in zip(feet, hits)]
        while len(terms) > 1:
            terms = [x + y for x, y in zip(terms[::2], terms[1::2])]
        counts[f * touch : (f + 1) * touch] = terms[0]

    wide = 16

    @pl.loop(0, groups)
    def _(i):
        both = by_slice.at[pl.ds(0, 2 * group_size)]
        pltpu.make_async_copy(both, both, sems.at[i]).wait()
        for j in range(group_size):
            z = i * group_size + j
            pair = jnp.concatenate([by_slice[z], by_slice[z + half]], axis=1).astype(BF16)
            for first in range(0, foot_count, wide):
                group = jnp.dot(
                    counts[first * touch : (first + wide) * touch, :row_count],
                    pair,
                    preferred_element_type=F32,
                ).astype(BF16)
                for f in range(wide):
                    grouped[first + f, pl.ds(pl.multiple_of(z * touch, touch), touch), :] = group[
                        f * touch : (f + 1) * touch
                    ]

    head[...] = by_slice[0]
    tail[...] = by_slice[slice_count - 1]
    prints_copy.wait()
    block = 256
    zero = jnp.zeros(prints.shape[1:], BF16)
    weights = []
    for f in range(foot_count):
        weight = prints_buf[f]
        weights.append(jnp.concatenate([weight, zero], axis=1))
        weights.append(jnp.concatenate([zero, weight], axis=1))
    weights = jnp.concatenate(weights, axis=0)
    for m in range(0, half * touch, block):
        left = [grouped[f, m : m + block, :] for f in range(foot_count)]
        both = jnp.dot(jnp.concatenate(left, axis=1), weights, preferred_element_type=F32)
        rays = both.shape[1] // 2
        sums[m : m + block] = both[:, :rays]
        sums[half * touch + m : half * touch + m + block] = both[:, rays:]

    compact[touch] = jnp.zeros(compact.shape[1:], BF16)
    compact[:touch] = jnp.swapaxes(sums[...].reshape(slice_count, touch, -1), 0, 1).astype(BF16)
    for copy in small[3:]:
        copy.wait()
    table_copy.wait()
    for t in range(owners):
        place = table[0, t]
        sent[t] = compact[jnp.where(place >= 0, place, touch)]


def forward(touch, owned, owners, ray_slot, blocks, foots, volume, prints):
    rows, slices, pixels = volume.shape
    foot_count, _, rays = prints.shape
    return pl.pallas_call(
        functools.partial(forward_kernel, touch, owned),
        out_shape=(
            jax.ShapeDtypeStruct((owners, slices, rays), BF16),
            jax.ShapeDtypeStruct((8, lanes), jnp.int32),
            jax.ShapeDtypeStruct((foot_count * touch, lanes), BF16),
            jax.ShapeDtypeStruct((rows, pixels), F32),
            jax.ShapeDtypeStruct((rows, pixels), F32),
            jax.ShapeDtypeStruct((slices, pixels), F32),
            jax.ShapeDtypeStruct((slices, pixels), F32),
        ),
        in_specs=[HBM] * 5,
        out_specs=(VMEM, SMEM) + (VMEM,) * 5,
        scratch_shapes=[
            pltpu.VMEM((blocks.shape[0], 2 * lanes), jnp.int32),
            pltpu.VMEM(foots.shape, jnp.int32),
            pltpu.SMEM(ray_slot.shape, jnp.int32),
            pltpu.VMEM((slices, rows, pixels), F32),
            pltpu.VMEM(prints.shape, BF16),
            pltpu.VMEM((foot_count, slices // 2 * touch, 2 * pixels), BF16),
            pltpu.VMEM((slices * touch, rays), F32),
            pltpu.VMEM((touch + 1, slices, rays), BF16),
            pltpu.VMEM((8, lanes), jnp.int32),
            pltpu.SemaphoreType.DMA((4,)),
            pltpu.SemaphoreType.DMA((5,)),
            pltpu.SemaphoreType.DMA,
            pltpu.SemaphoreType.DMA,
        ],
        compiler_params=pltpu.CompilerParams(vmem_limit_bytes=24 << 20),
        name="forward",
    )(*in_hbm(ray_slot, blocks, foots, volume, prints))


def tables_kernel(owned, ray_slot, blocks, counts, counts_turned, picks):
    position = lax.axis_index("tile")
    rows = counts_turned.shape[0]

    counts_turned[...] = counts[...].astype(F32).T[:rows].astype(BF16)

    owners = picks.shape[0]
    width = blocks.shape[1]
    second = jnp.int32(0)
    for b in range(ray_slot.shape[0]):
        second = jnp.where(ray_slot[b] == position * owned + 1, b, second)
    hit = jnp.max(jnp.where(blocks[...] == second, 1.0, 0.0), axis=0, keepdims=True)
    start = iota((owners, width), 0) * rows
    at = iota((owners, width), 1)
    member = ((at >= start) & (at < start + rows)).astype(BF16)
    count = lax.dot_general(
        member,
        jnp.broadcast_to(hit, (lanes, width)).astype(BF16),
        (((1,), (1,)), ((), ())),
        preferred_element_type=F32,
    )
    picks[...] = jnp.where(count > 0.5, 1.0, 0.0)


def tables(owned, owners, rows, ray_slot, blocks, counts):
    return pl.pallas_call(
        functools.partial(tables_kernel, owned),
        out_shape=(
            jax.ShapeDtypeStruct((rows, counts.shape[0]), BF16),
            jax.ShapeDtypeStruct((owners, lanes), F32),
        ),
        in_specs=[SMEM] + [VMEM] * 2,
        out_specs=(VMEM,) * 2,
        compiler_params=pltpu.CompilerParams(vmem_limit_bytes=8 << 20),
        name="tables",
    )(ray_slot, blocks, counts)


def variation_kernel(
    volume, before_slice, after_slice, before_row, after_row, first_row,
    base, by_slice, row_flux, sems,
):
    slices, rows, pixels = base.shape

    groups = sems.shape[0]
    size = slices // groups
    for z in range(slices):
        pltpu.make_async_copy(volume.at[:, z, :], by_slice.at[z], sems.at[z // size]).start()

    def wait_group(i):
        span = by_slice.at[pl.ds(i * size, size)]
        pltpu.make_async_copy(span, span, sems.at[i]).wait()

    position = lax.axis_index("tile")
    layer = lax.axis_index("slab")
    last_position = lax.axis_size("tile") - 1
    last_layer = lax.axis_size("slab") - 1
    lane = iota((1, pixels), 1)
    inner = lane < pixels - 1
    first = lane == 0

    def col_grad(x):
        return jnp.where(inner, pltpu.roll(x, pixels - 1, 1) - x, 0.0)

    def scale(a, b, c):
        return lax.rsqrt(a * a + b * b + c * c + smoothing)

    low = before_row[:slices]
    z_id = iota((slices, 1), 0)
    grad_slices = before_row[1 : slices + 1] - low
    grad_slices = jnp.where((z_id == slices - 1) & (layer == last_layer), 0.0, grad_slices)
    grad_rows = first_row[...] - low
    flux = grad_rows * scale(grad_rows, grad_slices, col_grad(low))
    row_flux[...] = jnp.where(position == 0, 0.0, flux)

    row_id = iota((rows, 1), 0)
    top = row_id == rows - 1
    bottom = row_id == 0
    keep = jnp.where(top & (position == last_position), 0.0, 1.0)

    def fluxes(here, next_slice, beyond, last):
        up = jnp.where(top, beyond, pltpu.roll(here, rows - 1, 0))
        grad_rows = (up - here) * keep
        grad_slices = jnp.where(last, 0.0, next_slice - here)
        grad_cols = col_grad(here)
        inverse = scale(grad_rows, grad_slices, grad_cols)
        return grad_rows * inverse, grad_slices * inverse, grad_cols * inverse

    wait_group(0)
    _, start, _ = fluxes(before_slice[...], by_slice[0], after_row[slices : slices + 1], False)
    start = jnp.where(layer == 0, 0.0, start)

    def one(z, here, next_slice, previous, last):
        flux_rows, flux_slices, flux_cols = fluxes(
            here, next_slice, after_row[pl.ds(z, 1), :], last
        )
        below = jnp.where(bottom, row_flux[pl.ds(z, 1), :], pltpu.roll(flux_rows, 1, 0))
        left = jnp.where(first, 0.0, pltpu.roll(flux_cols, 1, 1))
        variation = (previous - flux_slices) + (below - flux_rows) + (left - flux_cols)
        base[z] = here - (step_length * variation_weight) * variation
        return flux_slices

    def step(z, previous):
        @pl.when((z + 1) % size == 0)
        def _():
            wait_group((z + 1) // size)

        return one(z, by_slice[z], by_slice[z + 1], previous, False)

    final = lax.fori_loop(0, slices - 1, step, start)
    one(slices - 1, by_slice[slices - 1], after_slice[...], final, layer == last_layer)


def variation(volume, *halos):
    rows, slices, pixels = volume.shape
    return pl.pallas_call(
        variation_kernel,
        out_shape=jax.ShapeDtypeStruct((slices, rows, pixels), F32),
        in_specs=[HBM] + [VMEM] * 5,
        out_specs=VMEM,
        scratch_shapes=[
            pltpu.VMEM((slices, rows, pixels), F32),
            pltpu.VMEM((slices, pixels), F32),
            pltpu.SemaphoreType.DMA((8,)),
        ],
        compiler_params=pltpu.CompilerParams(vmem_limit_bytes=8 << 20),
        name="variation",
    )(*in_hbm(volume), *halos)


def residual_kernel(arrived, picks, measured, weights, returned, answer, sem):
    owners = arrived.shape[0]
    sums = [jnp.zeros(measured.shape[1:], F32) for _ in range(2)]
    for j in range(owners):
        part = arrived[j].astype(F32)
        chosen = picks[j : j + 1, :] > 0.5
        sums[0] = sums[0] + part
        sums[1] = sums[1] + jnp.where(chosen, part, 0.0)
    sums[0] = sums[0] - sums[1]
    out = [(weights[i] * (sums[i] - measured[i])).astype(BF16).astype(F32) for i in range(2)]
    for j in range(owners):
        answer[j] = jnp.where(picks[j : j + 1, :] > 0.5, out[1], out[0]).astype(BF16)
        if j % 4 == 3:
            span = pl.ds(j - 3, 4)
            pltpu.make_async_copy(answer.at[span], returned.at[span], sem).start()
    pltpu.make_async_copy(answer, returned, sem).wait()


def residual(arrived, picks, measured, weights):
    return pl.pallas_call(
        residual_kernel,
        out_shape=jax.ShapeDtypeStruct(arrived.shape, BF16),
        in_specs=[VMEM] * 4,
        out_specs=HBM,
        scratch_shapes=[pltpu.VMEM(arrived.shape, BF16), pltpu.SemaphoreType.DMA],
        compiler_params=pltpu.CompilerParams(vmem_limit_bytes=4 << 20),
        name="residual",
    )(arrived, picks, measured, weights)


def backward_kernel(
    touch, table, returned, prints, counts_turned, base,
    out, returned_buf, gathered, mixed, spread, out_buf, prints_buf, sems, prints_sems, returned_sem,
):
    slices, _, pixels = base.shape
    foot_count, _, rays = prints.shape
    parts = prints_sems.shape[0]
    per_part = foot_count // parts

    def prints_copy(g):
        span = pl.ds(g * per_part, per_part)
        return pltpu.make_async_copy(prints.at[span], prints_buf.at[span], prints_sems.at[g])

    returned_copy = pltpu.make_async_copy(returned, returned_buf, returned_sem)
    returned_copy.start()
    for g in range(parts):
        prints_copy(g).start()
    returned_copy.wait()
    for s in range(touch):
        owner = table[1, s]
        block = returned_buf[jnp.maximum(owner, 0)].astype(F32)
        gathered[s] = jnp.where(owner >= 0, block, 0.0)
    mixed[...] = jnp.swapaxes(gathered[...], 0, 1).reshape(slices * touch, rays).astype(BF16)
    half = slices // 2
    block = 256
    zero = jnp.zeros(prints.shape[1:], BF16)

    @pl.loop(0, parts)
    def _(g):
        prints_copy(g).wait()
        for f in range(per_part):
            weight = prints_buf[per_part * g + f]
            weights = jnp.concatenate(
                [
                    jnp.concatenate([weight, zero], axis=1),
                    jnp.concatenate([zero, weight], axis=1),
                ],
                axis=0,
            )
            for m in range(0, half * touch, block):
                left = jnp.concatenate(
                    [mixed[m : m + block], mixed[half * touch + m : half * touch + m + block]], axis=1
                )
                value = lax.dot_general(
                    left, weights, (((1,), (1,)), ((), ())), preferred_element_type=F32
                ).astype(BF16)
                for i in range(block // touch):
                    row = pl.multiple_of((per_part * g + f) * touch, touch)
                    spread[m // touch + i, pl.ds(row, touch), :] = value[
                        i * touch : (i + 1) * touch
                    ]

    groups = sems.shape[0]
    group_size = half // groups

    @pl.loop(0, groups)
    def _(i):
        for j in range(group_size):
            z = i * group_size + j
            grad = jnp.dot(counts_turned[...], spread[z], preferred_element_type=F32)
            for g in range(2):
                at = z + g * half
                out_buf[at] = jnp.maximum(
                    base[at] - step_length * grad[:, g * pixels : (g + 1) * pixels], 0.0
                )
            if j % 4 == 3:
                for at in [z - 3 + k + g * half for k in range(4) for g in range(2)]:
                    pltpu.make_async_copy(out_buf.at[at], out.at[:, at, :], sems.at[i]).start()

    for i in range(groups):
        both = out_buf.at[pl.ds(0, 2 * group_size)]
        pltpu.make_async_copy(both, both, sems.at[i]).wait()


def backward(touch, table, returned, prints, counts_turned, base):
    slices, rows, pixels = base.shape
    codes = prints.shape[0] * touch
    return pl.pallas_call(
        functools.partial(backward_kernel, touch),
        out_shape=jax.ShapeDtypeStruct((rows, slices, pixels), F32),
        in_specs=[SMEM, HBM, HBM, VMEM, VMEM],
        out_specs=HBM,
        scratch_shapes=[
            pltpu.VMEM(returned.shape, BF16),
            pltpu.VMEM((touch, slices, prints.shape[2]), F32),
            pltpu.VMEM((slices * touch, prints.shape[2]), BF16),
            pltpu.VMEM((slices // 2, codes, 2 * pixels), BF16),
            pltpu.VMEM((slices, rows, pixels), F32),
            pltpu.VMEM(prints.shape, BF16),
            pltpu.SemaphoreType.DMA((2,)),
            pltpu.SemaphoreType.DMA((2,)),
            pltpu.SemaphoreType.DMA,
        ],
        compiler_params=pltpu.CompilerParams(vmem_limit_bytes=24 << 20),
        name="backward",
    )(table, *in_hbm(returned, prints), counts_turned, base)


def shifted(x, axis, forward_way):
    count = lax.axis_size(axis)
    if forward_way:
        pairs = [(i, i + 1) for i in range(count - 1)]
    else:
        pairs = [(i + 1, i) for i in range(count - 1)]
    return lax.ppermute(x, axis, pairs)


def per_device(volume, footprints, foot_index, ray_block, ray_slot, measured, weights):
    row_count, _, _ = volume.shape
    owners = lax.axis_size("tile")
    owned = measured.shape[0]
    touch = owners // 2
    blocks = ray_block.T
    sent, table, counts, head, tail, first_row, last_row = forward(
        touch, owned, owners, ray_slot, blocks, foot_index.T, volume, footprints
    )
    arrived = lax.all_to_all(sent, "tile", split_axis=0, concat_axis=0, tiled=True)
    before_slice = shifted(tail, "slab", True)
    after_slice = shifted(head, "slab", False)
    counts_turned, picks = tables(owned, owners, row_count, ray_slot, blocks, counts)

    last_edge = jnp.concatenate([last_row, after_slice[row_count - 1 :]], axis=0)
    first_edge = jnp.concatenate([first_row, before_slice[:1]], axis=0)
    before_row = shifted(last_edge, "tile", True)
    after_row = shifted(first_edge, "tile", False)
    arrived, _, _ = lax.optimization_barrier((arrived, first_edge, last_edge))
    answer = residual(arrived, picks, measured, weights)
    returned = lax.all_to_all(answer, "tile", split_axis=0, concat_axis=0, tiled=True)
    halos, _ = lax.optimization_barrier(
        ((before_slice, after_slice, before_row, after_row, first_row), answer)
    )
    base = variation(volume, *halos)
    return backward(touch, table, returned, footprints, counts_turned, base)


def solution(mesh):
    in_specs = (
        P("tile", "slab", None),
        P(),
        P("tile", None),
        P(),
        P(),
        P("tile", "slab", None),
        P("tile", "slab", None),
    )
    out_specs = P("tile", "slab", None)
    return jax.shard_map(
        per_device, mesh=mesh, in_specs=in_specs, out_specs=out_specs, check_vma=False
    )
```
